32 devices in a mesh: wide: 8 (over z, x), narrow: 4 (over y, core).
Axes of the slice: x: 2, y: 2, z: 4, core: 2. Of those that a mesh axis runs over, the one named last changes fastest.
Arguments:
- tokens: bfloat16 [32768, 768], P(('wide', 'narrow')), may hold values from -6 to 6
- qkv_weight: float32 [768, 2304], P('wide', 'narrow'), may hold values from -0.875 to 0.875
- qv_bias: float32 [1536], P(('wide', 'narrow')), may hold values from -3 to 3
- out_weight: float32 [768, 768], P('wide', 'narrow'), may hold values from -2 to 2
- out_bias: float32 [768], P(('wide', 'narrow')), may hold values from -4 to 4
- up_weight: float32 [768, 3072], P('wide', 'narrow'), may hold values from -0.21875 to 0.21875
- up_bias: float32 [3072], P(('wide', 'narrow')), may hold values from -3 to 3
- down_weight: float32 [3072, 768], P('wide', 'narrow'), may hold values from -0.875 to 0.875
- down_bias: float32 [768], P(('wide', 'narrow')), may hold values from -4 to 4
- norm1_gain: float32 [768], P(('wide', 'narrow')), may hold values from 0.5 to 1.5
- norm1_bias: float32 [768], P(('wide', 'narrow')), may hold values from -2 to 2
- norm2_gain: float32 [768], P(('wide', 'narrow')), may hold values from 0.5 to 1.5
- norm2_bias: float32 [768], P(('wide', 'narrow')), may hold values from -2 to 2
- lengths: int32 [32, 2], P(('wide', 'narrow')), may hold values from 0 to 1024, as said below
- cotangent: bfloat16 [32768, 768], P(('wide', 'narrow')), may hold values from -6 to 6
Outputs:
- output: bfloat16 [32768, 768], P(('wide', 'narrow'))
- grad_tokens: bfloat16 [32768, 768], P(('wide', 'narrow'))
- grad_qkv_weight: float32 [768, 2304], P('wide', 'narrow')
- grad_qv_bias: float32 [1536], P(('wide', 'narrow'))
- grad_out_weight: float32 [768, 768], P('wide', 'narrow')
- grad_out_bias: float32 [768], P(('wide', 'narrow'))
- grad_up_weight: float32 [768, 3072], P('wide', 'narrow')
- grad_up_bias: float32 [3072], P(('wide', 'narrow'))
- grad_down_weight: float32 [3072, 768], P('wide', 'narrow')
- grad_down_bias: float32 [768], P(('wide', 'narrow'))
- grad_norm1_gain: float32 [768], P(('wide', 'narrow'))
- grad_norm1_bias: float32 [768], P(('wide', 'narrow'))
- grad_norm2_gain: float32 [768], P(('wide', 'narrow'))
- grad_norm2_bias: float32 [768], P(('wide', 'narrow'))
The draws below stay inside these ranges and needn't reach their ends.
Inputs may be any that keep to these rules, and one draw needn't show every extreme that they name: `lengths`: each device row holds either one sequence of 1024 tokens (second length 0), two of 512, or one of 1024 / 2 (second length 0); some device holds 1024 tokens.
All inputs are finite; a program needn't handle non-finite values.
Results may differ from the reference program's by a relative error of at most 0.015.
The reference program's roundings to bfloat16 on the way count: a program that leaves them out, or rounds other values in their place, can miss the bound.
Values may be sent and summed in bfloat16 or wider, within the bound.
No kernel may reach another device: no remote copies, remote signals or barrier semaphores. Data moves between devices by JAX's collectives and lax.ppermute only.
A program may use at most 256 MiB of HBM per device.

```python
import jax
import jax.numpy as jnp
from jax import lax

D = 768
HEADS = 12
HD = 64
FF = 3072
CAP = 1024
TOKENS = 32768
N_WIDE = 8
N_NARROW = 4


def draw_lengths(key, part):
    device_count = N_WIDE * N_NARROW
    layout_kind = jax.random.randint(jax.random.fold_in(key, 11), (device_count,), 0, 4)
    forced = jax.random.randint(jax.random.fold_in(key, 12), (), 0, device_count)
    layout_kind = jnp.where(jnp.arange(device_count) == forced, 0, layout_kind)
    half_cap = CAP // 2
    first_len = jnp.where(layout_kind <= 1, CAP, half_cap)
    second_len = jnp.where(layout_kind == 2, half_cap, 0)
    return jnp.stack([first_len, second_len], axis=1).astype(jnp.int32)


def with_spikes(array, own_key, source, target, shards_of, factor):
    owner, partner = [(jnp.arange(array.shape[dim]) // (array.shape[dim] // shards_of)).reshape([-1 if axis == dim else 1 for axis in range(array.ndim)]) for dim in (source, target)]
    chosen = jax.random.permutation(own_key, shards_of)[partner]
    strong = (owner == chosen) | (owner == (partner + shards_of // 2) % shards_of)
    return jnp.where(strong, factor * array, array)


def level_of(key, extent, shards, least, top_value):
    def one(axis_at, blocks):
        heights = jax.random.uniform(jax.random.fold_in(jax.random.fold_in(key, 6), axis_at), (blocks,), jnp.float32, least / len(shards), top_value / len(shards))
        return jnp.repeat(jnp.exp(heights), extent[axis_at] // blocks).reshape((-1,) + (1,) * (len(extent) - axis_at - 1))

    loudness = one(*shards[0])
    for cut in shards[1:]:
        loudness = loudness * one(*cut)
    return loudness


def scatter_about(stream_key, dims, width, bound, cuts=(), kind=jnp.bfloat16):
    gain = level_of(stream_key, dims, cuts, -0.22, 0.18) if cuts else 1.0
    entries = jax.random.normal(stream_key, dims, jnp.float32) * width * gain
    return jnp.minimum(jnp.maximum(entries, -bound), bound).astype(kind)


def gaussian_with(stream_key, extent, scale, most, shards, heavy, kind=jnp.bfloat16):
    array = scale * jax.random.normal(stream_key, extent, jnp.float32)
    if shards:
        array = array * level_of(stream_key, extent, shards, -0.22, 0.18)
    return jnp.clip(with_spikes(array, jax.random.fold_in(stream_key, 3), *heavy), -most, most).astype(kind)


def setup_inputs(seed: int = 0) -> dict:
    splits = jax.random.split(jax.random.key(seed), 16)
    return {
        "tokens": scatter_about(splits[0], (TOKENS, D), 1.0, 6.0, ((0, 32),)),
        "qkv_weight": scatter_about(splits[1], (D, 3 * D), (D // 16) ** -0.5, 0.875, ((0, 8), (1, 4)), jnp.float32),
        "qv_bias": scatter_about(splits[2], (2 * D,), 0.5, 3.0, ((0, 32),), jnp.float32),
        "out_weight": scatter_about(splits[3], (D, D), (D // 96) ** -0.5, 2.0, ((0, 8), (1, 4)), jnp.float32),
        "out_bias": scatter_about(splits[4], (D,), 1.0, 4.0, ((0, 32),), jnp.float32),
        "up_weight": scatter_about(splits[5], (D, FF), D ** -0.5, 0.21875, ((0, 8), (1, 4)), jnp.float32),
        "up_bias": scatter_about(splits[6], (FF,), 0.5, 3.0, ((0, 32),), jnp.float32),
        "down_weight": scatter_about(splits[7], (FF, D), (FF // 64) ** -0.5, 0.875, ((0, 8), (1, 4)), jnp.float32),
        "down_bias": scatter_about(splits[8], (D,), 1.0, 4.0, ((0, 32),), jnp.float32),
        "norm1_gain": jnp.clip(1.0 + 0.1 * jax.random.normal(splits[9], (D,), jnp.float32), 0.5, 1.5),
        "norm1_bias": scatter_about(splits[10], (D,), 0.3, 2.0, ((0, 32),), jnp.float32),
        "norm2_gain": jnp.clip(1.0 + 0.1 * jax.random.normal(splits[11], (D,), jnp.float32), 0.5, 1.5),
        "norm2_bias": scatter_about(splits[12], (D,), 0.3, 2.0, ((0, 32),), jnp.float32),
        "lengths": draw_lengths(jax.random.fold_in(splits[15], 71), 0),
        "cotangent": gaussian_with(splits[14], (TOKENS, D), 1.0, 6.0, ((0, 32),), (0, 1, 32, 2.75)),
    }


@jax.custom_vjp
def low(v):
    return lax.optimization_barrier(v.astype(jnp.bfloat16)).astype(jnp.float32)

@jax.custom_vjp
def low_back(v):
    return v

def low_keep(v):
    return (low(v), None)

def low_pass(kept, grad):
    return (grad,)

def back_keep(v):
    return (v, None)

def back_low(kept, grad):
    return (low(grad),)
low.defvjp(low_keep, low_pass)
low_back.defvjp(back_keep, back_low)
epsilon = 1e-05
branch_scale = 24 ** (-0.5)

def layer_norm(values, norm_gain, norm_shift):
    average = lax.optimization_barrier(jnp.mean(values, axis=-1, keepdims=True))
    centred = values - average
    spread = lax.optimization_barrier(jnp.mean(centred * centred, axis=-1, keepdims=True))
    return centred * lax.rsqrt(spread + epsilon) * norm_gain + norm_shift

def round_both(values):
    return low_back(low(values))

def segments_of(own_lengths, row_count):
    positions = jnp.arange(row_count, dtype=jnp.int32)
    first_len = own_lengths[0]
    total_len = own_lengths[0] + own_lengths[1]
    segment = jnp.where(positions < first_len, 0, jnp.where(positions < total_len, 1, 2)).astype(jnp.int32)
    return (positions, segment, positions < total_len)

def dense(left, right):
    return jnp.dot(left, right, precision=lax.Precision.HIGHEST, preferred_element_type=jnp.float32)

def layer(params, block_rows, own_lengths):
    rounded = [low(param) for param in params]
    w_qkv, w_out, w_up, w_down, b_qv, b_out, b_up, b_down, gain_one, shift_one, gain_two, shift_two = rounded
    row_count = block_rows.shape[0]
    positions, segment, live_rows = segments_of(own_lengths, row_count)
    normed_one = low(layer_norm(block_rows, gain_one, shift_one))
    projected = dense(normed_one, w_qkv)
    queries = round_both(projected[:, :D] + b_qv[:D]).reshape(row_count, HEADS, HD)
    key_rows = round_both(projected[:, D:2 * D]).reshape(row_count, HEADS, HD)
    value_rows = round_both(projected[:, 2 * D:] + b_qv[D:]).reshape(row_count, HEADS, HD)
    scores = low_back(jnp.einsum('qhd,khd->hqk', queries, key_rows, precision=lax.Precision.HIGHEST) * (1.0 / HD))
    allowed = (segment[:, None] == segment[None, :]) & (positions[None, :] <= positions[:, None])
    scores = jnp.where(allowed[None], scores, -1e+30)
    attention = low(jax.nn.softmax(scores, axis=-1))
    attended = round_both(jnp.einsum('hqk,khd->qhd', attention, value_rows, precision=lax.Precision.HIGHEST).reshape(row_count, D))
    branch = low_back(dense(attended, w_out) + b_out)
    middle = block_rows + branch_scale * branch
    normed_two = low(layer_norm(middle, gain_two, shift_two))
    hidden = low_back(dense(normed_two, w_up) + b_up)
    active = low(jax.nn.gelu(hidden, approximate=True))
    branch_two = low_back(dense(active, w_down) + b_down)
    return middle + branch_scale * branch_two

def reference(tokens, qkv_weight, qv_bias, out_weight, out_bias, up_weight, up_bias, down_weight, down_bias, norm1_gain, norm1_bias, norm2_gain, norm2_bias, lengths, cotangent):
    device_count = N_WIDE * N_NARROW
    params = (qkv_weight, out_weight, up_weight, down_weight, qv_bias, out_bias, up_bias, down_bias, norm1_gain, norm1_bias, norm2_gain, norm2_bias)
    blocks = tokens.astype(jnp.float32).reshape(device_count, CAP, D)
    cotans = cotangent.astype(jnp.float32).reshape(device_count, CAP, D)

    def one_device(totals, item):
        block_rows, own_lengths, cotan_rows = item
        live_rows = segments_of(own_lengths, CAP)[2]

        def forward(param_set, inputs):
            return layer(param_set, inputs, own_lengths)
        result, pull = jax.vjp(forward, params, block_rows)
        grads, grad_rows = pull(cotan_rows * live_rows[:, None].astype(jnp.float32))
        totals = jax.tree.map(jnp.add, totals, grads)
        return (totals, (result.astype(jnp.bfloat16), grad_rows.astype(jnp.bfloat16)))
    zeros = jax.tree.map(jnp.zeros_like, params)
    totals, stacked = lax.scan(one_device, zeros, (blocks, lengths, cotans))
    results, grad_inputs = stacked
    return (results.reshape(device_count * CAP, D), grad_inputs.reshape(device_count * CAP, D), totals[0], totals[4], totals[1], totals[5], totals[2], totals[6], totals[3], totals[7], totals[8], totals[9], totals[10], totals[11])
```

```python
import jax
import jax.numpy as jnp
import numpy as np
from jax import lax
from jax.experimental import pallas as pl
from jax.experimental.pallas import tpu as pltpu
from jax.sharding import PartitionSpec as P

HEADS = 12
BOTH = ("wide", "narrow")
bf16 = jnp.bfloat16
f32 = jnp.float32
epsilon = 1e-05
branch_scale = 24 ** (-0.5)
D = 768
FF = 3072
HD = 64
ROWS = 1024
PAIRS = HEADS // 2
QB = 256
NEG = -1e30
QKV_ROWS, OUT_ROWS, VEC_ROWS = 144, 48, 8
FAM_Q = QKV_ROWS + OUT_ROWS + VEC_ROWS
UP_ROWS, DN_ROWS = 192, 192
FAM_M = UP_ROWS + DN_ROWS
SMALL = (
    ("qv", 0, 48, 2),
    ("outb", 48, 24, 1),
    ("downb", 72, 24, 1),
    ("gain1", 96, 24, 1),
    ("shift1", 128, 24, 1),
    ("gain2", 152, 24, 1),
    ("shift2", 176, 24, 1),
    ("upb", 256, 96, 4),
)
ROW_OF = {}
_row = 0
for _name, _off, _wd, _n in SMALL:
    ROW_OF[_name] = _row
    _row += _n
VECS = 16


def nn(a, b):
    return lax.dot_general(a, b, (((1,), (0,)), ((), ())), preferred_element_type=f32)


def nt(a, b):
    return lax.dot_general(a, b, (((1,), (1,)), ((), ())), preferred_element_type=f32)


def normalize(values):
    average = jnp.mean(values, axis=-1, keepdims=True)
    centred = values - average
    spread = jnp.mean(centred * centred, axis=-1, keepdims=True)
    rinv = lax.rsqrt(spread + epsilon)
    return centred * rinv, rinv


def params(flops, bytes_accessed):
    return dict(
        compiler_params=pltpu.CompilerParams(vmem_limit_bytes=60 * 1024 * 1024),
        cost_estimate=pl.CostEstimate(
            flops=int(flops), transcendentals=0, bytes_accessed=int(bytes_accessed)
        ),
    )


VM = pl.BlockSpec(memory_space=pltpu.VMEM)
SM = pl.BlockSpec(memory_space=pltpu.SMEM)
HB = pl.BlockSpec(memory_space=pl.ANY)


def sds(shape, dtype):
    return jax.ShapeDtypeStruct(shape, dtype)


def held_by(meta, q, k, own):
    w, n = meta[0], meta[1]
    z, x, y, c = w // 2, w % 2, n // 2, n % 2
    core = c if own else 1 - c
    first, second = q % 2, q // 2
    dx = jnp.where(core == 0, first, second)
    dy = jnp.where(core == 0, second, first)
    zz = z ^ k
    return zz * 2 + (x ^ dx), core, y ^ dy


def slot_for(meta, i, core, y):
    w, n = meta[0], meta[1]
    dx = (w % 2) ^ (i % 2)
    dy = (n // 2) ^ y
    first = jnp.where(core == 0, dx, dy)
    second = jnp.where(core == 0, dy, dx)
    return first + 2 * second, (w // 2) ^ (i // 2), (n % 2) == core


def piece_loop(meta, quads, issue):
    for own in (True, False):
        for q in range(4):
            ref = quads[q if own else 4 + q]
            for k in range(4):
                i, core, y = held_by(meta, q, k, own)
                issue(ref.at[k], i, core, y)


def small_map(off, wd, row):
    lane = lax.broadcasted_iota(jnp.int32, (128, D), 1) + row * D
    within = lane - wd * jnp.floor((lane.astype(f32) + 0.5) * (1.0 / wd)).astype(jnp.int32)
    src = lax.broadcasted_iota(jnp.int32, (128, D), 0)
    return jnp.where(src == within + off % 128, 1.0, 0.0).astype(bf16)


def segment_mask(wd, row, rows_per_device, rows):
    lane = lax.broadcasted_iota(jnp.int32, (rows, D), 1) + row * D
    low = (lax.broadcasted_iota(jnp.int32, (rows, D), 0) // rows_per_device) * wd
    return (lane >= low) & (lane < low + wd)


def unpack_small(packed):
    rows = []
    for _, off, wd, count in SMALL:
        group = packed[:, off // 128 * 128 : off // 128 * 128 + 128]
        for row in range(count):
            spread = nn(group, small_map(off, wd, row))
            lane = lax.broadcasted_iota(jnp.int32, (256, D), 1) + row * D
            dev = lax.broadcasted_iota(jnp.int32, (256, D), 0)
            low = (dev >> 3) * wd
            keep = (lane >= low) & (lane < low + wd) & ((dev & 7) == 0)
            rows.append(jnp.sum(jnp.where(keep, spread, 0.0), axis=0, keepdims=True))
    rows.append(jnp.zeros((VECS - len(rows), D), f32))
    return jnp.concatenate(rows, axis=0)


def pack_small(vec_row):
    groups = [jnp.zeros((32, 128), f32) for _ in range(3)]
    for name, off, wd, count in SMALL:
        for row in range(count):
            lane = lax.broadcasted_iota(jnp.int32, (32, D), 1) + row * D
            low = lax.broadcasted_iota(jnp.int32, (32, D), 0) * wd
            keep = (lane >= low) & (lane < low + wd)
            spread = jnp.where(keep, vec_row(ROW_OF[name] + row), 0.0).astype(bf16)
            groups[off // 128] += nt(spread, small_map(off, wd, row))
    return jnp.concatenate(groups, axis=1)


def project_body(pieces, meta, tok, *refs):
    if pieces:
        quads, (a1_o, a1t_o, qkv_o, wq_o, wo_o, vec_o, packed, sem, sem2) = refs[:8], refs[8:]

        def issue(ref, i, core, y):
            at = pl.ds(pl.multiple_of((i * 2 + core) * 48, 16), 48)
            for t in range(3):
                pltpu.make_async_copy(ref.at[pl.ds(48 * t, 48)], wq_o.at[y, t, at], sem).start()
            pltpu.make_async_copy(ref.at[pl.ds(144, 48)], wo_o.at[y, at], sem).start()
            dev = pl.multiple_of((i * 4 + 2 * y + core) * 8, 8)
            pltpu.make_async_copy(ref.at[pl.ds(192, 8)], packed.at[pl.ds(dev, 8)], sem2).start()

        piece_loop(meta, quads, issue)
    else:
        wq_i, wo_i, vec_i, a1_o, a1t_o, qkv_o, wq_o, wo_o, vec_o, packed, sem, sem2 = refs
        pltpu.make_async_copy(wq_i, wq_o, sem).start()
        pltpu.make_async_copy(wo_i, wo_o, sem).start()
    if pieces:
        pltpu.make_async_copy(packed, packed, sem2).wait()
        vec = unpack_small(packed[...])
    else:
        vec = vec_i[...]
    vec_o[...] = vec
    for r in range(4):
        at = pl.ds(QB * r, QB)
        n1, _ = normalize(tok[at, :].astype(f32))
        a1_o[at, :] = (n1 * vec[ROW_OF["gain1"]][None] + vec[ROW_OF["shift1"]][None]).astype(bf16)
    a1t_o[...] = a1_o[...].T
    pltpu.make_async_copy(wq_o, wq_o, sem).wait()
    pltpu.make_async_copy(wo_o, wo_o, sem).wait()
    for r in range(4):
        at = pl.ds(QB * r, QB)
        rows = a1_o[at, :]
        for y in range(2):
            for t in range(3):
                block = nn(rows, wq_o[y, t])
                col = y * 1152 + t * 384
                for g in range(3):
                    part = block[:, 128 * g : 128 * g + 128]
                    head = col // 128 + g
                    if head < 6:
                        part = (part + vec[ROW_OF["qv"]][None, 128 * head : 128 * head + 128]).astype(bf16)
                        part = part * jnp.asarray(1.0 / HD, bf16)
                    elif head >= 12:
                        lane = 128 * (head - 12)
                        part = (part + vec[ROW_OF["qv"] + 1][None, lane : lane + 128]).astype(bf16)
                    else:
                        part = part.astype(bf16)
                    qkv_o[head, at, :] = part


def project(pieces, meta, tokens, weights):
    return pl.pallas_call(
        lambda *refs: project_body(pieces, *refs),
        out_shape=(
            sds((ROWS, D), bf16),
            sds((D, ROWS), bf16),
            sds((18, ROWS, 128), bf16),
            sds((2, 3, D, 384), bf16),
            sds((2, D, 384), bf16),
            sds((VECS, D), f32),
        ),
        in_specs=[SM, VM] + ([HB] * 8 if pieces else [HB, HB, VM]),
        out_specs=(VM,) * 6,
        scratch_shapes=[
            pltpu.VMEM((256, 384), bf16),
            pltpu.SemaphoreType.DMA(()),
            pltpu.SemaphoreType.DMA(()),
        ],
        name="project",
        **params(2 * ROWS * D * 2304, 16e6),
    )(meta, tokens, *weights)


def attend_body(lens, q_ref, k_ref, v_ref, o_ref, lse_ref):
    far = jnp.where(lens[0, 0] < ROWS, NEG, 0.0).astype(f32)
    lane = lax.broadcasted_iota(jnp.int32, (QB, 128), 1)
    causal = lax.broadcasted_iota(jnp.int32, (QB, QB), 1) <= lax.broadcasted_iota(
        jnp.int32, (QB, QB), 0
    )
    for j in range(ROWS // QB):
        size = QB * (j + 1)
        q = q_ref[0, QB * j : size, :]
        outs, logs = [], []
        for h in range(2):
            mine = (lane < HD) if h == 0 else (lane >= HD)
            s = nt(jnp.where(mine, q, jnp.zeros_like(q)), k_ref[0, :size, :])
            parts = []
            if j >= 2:
                parts.append(s[:, :512] + far)
                if j == 3:
                    parts.append(s[:, 512:768])
            elif j == 1:
                parts.append(s[:, :QB])
            parts.append(jnp.where(causal, s[:, size - QB :], NEG))
            s = jnp.concatenate(parts, axis=1)
            top = jnp.max(s, axis=1, keepdims=True)
            e = jnp.exp(s - top)
            total = jnp.sum(e, axis=1, keepdims=True)
            outs.append(nn((e / total).astype(bf16), v_ref[0, :size, :]))
            logs.append(top + jnp.log(total))
        o_ref[QB * j : size, :] = jnp.where(lane < HD, outs[0], outs[1]).astype(bf16)
        both = jnp.where(lane == 0, logs[0], logs[1])
        lse_ref[0, :, QB * j : size] = both.T[:8]


def attend(lens, qkv):
    block = lambda base: pl.BlockSpec((1, ROWS, 128), lambda g: (base + g, 0, 0))
    return pl.pallas_call(
        attend_body,
        grid=(PAIRS,),
        out_shape=(sds((ROWS, D), bf16), sds((PAIRS, 8, ROWS), f32)),
        in_specs=[SM, block(0), block(6), block(12)],
        out_specs=(
            pl.BlockSpec((ROWS, 128), lambda g: (0, g)),
            pl.BlockSpec((1, 8, ROWS), lambda g: (g, 0, 0)),
        ),
        name="attend",
        **params(12e9, 8e6),
    )(lens, qkv, qkv, qkv)


def middle_body(pieces, meta, lens, tok, o_ref, cot, vec, wo, *refs):
    count = 8 if pieces else 2
    quads = refs[:count]
    out_o, dh_o, do_o, own, other, dwo_o, sums_o = refs[count : count + 7]
    wup, wdn, h_s, a2_s, a2t_s, dm_s, dmt_s, m_s, da2_s, gl_s, dz_s, st_u, st_d, sem, sem_o = refs[
        count + 7 :
    ]
    if pieces:

        def issue(ref, i, core, y):
            n = 2 * y + core
            at = pl.ds(pl.multiple_of(i * 96, 32), 96)
            for half in range(2):
                pltpu.make_async_copy(
                    ref.at[pl.ds(96 * half, 96)], wup.at[n, at, pl.ds(384 * half, 384)], sem
                ).start()
            at = pl.ds(pl.multiple_of(n * 192, 64), 192)
            lanes = pl.ds(pl.multiple_of((i % 2) * 384, 128), 384)
            pltpu.make_async_copy(ref.at[pl.ds(192, 192)], wdn.at[i // 2, at, lanes], sem).start()

        piece_loop(meta, quads, issue)
    else:
        pltpu.make_async_copy(quads[0], wup, sem).start()
        pltpu.make_async_copy(quads[1], wdn, sem).start()
    total = lens[0, 0] + lens[0, 1]
    gain2 = vec[ROW_OF["gain2"] : ROW_OF["gain2"] + 1, :]
    shift2 = vec[ROW_OF["shift2"] : ROW_OF["shift2"] + 1, :]
    outb = vec[ROW_OF["outb"] : ROW_OF["outb"] + 1, :]
    downb = vec[ROW_OF["downb"] : ROW_OF["downb"] + 1, :]
    sums_o[...] = jnp.zeros_like(sums_o)
    ROW_DN, ROW_G2, ROW_B2, ROW_OB = 0, 1, 2, 3
    for r in range(4):
        at = pl.ds(QB * r, QB)
        o = o_ref[at, :]
        u = jnp.concatenate([nn(o, wo[0]), nn(o, wo[1])], axis=1) + outb
        h = tok[at, :].astype(f32) + branch_scale * u
        h_s[at, :] = h
        n2, _ = normalize(h)
        a2_s[at, :] = (n2 * gain2 + shift2).astype(bf16)
        live = (lax.broadcasted_iota(jnp.int32, (QB, D), 0) + QB * r) < total
        dm = (branch_scale * jnp.where(live, cot[at, :].astype(f32), 0.0)).astype(bf16)
        dm_s[at, :] = dm
        sums_o[ROW_DN : ROW_DN + 1, :] += jnp.sum(dm.astype(f32), axis=0, keepdims=True)
    a2t_s[...] = a2_s[...].T
    dmt_s[...] = dm_s[...].T
    m_s[...] = jnp.zeros_like(m_s)
    da2_s[...] = jnp.zeros_like(da2_s)
    pltpu.make_async_copy(wup, wup, sem).wait()
    pltpu.make_async_copy(wdn, wdn, sem).wait()

    c0 = 0.7978845608028654
    c1 = 0.044715 * c0

    def step(f, carry):
        up = wup[f]
        dn = wdn[f]
        bup = vec[pl.ds(ROW_OF["upb"] + f, 1), :]
        bsum = jnp.zeros((1, D), f32)
        for r in range(4):
            at = pl.ds(QB * r, QB)
            z = nn(a2_s[at, :], up) + bup
            dgl = nn(dm_s[at, :], dn)
            zz = z * z
            th = jnp.tanh(z * (c0 + c1 * zz))
            half = 0.5 * th + 0.5
            gl = (z * half).astype(bf16)
            slope = half + (0.5 * z) * (1.0 - th * th) * (c0 + (3.0 * c1) * zz)
            dz = (dgl * slope).astype(bf16)
            gl_s[at, :] = gl
            dz_s[at, :] = dz
            bsum += jnp.sum(dz.astype(f32), axis=0, keepdims=True)
            m_s[at, :] += nt(gl, dn)
            da2_s[at, :] += nt(dz, up)
        sums_o[pl.ds(4 + f, 1), :] = bsum
        slot = f % 2

        @pl.when(f >= 2)
        def _():
            pltpu.make_async_copy(st_u.at[slot], st_u.at[slot], sem_o.at[slot]).wait()
            pltpu.make_async_copy(st_d.at[slot], st_d.at[slot], sem_o.at[slot]).wait()

        st_u[slot] = nn(a2t_s[...], dz_s[...]).astype(bf16)
        st_d[slot] = nn(dmt_s[...], gl_s[...]).astype(bf16)
        for i in range(8):
            for half in range(2):
                emit_at(
                    st_u.at[slot, pl.ds(96 * i, 96), pl.ds(384 * half, 384)],
                    i, f % 2, f // 2, 96 * half, slot,
                )
        for n in range(4):
            for half in range(2):
                emit_at(
                    st_d.at[slot, pl.ds(192 * n, 192), pl.ds(384 * half, 384)],
                    2 * f + half, n % 2, n // 2, 192, slot,
                )
        return carry

    def emit_at(src, i, core, y, row, slot):
        rows = src.shape[0]
        if pieces:
            q, k, mine = slot_for(meta, i, core, y)

            @pl.when(mine)
            def _():
                pltpu.make_async_copy(src, own.at[q, k, pl.ds(row, rows)], sem_o.at[slot]).start()

            @pl.when(jnp.logical_not(mine))
            def _():
                pltpu.make_async_copy(src, other.at[q, k, pl.ds(row, rows)], sem_o.at[slot]).start()
        else:
            pltpu.make_async_copy(src, own.at[i, 2 * y + core, pl.ds(row, rows)], sem_o.at[slot]).start()

    lax.fori_loop(0, 4, step, 0)
    for r in range(4):
        at = pl.ds(QB * r, QB)
        h = h_s[at, :]
        out_o[at, :] = (h + branch_scale * (m_s[at, :] + downb)).astype(bf16)
        n2, r2 = normalize(h)
        da2 = da2_s[at, :]
        sums_o[ROW_G2 : ROW_G2 + 1, :] += jnp.sum(da2 * n2, axis=0, keepdims=True)
        sums_o[ROW_B2 : ROW_B2 + 1, :] += jnp.sum(da2, axis=0, keepdims=True)
        e = da2 * gain2
        live = (lax.broadcasted_iota(jnp.int32, (QB, D), 0) + QB * r) < total
        dy = jnp.where(live, cot[at, :].astype(f32), 0.0)
        dh = dy + r2 * (
            e
            - jnp.mean(e, axis=-1, keepdims=True)
            - n2 * jnp.mean(e * n2, axis=-1, keepdims=True)
        )
        dh_o[at, :] = dh
        du = (branch_scale * dh).astype(bf16)
        sums_o[ROW_OB : ROW_OB + 1, :] += jnp.sum(du.astype(f32), axis=0, keepdims=True)
        gl_s[at, :] = du
        do_o[at, :] = (nt(du[:, :384], wo[0]) + nt(du[:, 384:], wo[1])).astype(bf16)
    dwo_o[...] = nn(o_ref[...].T, gl_s[...]).astype(bf16)
    for slot in range(2):
        pltpu.make_async_copy(st_u.at[slot], st_u.at[slot], sem_o.at[slot]).wait()
        pltpu.make_async_copy(st_d.at[slot], st_d.at[slot], sem_o.at[slot]).wait()


def middle(pieces, meta, lens, tokens, attended, cotangent, vec, wo, weights):
    if pieces:
        grads = (sds((4, 4, FAM_M, 384), bf16), sds((4, 4, FAM_M, 384), bf16))
    else:
        grads = (sds((8, 4, FAM_M, 384), bf16), sds((8, 128), bf16))
    return pl.pallas_call(
        lambda *refs: middle_body(pieces, *refs),
        out_shape=(
            sds((ROWS, D), bf16),
            sds((ROWS, D), f32),
            sds((ROWS, D), bf16),
            *grads,
            sds((D, D), bf16),
            sds((8, D), f32),
        ),
        in_specs=[SM, SM, VM, VM, VM, VM, VM] + [HB] * (8 if pieces else 2),
        out_specs=(VM, VM, VM, HB, HB, VM, VM),
        scratch_shapes=[
            pltpu.VMEM((4, D, D), bf16),
            pltpu.VMEM((4, D, D), bf16),
            pltpu.VMEM((ROWS, D), f32),
            pltpu.VMEM((ROWS, D), bf16),
            pltpu.VMEM((D, ROWS), bf16),
            pltpu.VMEM((ROWS, D), bf16),
            pltpu.VMEM((D, ROWS), bf16),
            pltpu.VMEM((ROWS, D), f32),
            pltpu.VMEM((ROWS, D), f32),
            pltpu.VMEM((ROWS, D), bf16),
            pltpu.VMEM((ROWS, D), bf16),
            pltpu.VMEM((2, D, D), bf16),
            pltpu.VMEM((2, D, D), bf16),
            pltpu.SemaphoreType.DMA(()),
            pltpu.SemaphoreType.DMA((2,)),
        ],
        name="middle",
        **params(6 * 2 * ROWS * D * FF, 40e6),
    )(meta, lens, tokens, attended, cotangent, vec, wo, *weights)


def attend_back_body(lens, q_ref, k_ref, v_ref, do_ref, lse_ref, dq_o, dk_o, dv_o, sums_o, dk_s, dv_s):
    far = jnp.where(lens[0, 0] < ROWS, NEG, 0.0).astype(f32)
    lane = lax.broadcasted_iota(jnp.int32, (QB, 128), 1)
    causal = lax.broadcasted_iota(jnp.int32, (QB, QB), 0) <= lax.broadcasted_iota(
        jnp.int32, (QB, QB), 1
    )
    kt = k_ref[0].T
    sub = lax.broadcasted_iota(jnp.int32, (128, ROWS), 0)
    dk_s[...] = jnp.zeros_like(dk_s)
    dv_s[...] = jnp.zeros_like(dv_s)
    qsum = jnp.zeros((1, 128), f32)
    for j in range(ROWS // QB):
        size = QB * (j + 1)
        q = q_ref[0, QB * j : size, :]
        do = do_ref[QB * j : size, :]
        dq = jnp.zeros((128, QB), f32)
        dk = jnp.zeros((size, 128), f32)
        dv = jnp.zeros((size, 128), f32)
        for h in range(2):
            mine = (lane < HD) if h == 0 else (lane >= HD)
            qh = jnp.where(mine, q, jnp.zeros_like(q))
            doh = jnp.where(mine, do, jnp.zeros_like(do))
            s = nt(k_ref[0, :size, :], qh)
            parts = []
            if j >= 2:
                parts.append(s[:512] + far)
                if j == 3:
                    parts.append(s[512:768])
            elif j == 1:
                parts.append(s[:QB])
            parts.append(jnp.where(causal, s[size - QB :], NEG))
            s = jnp.concatenate(parts, axis=0)
            p = jnp.exp(s - lse_ref[0, h : h + 1, QB * j : size])
            dp = nt(v_ref[0, :size, :], doh)
            dot = jnp.sum(p * dp, axis=0, keepdims=True)
            ds = (p * (dp - dot)).astype(bf16)
            dv += nn(p.astype(bf16), doh)
            dk += nn(ds, qh)
            keep = (sub < HD) if h == 0 else (sub >= HD)
            dq += nn(jnp.where(keep, kt, jnp.zeros_like(kt))[:, :size], ds)
        dqb = (dq.T * (1.0 / HD)).astype(bf16)
        dq_o[0, QB * j : size, :] = dqb
        qsum += jnp.sum(dqb.astype(f32), axis=0, keepdims=True)
        dk_s[:size, :] += dk
        dv_s[:size, :] += dv
    dk_o[0] = dk_s[...].astype(bf16)
    dvb = dv_s[...].astype(bf16)
    dv_o[0] = dvb
    vsum = jnp.sum(dvb.astype(f32), axis=0, keepdims=True)
    row = lax.broadcasted_iota(jnp.int32, (8, 128), 0)
    sums_o[...] = jnp.where(row == 0, qsum, vsum)


def attend_back(lens, qkv, do, lse):
    block = lambda base: pl.BlockSpec((1, ROWS, 128), lambda g: (base + g, 0, 0))
    cols = pl.BlockSpec((ROWS, 128), lambda g: (0, g))
    return pl.pallas_call(
        attend_back_body,
        grid=(PAIRS,),
        out_shape=(
            sds((PAIRS, ROWS, 128), bf16),
            sds((PAIRS, ROWS, 128), bf16),
            sds((PAIRS, ROWS, 128), bf16),
            sds((8, D), f32),
        ),
        in_specs=[SM, block(0), block(6), block(12), cols, pl.BlockSpec((1, 8, ROWS), lambda g: (g, 0, 0))],
        out_specs=(block(0), block(0), block(0), pl.BlockSpec((8, 128), lambda g: (0, g))),
        scratch_shapes=[pltpu.VMEM((ROWS, 128), f32), pltpu.VMEM((ROWS, 128), f32)],
        name="attend_back",
        **params(30e9, 12e6),
    )(lens, qkv, qkv, qkv, do, lse)


def columns(dq, dk, dv, first, at):
    out = []
    for g in range(first, first + 3):
        ref = (dq, dk, dv)[g // 6]
        out.append(ref[g % 6, at, :])
    return jnp.concatenate(out, axis=1)


def first_norm_back_body(tok, dq, dk, dv, wq, dh, vec, gt_o, sums_o):
    gain1 = vec[ROW_OF["gain1"] : ROW_OF["gain1"] + 1, :]
    sums_o[...] = jnp.zeros_like(sums_o)
    for r in range(4):
        at = pl.ds(QB * r, QB)
        da1 = jnp.zeros((QB, D), f32)
        for b in range(6):
            da1 += nt(columns(dq, dk, dv, 3 * b, at), wq[b // 3, b % 3])
        n1, r1 = normalize(tok[at, :].astype(f32))
        sums_o[0:1, :] += jnp.sum(da1 * n1, axis=0, keepdims=True)
        sums_o[1:2, :] += jnp.sum(da1, axis=0, keepdims=True)
        e = da1 * gain1
        back = r1 * (
            e
            - jnp.mean(e, axis=-1, keepdims=True)
            - n1 * jnp.mean(e * n1, axis=-1, keepdims=True)
        )
        gt_o[at, :] = (dh[at, :] + back).astype(bf16)


def first_norm_back(tokens, dq, dk, dv, wq, dh, vec):
    return pl.pallas_call(
        first_norm_back_body,
        out_shape=(sds((ROWS, D), bf16), sds((8, D), f32)),
        in_specs=[VM] * 7,
        out_specs=(VM, VM),
        name="first_norm_back",
        **params(2 * ROWS * D * 2304, 18e6),
    )(tokens, dq, dk, dv, wq, dh, vec)


def qkv_grad_body(pieces, meta, a1t, dq, dk, dv, dwo, mid, att, fst, own, other, st_q, st_o, st_v, sem):
    everything = pl.ds(0, ROWS)

    def emit_at(src, i, core, y, row):
        rows = src.shape[0]
        if pieces:
            q, k, mine = slot_for(meta, i, core, y)

            @pl.when(mine)
            def _():
                pltpu.make_async_copy(src, own.at[q, k, pl.ds(row, rows)], sem).start()

            @pl.when(jnp.logical_not(mine))
            def _():
                pltpu.make_async_copy(src, other.at[q, k, pl.ds(row, rows)], sem).start()
        else:
            pltpu.make_async_copy(src, own.at[i, 2 * y + core, pl.ds(row, rows)], sem).start()

    rows = {
        "qv": att[0:1, :],
        "outb": mid[3:4, :],
        "downb": mid[0:1, :],
        "gain1": fst[0:1, :],
        "shift1": fst[1:2, :],
        "gain2": mid[1:2, :],
        "shift2": mid[2:3, :],
    }

    def vec_row(r):
        if r == 1:
            return att[1:2, :]
        for name, start in ROW_OF.items():
            if name in rows and start == r:
                return rows[name]
        r -= ROW_OF["upb"]
        return mid[4 + r : 5 + r, :]

    small = pack_small(vec_row)
    st_v[...] = jnp.broadcast_to(small[:, None, :], (32, 8, 384)).reshape(256, 384).astype(bf16)
    for i in range(8):
        for n in range(4):
            emit_at(st_v.at[pl.ds((i * 4 + n) * 8, 8)], i, n % 2, n // 2, 192)
    for y in range(2):
        st_o[y] = dwo[:, 384 * y : 384 * y + 384]
        for i in range(8):
            for core in range(2):
                emit_at(st_o.at[y, pl.ds((2 * i + core) * 48, 48)], i, core, y, 144)
    for y in range(2):
        for t in range(3):
            st_q[y, t] = nn(a1t[...], columns(dq, dk, dv, 9 * y + 3 * t, everything)).astype(bf16)
            for i in range(8):
                for core in range(2):
                    emit_at(st_q.at[y, t, pl.ds((2 * i + core) * 48, 48)], i, core, y, 48 * t)
    pltpu.make_async_copy(st_v, st_v, sem).wait()
    pltpu.make_async_copy(st_o, st_o, sem).wait()
    pltpu.make_async_copy(st_q, st_q, sem).wait()


def qkv_grad(pieces, meta, a1t, dq, dk, dv, dwo, mid, att, fst):
    if pieces:
        grads = (sds((4, 4, FAM_Q, 384), bf16), sds((4, 4, FAM_Q, 384), bf16))
    else:
        grads = (sds((8, 4, FAM_Q, 384), bf16), sds((8, 128), bf16))
    return pl.pallas_call(
        lambda *refs: qkv_grad_body(pieces, *refs),
        out_shape=grads,
        in_specs=[SM] + [VM] * 8,
        out_specs=(HB, HB),
        scratch_shapes=[
            pltpu.VMEM((2, 3, D, 384), bf16),
            pltpu.VMEM((2, D, 384), bf16),
            pltpu.VMEM((256, 384), bf16),
            pltpu.SemaphoreType.DMA(()),
        ],
        name="qkv_grad",
        **params(2 * ROWS * D * 2304, 16e6),
    )(meta, a1t, dq, dk, dv, dwo, mid, att, fst)


def links(step):
    pairs = []
    for z in range(4):
        for x in range(2):
            for y in range(2):
                for c in range(2):
                    tz, tx, ty, tc = step(z, x, y, c)
                    pairs.append(((z * 2 + x) * 4 + y * 2 + c, (tz * 2 + tx) * 4 + ty * 2 + tc))
    return pairs


TO_CORE = links(lambda z, x, y, c: (z, x, y, 1 - c))
TO_FIRST = links(lambda z, x, y, c: (z, 1 - x, y, c) if c == 0 else (z, x, 1 - y, c))
TO_SECOND = links(lambda z, x, y, c: (z, x, 1 - y, c) if c == 0 else (z, 1 - x, y, c))
TO_Z = [None] + [links(lambda z, x, y, c, k=k: (z ^ k, x, y, c)) for k in (1, 2, 3)]


def send(value, pairs):
    return lax.ppermute(value, BOTH, pairs)


def spread(piece):
    line = jnp.stack([piece] + [send(piece, TO_Z[k]) for k in (1, 2, 3)], axis=0)
    first = send(line, TO_FIRST)
    second = send(line, TO_SECOND)
    corner = send(first, TO_SECOND)
    mine = (line, first, second, corner)
    return mine + tuple(send(part, TO_CORE) for part in mine)


def add(*parts):
    total = parts[0].astype(f32)
    for part in parts[1:]:
        total = total + part.astype(f32)
    return total


def gather_up(own, other):
    got = send(other, TO_CORE)
    corner = send(add(own[3], got[3]).astype(bf16), TO_SECOND)
    second = send(add(own[2], got[2]).astype(bf16), TO_SECOND)
    first = send(add(own[1], got[1], corner).astype(bf16), TO_FIRST)
    mine = [add(own[0, k], got[0, k], first[k], second[k]) for k in range(4)]
    far = [send(mine[k].astype(bf16), TO_Z[k]) for k in (1, 2, 3)]
    return add(mine[0], *far)


def fast_weights(qkv_weight, out_weight, up_weight, down_weight, small):
    core = lax.axis_index("narrow") % 2
    both = jnp.concatenate([qkv_weight, out_weight], axis=1).astype(bf16)
    keep = jnp.where(core == 0, both[:48], both[48:])
    give = jnp.where(core == 0, both[48:], both[:48])
    got = send(give, TO_CORE)
    left = jnp.where(core == 0, keep, got)
    right = jnp.where(core == 0, got, keep)
    wide_rows = jnp.concatenate([left[:, :576], right[:, :576]], axis=1)
    piece_q = jnp.concatenate(
        [
            wide_rows[:, :384],
            wide_rows[:, 384:768],
            wide_rows[:, 768:],
            jnp.concatenate([left[:, 576:], right[:, 576:]], axis=1),
            small,
        ],
        axis=0,
    )
    up = up_weight.astype(bf16)
    piece_m = jnp.concatenate([up[:, :384], up[:, 384:], down_weight.astype(bf16).T], axis=0)
    return spread(piece_q), spread(piece_m)


def fast_grads(own_q, other_q, own_m, other_m):
    core = lax.axis_index("narrow") % 2
    total_m = gather_up(own_m, other_m)
    grad_up = jnp.concatenate([total_m[:96], total_m[96:192]], axis=1)
    grad_down = total_m[192:].T
    total_q = gather_up(own_q, other_q)
    cols = jnp.concatenate([total_q[:48], total_q[48:96], total_q[96:144]], axis=1)
    outs = total_q[144:192]
    low = jnp.concatenate([cols[:, :576], outs[:, :192]], axis=1)
    high = jnp.concatenate([cols[:, 576:], outs[:, 192:]], axis=1)
    keep = jnp.where(core == 0, low, high)
    got = send(jnp.where(core == 0, high, low), TO_CORE)
    rows = jnp.concatenate(
        [jnp.where(core == 0, keep, got), jnp.where(core == 0, got, keep)], axis=0
    )
    return rows[:, :576], rows[:, 576:], grad_up, grad_down, total_q[192]


def whole(value, dims):
    for axis, dim in dims:
        value = lax.all_gather(value, axis, axis=dim, tiled=True)
    return value


def plain_weights(qkv_weight, out_weight, up_weight, down_weight, vectors):
    matrix = lambda w: whole(w.astype(bf16), (("narrow", 1), ("wide", 0)))
    wq = matrix(qkv_weight).reshape(D, 2, 3, 384).transpose(1, 2, 0, 3)
    wo = matrix(out_weight).reshape(D, 2, 384).transpose(1, 0, 2)
    up = matrix(up_weight).reshape(D, 4, D).transpose(1, 0, 2)
    down = matrix(down_weight).reshape(4, D, D).transpose(0, 2, 1)
    rows = [
        whole(vectors[name].astype(bf16), (("narrow", 0), ("wide", 0))).astype(f32).reshape(count, D)
        for name, _, _, count in SMALL
    ]
    vec = jnp.concatenate(rows + [jnp.zeros((VECS - 12, D), f32)], axis=0)
    return (wq, wo, vec), (up, down)


def plain_grads(all_q, all_m):
    def reduce(matrix):
        rows = lax.psum_scatter(matrix.astype(f32), "wide", scatter_dimension=0, tiled=True)
        return lax.psum_scatter(rows.astype(bf16), "narrow", scatter_dimension=1, tiled=True).astype(f32)

    def vector(values):
        rows = lax.psum_scatter(values, "wide", scatter_dimension=0, tiled=True)
        return lax.psum_scatter(rows.astype(bf16), "narrow", scatter_dimension=0, tiled=True).astype(f32)

    q = all_q[:, :, :192].reshape(8, 2, 2, 4, 48, 384)
    qkv = q[:, :, :, :3].transpose(0, 2, 4, 1, 3, 5).reshape(D, 2304)
    out = q[:, :, :, 3].transpose(0, 2, 3, 1, 4).reshape(D, D)
    m = all_m.reshape(8, 4, 2, 192, 384)
    up = m[:, :, 0].reshape(8, 4, 2, 96, 384).transpose(0, 3, 1, 2, 4).reshape(D, FF)
    down = m[:, :, 1].transpose(0, 3, 1, 2).reshape(FF, D)
    small = all_q[:, :, 192].reshape(32, 384).astype(f32)
    vecs = {name: vector(small[:, off : off + wd].reshape(-1)) for name, off, wd, _ in SMALL}
    return reduce(qkv), reduce(out), reduce(up), reduce(down), vecs


def local(
    tokens,
    qkv_weight,
    qv_bias,
    out_weight,
    out_bias,
    up_weight,
    up_bias,
    down_weight,
    down_bias,
    norm1_gain,
    norm1_bias,
    norm2_gain,
    norm2_bias,
    lengths,
    cotangent,
    fast,
):
    vectors = {
        "qv": qv_bias,
        "outb": out_bias,
        "downb": down_bias,
        "gain1": norm1_gain,
        "shift1": norm1_bias,
        "gain2": norm2_gain,
        "shift2": norm2_bias,
        "upb": up_bias,
    }
    meta = jnp.stack([lax.axis_index("wide"), lax.axis_index("narrow")]).astype(jnp.int32)
    if fast:
        zeros = lambda size: jnp.zeros((size,), f32)
        small = jnp.concatenate(
            [qv_bias, out_bias, down_bias, norm1_gain, zeros(8)]
            + [norm1_bias, norm2_gain, norm2_bias, zeros(56), up_bias, zeros(32)]
        )
        small = jnp.broadcast_to(small.astype(bf16)[None], (8, 384))
        weights_q, weights_m = fast_weights(qkv_weight, out_weight, up_weight, down_weight, small)
    else:
        weights_q, weights_m = plain_weights(
            qkv_weight, out_weight, up_weight, down_weight, vectors
        )
    a1, a1t, qkv, wq, wo, vec = project(fast, meta, tokens, weights_q)
    attended, lse = attend(lengths, qkv)
    output, dh, do, own_m, other_m, dwo, mid = middle(
        fast, meta, lengths, tokens, attended, cotangent, vec, wo, weights_m
    )
    dq, dk, dv, att = attend_back(lengths, qkv, do, lse)
    grad_tokens, fst = first_norm_back(tokens, dq, dk, dv, wq, dh, vec)
    own_q, other_q = qkv_grad(fast, meta, a1t, dq, dk, dv, dwo, mid, att, fst)
    if fast:
        g_qkv, g_out, g_up, g_down, row = fast_grads(own_q, other_q, own_m, other_m)
        vecs = {name: row[off : off + wd] for name, off, wd, _ in SMALL}
    else:
        g_qkv, g_out, g_up, g_down, vecs = plain_grads(own_q, own_m)
    return (
        output,
        grad_tokens,
        g_qkv,
        vecs["qv"],
        g_out,
        vecs["outb"],
        g_up,
        vecs["upb"],
        g_down,
        vecs["downb"],
        vecs["gain1"],
        vecs["shift1"],
        vecs["gain2"],
        vecs["shift2"],
    )


def solution(mesh):
    fast = mesh.shape["wide"] == 8 and mesh.shape["narrow"] == 4
    rows, matrix, vector = P(BOTH, None), P("wide", "narrow"), P(BOTH)
    return jax.shard_map(
        lambda *args: local(*args, fast),
        mesh=mesh,
        in_specs=(
            rows, matrix, vector, matrix, vector, matrix, vector, matrix, vector,
            vector, vector, vector, vector, rows, rows,
        ),
        out_specs=(
            rows, rows, matrix, vector, matrix, vector, matrix, vector, matrix, vector,
            vector, vector, vector, vector,
        ),
        check_vma=False,
    )
```

```python
import jax
import jax.numpy as jnp
import numpy as np
from jax import lax
from jax.experimental import pallas as pl
from jax.experimental.pallas import tpu as pltpu
from jax.sharding import PartitionSpec as P

HEADS = 12
BOTH = ("wide", "narrow")
bf16 = jnp.bfloat16
f32 = jnp.float32
epsilon = 1e-05
branch_scale = 24 ** (-0.5)
D = 768
FF = 3072
HD = 64
ROWS = 1024
QB = 256
NEG = -1e30
UNIT = (48, 128)
SMALL = (
    ("qv", 0, 48, 2),
    ("outb", 48, 24, 1),
    ("downb", 72, 24, 1),
    ("gain1", 96, 24, 1),
    ("shift1", 128, 24, 1),
    ("gain2", 152, 24, 1),
    ("shift2", 176, 24, 1),
    ("upb", 256, 96, 4),
)
ROW_OF = {}
_row = 0
for _name, _off, _wd, _n in SMALL:
    ROW_OF[_name] = _row
    _row += _n
VECS = 16


def nn(a, b):
    return lax.dot_general(a, b, (((1,), (0,)), ((), ())), preferred_element_type=f32)


def nt(a, b):
    return lax.dot_general(a, b, (((1,), (1,)), ((), ())), preferred_element_type=f32)


def normalize(values):
    average = jnp.mean(values, axis=-1, keepdims=True)
    centred = values - average
    spread = jnp.mean(centred * centred, axis=-1, keepdims=True)
    rinv = lax.rsqrt(spread + epsilon)
    return centred * rinv, rinv


def params(flops, bytes_accessed):
    return dict(
        compiler_params=pltpu.CompilerParams(vmem_limit_bytes=60 * 1024 * 1024),
        cost_estimate=pl.CostEstimate(
            flops=int(flops), transcendentals=0, bytes_accessed=int(bytes_accessed)
        ),
    )


VM = pl.BlockSpec(memory_space=pltpu.VMEM)
SM = pl.BlockSpec(memory_space=pltpu.SMEM)
HB = pl.BlockSpec(memory_space=pl.ANY)


def sds(shape, dtype):
    return jax.ShapeDtypeStruct(shape, dtype)


def over_rows(body, blocks=ROWS // QB):
    def step(r, carry):
        body(pl.ds(pl.multiple_of(r * QB, QB), QB), r)
        return carry

    lax.fori_loop(0, blocks, step, 0)


def wait(ref, sem):
    pltpu.make_async_copy(ref, ref, sem).wait()


def lanes(ref, count):
    return jnp.concatenate([ref[g].reshape(D, 128) for g in range(count)], axis=1)


def held_by(meta, q, k, own):
    w, n = meta[0], meta[1]
    z, x, y, c = w // 2, w % 2, n // 2, n % 2
    core = c if own else 1 - c
    first, second = q % 2, q // 2
    dx = jnp.where(core == 0, first, second)
    dy = jnp.where(core == 0, second, first)
    zz = z ^ k
    return zz * 2 + (x ^ dx), core, y ^ dy


def piece_loop(meta, quads, issue):
    for own in (True, False):
        for q in range(4):
            ref = quads[q if own else 4 + q]
            for k in range(4):
                i, core, y = held_by(meta, q, k, own)
                issue(ref.at[k], i, core, y)


def place_loop(pieces, meta, own, other, issue):
    if pieces:
        for mine, ref in ((True, own), (False, other)):
            for q in range(4):
                for k in range(4):
                    i, core, y = held_by(meta, q, k, mine)
                    issue(ref.at[q, k], i, core, y)
    else:
        for i in range(8):
            for n in range(4):
                issue(own.at[i, n], i, n % 2, n // 2)


def places(pieces, units):
    if pieces:
        return (sds((4, 4, units) + UNIT, bf16), sds((4, 4, units) + UNIT, bf16))
    return (sds((8, 4, units) + UNIT, bf16), sds((8, 128), bf16))


def small_map(off, wd, row):
    lane = lax.broadcasted_iota(jnp.int32, (128, D), 1) + row * D
    within = lane - wd * jnp.floor((lane.astype(f32) + 0.5) * (1.0 / wd)).astype(jnp.int32)
    src = lax.broadcasted_iota(jnp.int32, (128, D), 0)
    return jnp.where(src == within + off % 128, 1.0, 0.0).astype(bf16)


def unpack_small(packed):
    rows = []
    for _, off, wd, count in SMALL:
        base = off // 128 * 16
        group = packed[:, base : base + 16, :].astype(f32)[:, 0, :].astype(bf16)
        for row in range(count):
            spread = nn(group, small_map(off, wd, row))
            lane = lax.broadcasted_iota(jnp.int32, (32, D), 1) + row * D
            low = lax.broadcasted_iota(jnp.int32, (32, D), 0) * wd
            keep = (lane >= low) & (lane < low + wd)
            rows.append(jnp.sum(jnp.where(keep, spread, 0.0), axis=0, keepdims=True))
    rows.append(jnp.zeros((VECS - len(rows), D), f32))
    return jnp.concatenate(rows, axis=0)


def pack_small(vec_row):
    groups = [jnp.zeros((32, 128), f32) for _ in range(3)]
    for name, off, wd, count in SMALL:
        for row in range(count):
            lane = lax.broadcasted_iota(jnp.int32, (32, D), 1) + row * D
            low = lax.broadcasted_iota(jnp.int32, (32, D), 0) * wd
            keep = (lane >= low) & (lane < low + wd)
            spread = jnp.where(keep, vec_row(ROW_OF[name] + row), 0.0).astype(bf16)
            groups[off // 128] += nt(spread, small_map(off, wd, row))
    return groups


def attend_rows(far, get, put):
    lane = lax.broadcasted_iota(jnp.int32, (QB, 128), 1)
    causal = lax.broadcasted_iota(jnp.int32, (QB, QB), 1) <= lax.broadcasted_iota(
        jnp.int32, (QB, QB), 0
    )
    for j in range(ROWS // QB):
        size = QB * (j + 1)
        q = get(0, QB * j, QB)
        outs, logs = [], []
        for h in range(2):
            mine = (lane < HD) if h == 0 else (lane >= HD)
            s = nt(jnp.where(mine, q, jnp.zeros_like(q)), get(1, 0, size))
            parts = []
            if j >= 2:
                parts.append(s[:, :512] + far)
                if j == 3:
                    parts.append(s[:, 512:768])
            elif j == 1:
                parts.append(s[:, :QB])
            parts.append(jnp.where(causal, s[:, size - QB :], NEG))
            s = jnp.concatenate(parts, axis=1)
            top = jnp.max(s, axis=1, keepdims=True)
            e = jnp.exp(s - top)
            total = jnp.sum(e, axis=1, keepdims=True)
            outs.append(nn(e.astype(bf16), get(2, 0, size)) * (1.0 / total))
            logs.append(top + jnp.log(total))
        put(QB * j, jnp.where(lane < HD, outs[0], outs[1]).astype(bf16), jnp.where(lane == 0, logs[0], logs[1]).T[:8])


def front_body(pieces, third, meta, lens, *refs):
    count = 8 if pieces else 1
    if third == 0:
        tok, quads, refs = refs[0], refs[1 : 1 + count], refs[1 + count :]
        if not pieces:
            vec_i, refs = refs[0], refs[1:]
        a1, a1t_o, vec, *refs = refs
    else:
        a1, vec, quads, refs = refs[0], refs[1], refs[2 : 2 + count], refs[2 + count :]
    qkv_o, o_o, lse_o, wq, packed, sem, sem2 = refs
    if pieces:

        def issue(ref, i, core, y):
            pltpu.make_async_copy(
                ref.at[pl.ds(3 * third, 3)], wq.at[pl.ds(3 * y, 3), 2 * i + core], sem
            ).start()
            if third == 0:
                pltpu.make_async_copy(ref.at[9], packed.at[i * 4 + 2 * y + core], sem2).start()

        piece_loop(meta, quads, issue)
    else:
        pltpu.make_async_copy(quads[0], wq, sem).start()
    if third == 0:
        if pieces:
            wait(packed, sem2)
            vec[...] = unpack_small(packed[...])
        else:
            vec[...] = vec_i[...]
        def first_norm(at, r):
            n1, _ = normalize(tok[at, :].astype(f32))
            a1[at, :] = (
                n1 * vec[ROW_OF["gain1"] : ROW_OF["gain1"] + 1, :]
                + vec[ROW_OF["shift1"] : ROW_OF["shift1"] + 1, :]
            ).astype(bf16)

        over_rows(first_norm)
        a1t_o[...] = a1[...].T
    wait(wq, sem)
    bias = []
    for g, row in ((0, 0), (1, 0), (4, 1), (5, 1)):
        lane = 128 * (third + 3 * (g % 2))
        bias.append(vec[ROW_OF["qv"] + row : ROW_OF["qv"] + row + 1, lane : lane + 128])
    zero = jnp.zeros((1, 128), f32)
    bias = jnp.concatenate([bias[0], bias[1], zero, zero, bias[2], bias[3]], axis=1)
    weights = lanes(wq, 6)

    def projection(at, r):
        block = (nn(a1[at, :], weights) + bias).astype(bf16)
        for g in range(6):
            part = block[:, 128 * g : 128 * g + 128]
            qkv_o[g, at, :] = part * jnp.asarray(1.0 / HD, bf16) if g < 2 else part

    over_rows(projection)
    far = jnp.where(lens[0, 0] < ROWS, NEG, 0.0).astype(f32)

    def one(pair, carry):
        def put(row, o, lse):
            o_o[pair, row : row + QB, :] = o
            lse_o[pair, :, row : row + QB] = lse

        attend_rows(far, lambda which, row, n: qkv_o[2 * which + pair, row : row + n, :], put)
        return carry

    lax.fori_loop(0, 2, one, 0)


def front(pieces, third, meta, lens, first, vec, weights):
    shapes = [
        sds((6, ROWS, 128), bf16),
        sds((2, ROWS, 128), bf16),
        sds((2, 8, ROWS), f32),
        sds((6, 16) + UNIT, bf16),
    ]
    if third == 0:
        shapes = [sds((ROWS, D), bf16), sds((D, ROWS), bf16), sds((VECS, D), f32)] + shapes
        args = (first,) + tuple(weights) + (() if pieces else (vec,))
        specs = [VM] + [HB] * len(weights) + ([] if pieces else [VM])
    else:
        args = (first, vec) + tuple(weights)
        specs = [VM, VM] + [HB] * len(weights)
    return pl.pallas_call(
        lambda *refs: front_body(pieces, third, *refs),
        out_shape=tuple(shapes),
        in_specs=[SM, SM] + specs,
        out_specs=(VM,) * len(shapes),
        scratch_shapes=[
            pltpu.VMEM((32,) + UNIT, bf16),
            pltpu.SemaphoreType.DMA(()),
            pltpu.SemaphoreType.DMA(()),
        ],
        name=f"front_{third}",
        **params(20e9 if third == 0 else 13e9, 8e6),
    )(meta, lens, *args)


ROW_DN, ROW_G2, ROW_B2, ROW_OB, ROW_UP = 0, 1, 2, 3, 4


def middle_body(pieces, meta, lens, tok, o_0, o_1, o_2, cot, vec, *refs):
    count = 8 if pieces else 3
    quads, refs = refs[:count], refs[count:]
    out_o, dh_o, do_o, own_a, other_a, own_b, other_b, sums_o = refs[:8]
    (
        wo, wup, wdn, h_s, a2_s, a2t_s, dm_s, dmt_s, m_s, da2_s, gl_s, dz_s, st_u, st_d, st_o, upb_s,
        sem_w, sem_m, sem_o, sem_p,
    ) = refs[8:]
    if pieces:

        def issue(ref, i, core, y):
            n = 2 * y + core
            pltpu.make_async_copy(
                ref.at[pl.ds(24, 3)], wo.at[pl.ds(3 * y, 3), 2 * i + core], sem_w
            ).start()
            for third in range(3):
                base = 8 * third
                for half in range(2):
                    pltpu.make_async_copy(
                        ref.at[pl.ds(base + 2 * half, 2)],
                        wup.at[third, 2 * n + half, pl.ds(2 * i, 2)],
                        sem_m,
                    ).start()
                pltpu.make_async_copy(
                    ref.at[pl.ds(base + 4, 4)], wdn.at[third, i, pl.ds(4 * n, 4)], sem_m
                ).start()

        piece_loop(meta, quads, issue)
    else:
        pltpu.make_async_copy(quads[0], wo, sem_w).start()
        pltpu.make_async_copy(quads[1], wup, sem_m).start()
        pltpu.make_async_copy(quads[2], wdn, sem_m).start()
    total = lens[0, 0] + lens[0, 1]
    row_of = lambda name: vec[ROW_OF[name] : ROW_OF[name] + 1, :]
    gain2, shift2, outb, downb = (row_of(n) for n in ("gain2", "shift2", "outb", "downb"))
    for t in range(3):
        upb_s[t : t + 1, :] = jnp.concatenate(
            [
                vec[
                    ROW_OF["upb"] + i // 2 : ROW_OF["upb"] + i // 2 + 1,
                    384 * (i % 2) + 128 * t : 384 * (i % 2) + 128 * t + 128,
                ]
                for i in range(8)
            ],
            axis=1,
        )
    sums_o[...] = jnp.zeros_like(sums_o)

    def attended(at):
        return jnp.concatenate([ref[p, at, :] for p in range(2) for ref in (o_0, o_1, o_2)], axis=1)

    wait(wo, sem_w)
    w_out = lanes(wo, 6)

    def prologue(at, r):
        h = tok[at, :].astype(f32) + branch_scale * (nn(attended(at), w_out) + outb)
        h_s[at, :] = h
        n2, _ = normalize(h)
        a2_s[at, :] = (n2 * gain2 + shift2).astype(bf16)
        live = (lax.broadcasted_iota(jnp.int32, (QB, D), 0) + QB * r) < total
        dm = (branch_scale * jnp.where(live, cot[at, :].astype(f32), 0.0)).astype(bf16)
        dm_s[at, :] = dm
        sums_o[ROW_DN : ROW_DN + 1, :D] += jnp.sum(dm.astype(f32), axis=0, keepdims=True)

    over_rows(prologue)
    a2t_s[...] = a2_s[...].T
    dmt_s[...] = dm_s[...].T
    m_s[...] = jnp.zeros_like(m_s)
    da2_s[...] = jnp.zeros_like(da2_s)
    wait(wup, sem_m)
    wait(wdn, sem_m)
    c0 = 0.7978845608028654
    c1 = 0.044715 * c0

    def emit(own, other, base):
        def issue(ref, i, core, y):
            n = 2 * y + core
            for half in range(2):
                pltpu.make_async_copy(
                    st_u.at[2 * n + half, pl.ds(2 * i, 2)], ref.at[pl.ds(base + 2 * half, 2)], sem_o
                ).start()
            pltpu.make_async_copy(
                st_d.at[i, pl.ds(4 * n, 4)], ref.at[pl.ds(base + 4, 4)], sem_o
            ).start()

        place_loop(pieces, meta, own, other, issue)

    def step(t, carry):
        up = lanes(wup.at[t], 8)
        dn = lanes(wdn.at[t], 8)
        bup = upb_s[pl.ds(t, 1), :]
        sums_o[pl.ds(ROW_UP + t, 1), :] = jnp.zeros((1, 1024), f32)

        def some(r, carry):
            at = pl.ds(pl.multiple_of(r * 256, 256), 256)
            z = nn(a2_s[at, :], up) + bup
            dgl = nn(dm_s[at, :], dn)
            zz = z * z
            th = jnp.tanh(z * (c0 + c1 * zz))
            half = 0.5 * th + 0.5
            gl = (z * half).astype(bf16)
            slope = half + (0.5 * z) * (1.0 - th * th) * (c0 + (3.0 * c1) * zz)
            dz = (dgl * slope).astype(bf16)
            gl_s[at, :] = gl
            dz_s[at, :] = dz
            sums_o[pl.ds(ROW_UP + t, 1), :] += jnp.sum(dz.astype(f32), axis=0, keepdims=True)
            m_s[at, :] += nt(gl, dn)
            da2_s[at, :] += nt(dz, up)
            return carry

        lax.fori_loop(0, 4, some, 0)

        @pl.when(t >= 1)
        def _():
            wait(st_u, sem_o)
            wait(st_d, sem_o)


        def some_rows(r, carry):
            at = pl.ds(pl.multiple_of(r * 384, 128), 384)
            for to, left, right in ((st_u, a2t_s, dz_s), (st_d, dmt_s, gl_s)):
                grad = nn(left[at, :], right[...]).astype(bf16)
                for b in range(8):
                    to[b, pl.ds(8 * r, 8)] = grad[:, 128 * b : 128 * b + 128].reshape((8,) + UNIT)
            return carry

        lax.fori_loop(0, 2, some_rows, 0)

        @pl.when(t == 0)
        def _():
            emit(own_a, other_a, 0)

        @pl.when(t == 1)
        def _():
            emit(own_a, other_a, 8)

        @pl.when(t == 2)
        def _():
            emit(own_b, other_b, 0)

        return carry

    lax.fori_loop(0, 3, step, 0)

    def epilogue(at, r):
        h = h_s[at, :]
        out_o[at, :] = (h + branch_scale * (m_s[at, :] + downb)).astype(bf16)
        n2, r2 = normalize(h)
        da2 = da2_s[at, :]
        sums_o[ROW_G2 : ROW_G2 + 1, :D] += jnp.sum(da2 * n2, axis=0, keepdims=True)
        sums_o[ROW_B2 : ROW_B2 + 1, :D] += jnp.sum(da2, axis=0, keepdims=True)
        e = da2 * gain2
        live = (lax.broadcasted_iota(jnp.int32, (QB, D), 0) + QB * r) < total
        dy = jnp.where(live, cot[at, :].astype(f32), 0.0)
        dh = dy + r2 * (
            e
            - jnp.mean(e, axis=-1, keepdims=True)
            - n2 * jnp.mean(e * n2, axis=-1, keepdims=True)
        )
        dh_o[at, :] = dh
        du = (branch_scale * dh).astype(bf16)
        sums_o[ROW_OB : ROW_OB + 1, :D] += jnp.sum(du.astype(f32), axis=0, keepdims=True)
        dm_s[at, :] = du
        do = nt(du, w_out).astype(bf16)
        for g in range(6):
            do_o[g, at, :] = do[:, 128 * g : 128 * g + 128]

    over_rows(epilogue)
    a2t_s[...] = attended(pl.ds(0, ROWS)).T
    grad = nn(a2t_s[...], dm_s[...])
    for g in range(6):
        st_o[g] = grad[:, 128 * g : 128 * g + 128].astype(bf16).reshape((16,) + UNIT)

    def issue_out(ref, i, core, y):
        pltpu.make_async_copy(
            st_o.at[pl.ds(3 * y, 3), 2 * i + core], ref.at[pl.ds(8, 3)], sem_p
        ).start()

    place_loop(pieces, meta, own_b, other_b, issue_out)
    wait(st_u, sem_o)
    wait(st_d, sem_o)
    wait(st_o, sem_p)


def middle(pieces, meta, lens, tokens, attended, cotangent, vec, weights):
    block = (16,) + UNIT
    return pl.pallas_call(
        lambda *refs: middle_body(pieces, *refs),
        out_shape=(
            sds((ROWS, D), bf16),
            sds((ROWS, D), f32),
            sds((6, ROWS, 128), bf16),
            *places(pieces, 16),
            *places(pieces, 11),
            sds((8, 1024), f32),
        ),
        in_specs=[SM, SM, VM, VM, VM, VM, VM, VM] + [HB] * len(weights),
        out_specs=(VM, VM, VM, HB, HB, HB, HB, VM),
        scratch_shapes=[
            pltpu.VMEM((6,) + block, bf16),
            pltpu.VMEM((3, 8) + block, bf16),
            pltpu.VMEM((3, 8) + block, bf16),
            pltpu.VMEM((ROWS, D), f32),
            pltpu.VMEM((ROWS, D), bf16),
            pltpu.VMEM((D, ROWS), bf16),
            pltpu.VMEM((ROWS, D), bf16),
            pltpu.VMEM((D, ROWS), bf16),
            pltpu.VMEM((ROWS, D), f32),
            pltpu.VMEM((ROWS, D), f32),
            pltpu.VMEM((ROWS, 1024), bf16),
            pltpu.VMEM((ROWS, 1024), bf16),
            pltpu.VMEM((8,) + block, bf16),
            pltpu.VMEM((8,) + block, bf16),
            pltpu.VMEM((6,) + block, bf16),
            pltpu.VMEM((8, 1024), f32),
            pltpu.SemaphoreType.DMA(()),
            pltpu.SemaphoreType.DMA(()),
            pltpu.SemaphoreType.DMA(()),
            pltpu.SemaphoreType.DMA(()),
        ],
        name="middle",
        **params(60e9, 40e6),
    )(meta, lens, tokens, *attended, cotangent, vec, *weights)


def back_pair(far, q_ref, k_ref, v_ref, do_ref, lse_ref, out, pair, dk_s, dv_s):
    lane = lax.broadcasted_iota(jnp.int32, (QB, 128), 1)
    causal = lax.broadcasted_iota(jnp.int32, (QB, QB), 0) <= lax.broadcasted_iota(
        jnp.int32, (QB, QB), 1
    )
    kt = k_ref[...].T
    sub = lax.broadcasted_iota(jnp.int32, (128, ROWS), 0)
    dk_s[...] = jnp.zeros_like(dk_s)
    dv_s[...] = jnp.zeros_like(dv_s)
    for j in range(ROWS // QB):
        size = QB * (j + 1)
        q = q_ref[QB * j : size, :]
        do = do_ref[QB * j : size, :]
        dq = jnp.zeros((128, QB), f32)
        dk = jnp.zeros((size, 128), f32)
        dv = jnp.zeros((size, 128), f32)
        for h in range(2):
            mine = (lane < HD) if h == 0 else (lane >= HD)
            qh = jnp.where(mine, q, jnp.zeros_like(q))
            doh = jnp.where(mine, do, jnp.zeros_like(do))
            s = nt(k_ref[:size, :], qh)
            parts = []
            if j >= 2:
                parts.append(s[:512] + far)
                if j == 3:
                    parts.append(s[512:768])
            elif j == 1:
                parts.append(s[:QB])
            parts.append(jnp.where(causal, s[size - QB :], NEG))
            s = jnp.concatenate(parts, axis=0)
            p = jnp.exp(s - lse_ref[h : h + 1, QB * j : size])
            dp = nt(v_ref[:size, :], doh)
            dot = jnp.sum(p * dp, axis=0, keepdims=True)
            ds = (p * (dp - dot)).astype(bf16)
            dv += nn(p.astype(bf16), doh)
            dk += nn(ds, qh)
            keep = (sub < HD) if h == 0 else (sub >= HD)
            dq += nn(jnp.where(keep, kt, jnp.zeros_like(kt))[:, :size], ds)
        out[pair, QB * j : size, :] = (dq.T * (1.0 / HD)).astype(bf16)
        dk_s[:size, :] += dk
        dv_s[:size, :] += dv
    out[2 + pair] = dk_s[...].astype(bf16)
    out[4 + pair] = dv_s[...].astype(bf16)


def back_body(pieces, third, meta, lens, qkv, do, lse, a1t, wq, vec, *refs):
    if third > 0:
        refs = refs[2:]
    if third == 2:
        mid, sums_0, sums_1, *refs = refs
    dqkv_o, own, other, sums_o, dk_s, dv_s, st, st_v, sem, sem2 = refs
    far = jnp.where(lens[0, 0] < ROWS, NEG, 0.0).astype(f32)

    def one(pair, carry):
        back_pair(
            far, qkv.at[pair], qkv.at[2 + pair], qkv.at[4 + pair], do.at[third + 3 * pair], lse.at[pair],
            dqkv_o, pair, dk_s, dv_s,
        )
        return carry

    lax.fori_loop(0, 2, one, 0)
    raw = jnp.zeros((D, 128), f32)
    plain = jnp.zeros((D, 128), f32)
    cols = []
    for two in range(3):
        blocks = nn(a1t[...], jnp.concatenate([dqkv_o[2 * two], dqkv_o[2 * two + 1]], axis=1))
        for g in (2 * two, 2 * two + 1):
            block = blocks[:, 128 * (g % 2) : 128 * (g % 2) + 128]
            col = jnp.sum(dqkv_o[g].astype(f32), axis=0, keepdims=True)
            cols.append(col)
            st[g] = block.astype(bf16).reshape((16,) + UNIT)
            weight = wq[g].reshape(D, 128).astype(f32)
            raw += block * weight
            plain += weight * col
    base = 3 * third

    def issue(ref, i, core, y):
        pltpu.make_async_copy(
            st.at[pl.ds(3 * y, 3), 2 * i + core], ref.at[pl.ds(base, 3)], sem
        ).start()

    place_loop(pieces, meta, own, other, issue)
    raw = jnp.sum(raw, axis=1, keepdims=True)
    plain = jnp.sum(plain, axis=1, keepdims=True)
    lane = lax.broadcasted_iota(jnp.int32, (D, 128), 1)
    flat = jnp.where(lane == 0, raw, plain).T[:8]
    sums = jnp.concatenate([jnp.concatenate(cols, axis=1), flat[:2], jnp.zeros((5, D), f32)], axis=0)
    sums_o[...] = sums
    if third == 2:
        per = [sums_0[...], sums_1[...], sums]
        raw = per[0][1:2] + per[1][1:2] + per[2][1:2]
        shift = per[0][2:3] + per[1][2:3] + per[2][2:3]
        row_of = lambda name: vec[ROW_OF[name] : ROW_OF[name] + 1, :]
        gain = (raw - row_of("shift1") * shift) / row_of("gain1")
        pick = lambda g: jnp.concatenate(
            [per[p % 3][0:1, 128 * (g + p // 3) : 128 * (g + p // 3) + 128] for p in range(6)], axis=1
        )
        known = {
            "outb": mid[ROW_OB : ROW_OB + 1, :D],
            "downb": mid[ROW_DN : ROW_DN + 1, :D],
            "gain1": gain,
            "shift1": shift,
            "gain2": mid[ROW_G2 : ROW_G2 + 1, :D],
            "shift2": mid[ROW_B2 : ROW_B2 + 1, :D],
        }
        rows = {ROW_OF["qv"]: pick(0), ROW_OF["qv"] + 1: pick(4)}
        for name, value in known.items():
            rows[ROW_OF[name]] = value
        for r in range(4):
            rows[ROW_OF["upb"] + r] = jnp.concatenate(
                [
                    mid[ROW_UP + t : ROW_UP + t + 1, 128 * i : 128 * i + 128]
                    for i in (2 * r, 2 * r + 1)
                    for t in range(3)
                ],
                axis=1,
            )
        groups = pack_small(lambda r: rows[r])
        for g in range(3):
            st_v[:, 16 * g : 16 * g + 16, :] = jnp.broadcast_to(
                groups[g][:, None, :], (32, 16, 128)
            ).astype(bf16)

        def issue_small(ref, i, core, y):
            pltpu.make_async_copy(st_v.at[i * 4 + 2 * y + core], ref.at[9], sem2).start()

        place_loop(pieces, meta, own, other, issue_small)
        wait(st_v, sem2)
    wait(st, sem)


def back(pieces, third, meta, lens, qkv, do, lse, a1t, wq, vec, before):
    args = [meta, lens, qkv, do, lse, a1t, wq, vec, *before]
    extra = [HB, HB] * (third > 0) + [VM, VM, VM] * (third == 2)
    return pl.pallas_call(
        lambda *refs: back_body(pieces, third, *refs),
        out_shape=(
            sds((6, ROWS, 128), bf16),
            *places(pieces, 10),
            sds((8, D), f32),
        ),
        in_specs=[SM, SM] + [VM] * 6 + extra,
        out_specs=(VM, HB, HB, VM),
        input_output_aliases={8: 1, 9: 2} if third > 0 else {},
        scratch_shapes=[
            pltpu.VMEM((ROWS, 128), f32),
            pltpu.VMEM((ROWS, 128), f32),
            pltpu.VMEM((6, 16) + UNIT, bf16),
            pltpu.VMEM((32,) + UNIT, bf16),
            pltpu.SemaphoreType.DMA(()),
            pltpu.SemaphoreType.DMA(()),
        ],
        name=f"back_{third}",
        **params(18e9, 8e6),
    )(*args)


def first_norm_back_body(tok, d_0, d_1, d_2, w_0, w_1, w_2, dh, vec, *refs):
    gt_o = refs[-1]
    gain1 = vec[ROW_OF["gain1"] : ROW_OF["gain1"] + 1, :]

    def body(at, r):
        da1 = jnp.zeros((QB, D), f32)
        for grad, weight in ((d_0, w_0), (d_1, w_1), (d_2, w_2)):
            rows = jnp.concatenate([grad[g, at, :] for g in range(6)], axis=1)
            da1 += nt(rows, lanes(weight, 6))
        n1, r1 = normalize(tok[at, :].astype(f32))
        e = da1 * gain1
        back = r1 * (
            e
            - jnp.mean(e, axis=-1, keepdims=True)
            - n1 * jnp.mean(e * n1, axis=-1, keepdims=True)
        )
        gt_o[at, :] = (dh[at, :] + back).astype(bf16)

    over_rows(body, 2)


def first_norm_back(half, tokens, grads, weights, dh, vec, before=None):
    count = ROWS // 2
    rows = pl.BlockSpec((count, D), lambda g: (half, 0))
    every = lambda shape: pl.BlockSpec(shape, lambda g: (0,) * len(shape))
    return pl.pallas_call(
        first_norm_back_body,
        grid=(1,),
        out_shape=sds((ROWS, D), bf16),
        in_specs=[rows]
        + [pl.BlockSpec((6, count, 128), lambda g: (0, half, 0))] * 3
        + [every((6, 16) + UNIT)] * 3
        + [rows, every((VECS, D))]
        + ([] if before is None else [HB]),
        out_specs=rows,
        input_output_aliases={} if before is None else {9: 0},
        name=f"first_norm_back_{half}",
        **params(8e9, 9e6),
    )(tokens, *grads, *weights, dh, vec, *(() if before is None else (before,)))


def links(step):
    pairs = []
    for z in range(4):
        for x in range(2):
            for y in range(2):
                for c in range(2):
                    tz, tx, ty, tc = step(z, x, y, c)
                    pairs.append(((z * 2 + x) * 4 + y * 2 + c, (tz * 2 + tx) * 4 + ty * 2 + tc))
    return pairs


TO_CORE = links(lambda z, x, y, c: (z, x, y, 1 - c))
TO_FIRST = links(lambda z, x, y, c: (z, 1 - x, y, c) if c == 0 else (z, x, 1 - y, c))
TO_SECOND = links(lambda z, x, y, c: (z, x, 1 - y, c) if c == 0 else (z, 1 - x, y, c))
TO_Z = [None] + [links(lambda z, x, y, c, k=k: (z ^ k, x, y, c)) for k in (1, 2, 3)]


def send(value, pairs):
    return lax.ppermute(value, BOTH, pairs)


def after(value, *others):
    return lax.optimization_barrier((value, *others))[0]


def add(*parts):
    total = parts[0].astype(f32)
    for part in parts[1:]:
        total = total + part.astype(f32)
    return total


def split(big, sizes):
    out, at = [], 0
    for size in sizes:
        out.append(big[at : at + size])
        at += size
    return out


def as_units(block):
    a, b = block.shape[0] // 48, block.shape[1] // 128
    return block.reshape(a, 48, b, 128).transpose(2, 0, 1, 3).reshape(a * b, 48, 128)


def first_pieces(qkv_weight, out_weight, small):
    core = lax.axis_index("narrow") % 2
    both = jnp.concatenate([qkv_weight, out_weight], axis=1).astype(bf16)
    keep = jnp.where(core == 0, both[:48], both[48:])
    give = jnp.where(core == 0, both[48:], both[:48])
    got = send(give, TO_CORE)
    left = jnp.where(core == 0, keep, got)
    right = jnp.where(core == 0, got, keep)
    cols = as_units(jnp.concatenate([left[:, :576], right[:, :576]], axis=1))
    out = as_units(jnp.concatenate([left[:, 576:], right[:, 576:]], axis=1))
    thirds = [cols[g] for t in range(3) for g in (t, 3 + t, 6 + t)]
    return jnp.concatenate([jnp.stack(thirds), small], axis=0), out


def feed_pieces(up_weight, down_weight):
    up = as_units(up_weight.astype(bf16))
    down = as_units(down_weight.astype(bf16).T)
    out = []
    for t in range(3):
        out.append(jnp.concatenate([up[2 * t : 2 * t + 2], up[6 + 2 * t : 8 + 2 * t], down[4 * t : 4 * t + 4]]))
    return out


def whole(value, dims):
    for axis, dim in dims:
        value = lax.all_gather(value, axis, axis=dim, tiled=True)
    return value


def plain_weights(qkv_weight, out_weight, up_weight, down_weight, vectors):
    matrix = lambda w: whole(w.astype(bf16), (("narrow", 1), ("wide", 0)))
    blocks = lambda w, b: w.reshape(16, 48, b, 128).transpose(2, 0, 1, 3)
    wq = blocks(matrix(qkv_weight), 18)
    wq = [jnp.stack([wq[g] for g in (t, 3 + t, 6 + t, 9 + t, 12 + t, 15 + t)]) for t in range(3)]
    wo = blocks(matrix(out_weight), 6)
    up = blocks(matrix(up_weight), 24).reshape(8, 3, 16, 48, 128).transpose(1, 0, 2, 3, 4)
    down = blocks(matrix(down_weight).T, 24).reshape(8, 3, 16, 48, 128).transpose(1, 0, 2, 3, 4)
    rows = [
        whole(vectors[name].astype(bf16), (("narrow", 0), ("wide", 0))).astype(f32).reshape(count, D)
        for name, _, _, count in SMALL
    ]
    vec = jnp.concatenate(rows + [jnp.zeros((VECS - 12, D), f32)], axis=0)
    return wq, wo, up, down, vec


def plain_grads(q_all, m_a, m_b):
    def reduce(matrix):
        rows = lax.psum_scatter(matrix.astype(f32), "wide", scatter_dimension=0, tiled=True)
        return lax.psum_scatter(rows.astype(bf16), "narrow", scatter_dimension=1, tiled=True).astype(f32)

    def vector(values):
        rows = lax.psum_scatter(values, "wide", scatter_dimension=0, tiled=True)
        return lax.psum_scatter(rows.astype(bf16), "narrow", scatter_dimension=0, tiled=True).astype(f32)

    q = q_all[:, :, :9].reshape(8, 2, 2, 3, 3, 48, 128)
    qkv = q.transpose(0, 2, 5, 1, 4, 3, 6).reshape(D, 2304)
    out = m_b[:, :, 8:].reshape(8, 2, 2, 3, 48, 128).transpose(0, 2, 4, 1, 3, 5).reshape(D, D)
    m = jnp.concatenate([m_a, m_b[:, :, :8]], axis=2).reshape(8, 4, 3, 2, 4, 48, 128)
    up = m[:, :, :, 0].reshape(8, 4, 3, 2, 2, 48, 128).transpose(0, 4, 5, 1, 3, 2, 6).reshape(D, FF)
    down = m[:, :, :, 1].transpose(0, 2, 5, 1, 3, 4).reshape(FF, D)
    small = q_all[:, :, 9].reshape(32, 3, 16, 128)[:, :, 0].reshape(32, 384).astype(f32)
    vecs = {name: vector(small[:, off : off + wd].reshape(-1)) for name, off, wd, _ in SMALL}
    return reduce(qkv), reduce(out), reduce(up), reduce(down), vecs


class Spread:
    def __init__(self, piece, *waits):
        near = send(after(piece, *waits), TO_Z[1])
        self.parts = [piece, near] + [send(piece, TO_Z[k]) for k in (2, 3)]

    def along(self, *waits):
        self.line = after(jnp.stack(self.parts, axis=0), *waits)
        self.first = send(self.line, TO_FIRST)
        self.second = send(self.line, TO_SECOND)

    def across(self, *waits):
        self.corner = send(after(self.first, *waits), TO_SECOND)

    def swap(self, *waits):
        self.swapped = [send(after(part, *waits), TO_CORE) for part in (self.line, self.first, self.second)]

    def end(self, *waits):
        last = send(after(self.corner, *waits), TO_CORE)
        return (self.line, self.first, self.second, self.corner, *self.swapped, last)


class Fold:
    def __init__(self, own, other):
        self.own = own
        self.got = send(other, TO_CORE)

    def second(self, *waits):
        self.got = after(self.got, *waits)
        self.sum_2 = add(self.own[2:], self.got[2:]).astype(bf16)
        self.sec = send(self.sum_2, TO_SECOND)

    def first(self, *waits):
        self.sec = after(self.sec, *waits)
        self.sum_1 = add(self.own[1], self.got[1], self.sec[1]).astype(bf16)
        self.fst = send(self.sum_1, TO_FIRST)

    def line(self, *waits):
        self.fst = after(self.fst, *waits)
        mine = [add(self.own[0, k], self.got[0, k], self.sec[0, k], self.fst[k]) for k in range(4)]
        self.mine = mine[0]
        self.sum_0 = [part.astype(bf16) for part in mine[1:]]
        self.far = [send(part, TO_Z[k + 1]) for k, part in enumerate(self.sum_0)]

    def end(self, *waits):
        return add(self.mine, *(after(part, *waits) for part in self.far))


def joined(blocks):
    return jnp.concatenate(blocks, axis=1)


def fast_grads(q_all, m_a, m_b):
    core = lax.axis_index("narrow") % 2
    m = jnp.concatenate([m_a, m_b[:8]], axis=0).reshape(3, 2, 4, 48, 128)
    grad_up = joined([m[t, 0, 2 * h : 2 * h + 2].reshape(96, 128) for h in range(2) for t in range(3)])
    grad_down = joined([m[t, 1].reshape(192, 128) for t in range(3)]).T
    cols = joined([q_all[3 * t + g] for g in range(3) for t in range(3)])
    outs = joined([m_b[8 + g] for g in range(3)])
    low = joined([cols[:, :576], outs[:, :192]])
    high = joined([cols[:, 576:], outs[:, 192:]])
    keep = jnp.where(core == 0, low, high)
    got = send(jnp.where(core == 0, high, low), TO_CORE)
    rows = jnp.concatenate([jnp.where(core == 0, keep, got), jnp.where(core == 0, got, keep)], axis=0)
    small = q_all[9].reshape(3, 16, 128)[:, 0].reshape(384)
    vecs = {name: small[off : off + wd] for name, off, wd, _ in SMALL}
    return rows[:, :576], rows[:, 576:], grad_up, grad_down, vecs


def local(
    tokens,
    qkv_weight,
    qv_bias,
    out_weight,
    out_bias,
    up_weight,
    up_bias,
    down_weight,
    down_bias,
    norm1_gain,
    norm1_bias,
    norm2_gain,
    norm2_bias,
    lengths,
    cotangent,
    fast,
):
    vectors = {
        "qv": qv_bias,
        "outb": out_bias,
        "downb": down_bias,
        "gain1": norm1_gain,
        "shift1": norm1_bias,
        "gain2": norm2_gain,
        "shift2": norm2_bias,
        "upb": up_bias,
    }
    meta = jnp.stack([lax.axis_index("wide"), lax.axis_index("narrow")]).astype(jnp.int32)
    if fast:
        zeros = lambda size: jnp.zeros((size,), f32)
        small = jnp.concatenate(
            [qv_bias, out_bias, down_bias, norm1_gain, zeros(8)]
            + [norm1_bias, norm2_gain, norm2_bias, zeros(56), up_bias, zeros(32)]
        )
        small = jnp.pad(small.astype(bf16).reshape(3, 1, 128), ((0, 0), (0, 15), (0, 0))).reshape(1, 48, 128)
        piece_q, piece_o = first_pieces(qkv_weight, out_weight, small)
        feed = feed_pieces(up_weight, down_weight)
        heads = Spread(piece_q)
        rest = Spread(jnp.concatenate(feed + [piece_o]), heads.parts[1])
        heads.along(rest.parts[1])
        heads.across(rest.parts[2])
        heads.swap()
        ready = heads.end()
        rest.along(heads.corner)
        first = after(tokens, rest.line)
        a1, a1t, vec, qkv_0, o_0, lse_0, wq_0 = front(True, 0, meta, lengths, first, None, ready)
        qkv_1, o_1, lse_1, wq_1 = front(True, 1, meta, lengths, a1, vec, ready)
        rest.across(o_1)
        rest.swap(o_1)
        qkv_2, o_2, lse_2, wq_2 = front(True, 2, meta, lengths, a1, vec, ready)
        weights = rest.end(o_2)
    else:
        wq, wo, up, down, vec = plain_weights(qkv_weight, out_weight, up_weight, down_weight, vectors)
        a1, a1t, vec, qkv_0, o_0, lse_0, wq_0 = front(False, 0, meta, lengths, tokens, vec, (wq[0],))
        qkv_1, o_1, lse_1, wq_1 = front(False, 1, meta, lengths, a1, vec, (wq[1],))
        qkv_2, o_2, lse_2, wq_2 = front(False, 2, meta, lengths, a1, vec, (wq[2],))
        weights = (wo, up, down)
    output, dh, do, own_a, other_a, own_b, other_b, mid = middle(
        fast, meta, lengths, tokens, (o_0, o_1, o_2), cotangent, vec, weights
    )
    args = lambda qkv, lse, wq: (qkv, do, lse, a1t, wq, vec)
    d_0, own, other, sums_0 = back(fast, 0, meta, lengths, *args(qkv_0, lse_0, wq_0), ())
    if fast:
        ff_a, ff_b = Fold(own_a, other_a), Fold(own_b, other_b)
        ff_a.second(d_0)
        do = after(do, ff_a.sum_2, ff_b.got)
    d_1, own, other, sums_1 = back(fast, 1, meta, lengths, *args(qkv_1, lse_1, wq_1), (own, other))
    if fast:
        ff_b.second(d_1)
        ff_a.first(d_1)
        do = after(do, ff_b.sum_2, ff_a.sum_1)
    d_2, own, other, _ = back(
        fast, 2, meta, lengths, *args(qkv_2, lse_2, wq_2), (own, other, mid, sums_0, sums_1)
    )
    grads, weights = (d_0, d_1, d_2), (wq_0, wq_1, wq_2)
    if fast:
        at = Fold(own, other)
        ff_b.first(d_2)
        dh = after(dh, ff_b.sum_1)
    top = first_norm_back(0, tokens, grads, weights, dh, vec)
    if fast:
        ff_a.line(top)
        at.second(top)
        dh = after(dh, at.sum_2, *ff_a.sum_0)
    grad_tokens = first_norm_back(1, tokens, grads, weights, dh, vec, top)
    if fast:
        at.first(grad_tokens)
        total_a = ff_a.end(at.sum_1)
        ff_b.line(total_a)
        at.line(*ff_b.sum_0)
        g_qkv, g_out, g_up, g_down, vecs = fast_grads(at.end(), total_a, ff_b.end(*at.sum_0))
    else:
        g_qkv, g_out, g_up, g_down, vecs = plain_grads(own, own_a, own_b)
    return (
        output,
        grad_tokens,
        g_qkv,
        vecs["qv"],
        g_out,
        vecs["outb"],
        g_up,
        vecs["upb"],
        g_down,
        vecs["downb"],
        vecs["gain1"],
        vecs["shift1"],
        vecs["gain2"],
        vecs["shift2"],
    )


def solution(mesh):
    fast = mesh.shape["wide"] == 8 and mesh.shape["narrow"] == 4
    rows, matrix, vector = P(BOTH, None), P("wide", "narrow"), P(BOTH)
    return jax.shard_map(
        lambda *args: local(*args, fast),
        mesh=mesh,
        in_specs=(
            rows, matrix, vector, matrix, vector, matrix, vector, matrix, vector,
            vector, vector, vector, vector, rows, rows,
        ),
        out_specs=(
            rows, rows, matrix, vector, matrix, vector, matrix, vector, matrix, vector,
            vector, vector, vector, vector,
        ),
        check_vma=False,
    )
```

```python
import jax
import jax.numpy as jnp
import numpy as np
from jax import lax
from jax.experimental import pallas as pl
from jax.experimental.pallas import tpu as pltpu
from jax.sharding import PartitionSpec as P

HEADS = 12
BOTH = ("wide", "narrow")
bf16 = jnp.bfloat16
f32 = jnp.float32
epsilon = 1e-05
branch_scale = 24 ** (-0.5)
D = 768
FF = 3072
HD = 64
ROWS = 1024
QB = 256
NEG = -1e30
UNIT = (48, 128)
SMALL = (
    ("qv", 0, 48, 2),
    ("outb", 48, 24, 1),
    ("downb", 72, 24, 1),
    ("gain1", 96, 24, 1),
    ("shift1", 128, 24, 1),
    ("gain2", 152, 24, 1),
    ("shift2", 176, 24, 1),
    ("upb", 256, 96, 4),
)
ROW_OF = {}
_row = 0
for _name, _off, _wd, _n in SMALL:
    ROW_OF[_name] = _row
    _row += _n
VECS = 16


def nn(a, b):
    return lax.dot_general(a, b, (((1,), (0,)), ((), ())), preferred_element_type=f32)


def nt(a, b):
    return lax.dot_general(a, b, (((1,), (1,)), ((), ())), preferred_element_type=f32)


def normalize(values):
    average = jnp.mean(values, axis=-1, keepdims=True)
    centred = values - average
    spread = jnp.mean(centred * centred, axis=-1, keepdims=True)
    rinv = lax.rsqrt(spread + epsilon)
    return centred * rinv, rinv


def params(flops, bytes_accessed, mib=60):
    return dict(
        compiler_params=pltpu.CompilerParams(vmem_limit_bytes=mib * 1024 * 1024),
        cost_estimate=pl.CostEstimate(
            flops=int(flops), transcendentals=0, bytes_accessed=int(bytes_accessed)
        ),
    )


VM = pl.BlockSpec(memory_space=pltpu.VMEM)
SM = pl.BlockSpec(memory_space=pltpu.SMEM)
HB = pl.BlockSpec(memory_space=pl.ANY)


def sds(shape, dtype):
    return jax.ShapeDtypeStruct(shape, dtype)


def over_rows(body, blocks=ROWS // QB):
    def step(r, carry):
        body(pl.ds(pl.multiple_of(r * QB, QB), QB), r)
        return carry

    lax.fori_loop(0, blocks, step, 0)


def wait(ref, sem):
    pltpu.make_async_copy(ref, ref, sem).wait()


def lanes(ref, count):
    return jnp.concatenate([ref[g].reshape(D, 128) for g in range(count)], axis=1)


def held_by(meta, q, k, own):
    w, n = meta[0], meta[1]
    z, x, y, c = w // 2, w % 2, n // 2, n % 2
    core = c if own else 1 - c
    first, second = q % 2, q // 2
    dx = jnp.where(core == 0, first, second)
    dy = jnp.where(core == 0, second, first)
    zz = z ^ k
    return zz * 2 + (x ^ dx), core, y ^ dy


def piece_loop(meta, quads, issue):
    for own in (True, False):
        for q in range(4):
            ref = quads[q if own else 4 + q]
            for k in range(4):
                i, core, y = held_by(meta, q, k, own)
                issue(ref.at[k], i, core, y)


def place_loop(pieces, meta, own, other, issue):
    if pieces:
        for mine, ref in ((True, own), (False, other)):
            for q in range(4):
                for k in range(4):
                    i, core, y = held_by(meta, q, k, mine)
                    issue(ref.at[q, k], i, core, y)
    else:
        for i in range(8):
            for n in range(4):
                issue(own.at[i, n], i, n % 2, n // 2)


def places(pieces, units):
    if pieces:
        return (sds((4, 4, units) + UNIT, bf16), sds((4, 4, units) + UNIT, bf16))
    return (sds((8, 4, units) + UNIT, bf16), sds((8, 128), bf16))


def small_map(off, wd, row):
    lane = lax.broadcasted_iota(jnp.int32, (128, D), 1) + row * D
    within = lane - wd * jnp.floor((lane.astype(f32) + 0.5) * (1.0 / wd)).astype(jnp.int32)
    src = lax.broadcasted_iota(jnp.int32, (128, D), 0)
    return jnp.where(src == within + off % 128, 1.0, 0.0).astype(bf16)


def unpack_small(packed):
    rows = []
    for _, off, wd, count in SMALL:
        base = off // 128 * 16
        group = packed[:, base : base + 16, :].astype(f32)[:, 0, :].astype(bf16)
        for row in range(count):
            spread = nn(group, small_map(off, wd, row))
            lane = lax.broadcasted_iota(jnp.int32, (32, D), 1) + row * D
            low = lax.broadcasted_iota(jnp.int32, (32, D), 0) * wd
            keep = (lane >= low) & (lane < low + wd)
            rows.append(jnp.sum(jnp.where(keep, spread, 0.0), axis=0, keepdims=True))
    rows.append(jnp.zeros((VECS - len(rows), D), f32))
    return jnp.concatenate(rows, axis=0)


def pack_small(vec_row):
    groups = [jnp.zeros((32, 128), f32) for _ in range(3)]
    for name, off, wd, count in SMALL:
        for row in range(count):
            lane = lax.broadcasted_iota(jnp.int32, (32, D), 1) + row * D
            low = lax.broadcasted_iota(jnp.int32, (32, D), 0) * wd
            keep = (lane >= low) & (lane < low + wd)
            spread = jnp.where(keep, vec_row(ROW_OF[name] + row), 0.0).astype(bf16)
            groups[off // 128] += nt(spread, small_map(off, wd, row))
    return groups


def attend_rows(far, get, put):
    lane = lax.broadcasted_iota(jnp.int32, (QB, 128), 1)
    causal = lax.broadcasted_iota(jnp.int32, (QB, QB), 1) <= lax.broadcasted_iota(
        jnp.int32, (QB, QB), 0
    )
    for j in range(ROWS // QB):
        size = QB * (j + 1)
        q = get(0, QB * j, QB)
        outs, logs = [], []
        for h in range(2):
            mine = (lane < HD) if h == 0 else (lane >= HD)
            s = nt(jnp.where(mine, q, jnp.zeros_like(q)), get(1, 0, size))
            parts = []
            if j >= 2:
                parts.append(s[:, :512] + far)
                if j == 3:
                    parts.append(s[:, 512:768])
            elif j == 1:
                parts.append(s[:, :QB])
            parts.append(jnp.where(causal, s[:, size - QB :], NEG))
            s = jnp.concatenate(parts, axis=1)
            top = jnp.max(s, axis=1, keepdims=True)
            e = jnp.exp(s - top)
            total = jnp.sum(e, axis=1, keepdims=True)
            outs.append(nn(e.astype(bf16), get(2, 0, size)) * (1.0 / total))
            logs.append(top + jnp.log(total))
        put(QB * j, jnp.where(lane < HD, outs[0], outs[1]).astype(bf16), jnp.where(lane == 0, logs[0], logs[1]).T[:8])


def front_body(pieces, third, meta, lens, *refs):
    count = 8 if pieces else 1
    if third == 0:
        tok, quads, refs = refs[0], refs[1 : 1 + count], refs[1 + count :]
        if not pieces:
            vec_i, refs = refs[0], refs[1:]
        a1, a1t_o, vec, *refs = refs
    else:
        a1, vec, quads, refs = refs[0], refs[1], refs[2 : 2 + count], refs[2 + count :]
    qkv_o, o_o, lse_o, wq, packed, sem, sem2 = refs
    if pieces:

        def issue(ref, i, core, y):
            pltpu.make_async_copy(
                ref.at[pl.ds(3 * third, 3)], wq.at[pl.ds(3 * y, 3), 2 * i + core], sem
            ).start()
            if third == 0:
                pltpu.make_async_copy(ref.at[9], packed.at[i * 4 + 2 * y + core], sem2).start()

        piece_loop(meta, quads, issue)
    else:
        pltpu.make_async_copy(quads[0], wq, sem).start()
    if third == 0:
        if pieces:
            wait(packed, sem2)
            vec[...] = unpack_small(packed[...])
        else:
            vec[...] = vec_i[...]
        def first_norm(at, r):
            n1, _ = normalize(tok[at, :].astype(f32))
            a1[at, :] = (
                n1 * vec[ROW_OF["gain1"] : ROW_OF["gain1"] + 1, :]
                + vec[ROW_OF["shift1"] : ROW_OF["shift1"] + 1, :]
            ).astype(bf16)

        over_rows(first_norm)
        a1t_o[...] = a1[...].T
    wait(wq, sem)
    bias = []
    for g, row in ((0, 0), (1, 0), (4, 1), (5, 1)):
        lane = 128 * (third + 3 * (g % 2))
        bias.append(vec[ROW_OF["qv"] + row : ROW_OF["qv"] + row + 1, lane : lane + 128])
    zero = jnp.zeros((1, 128), f32)
    bias = jnp.concatenate([bias[0], bias[1], zero, zero, bias[2], bias[3]], axis=1)
    weights = lanes(wq, 6)

    def projection(at, r):
        block = (nn(a1[at, :], weights) + bias).astype(bf16)
        for g in range(6):
            part = block[:, 128 * g : 128 * g + 128]
            qkv_o[g, at, :] = part * jnp.asarray(1.0 / HD, bf16) if g < 2 else part

    over_rows(projection)
    far = jnp.where(lens[0, 0] < ROWS, NEG, 0.0).astype(f32)

    def one(pair, carry):
        def put(row, o, lse):
            o_o[pair, row : row + QB, :] = o
            lse_o[pair, :, row : row + QB] = lse

        attend_rows(far, lambda which, row, n: qkv_o[2 * which + pair, row : row + n, :], put)
        return carry

    lax.fori_loop(0, 2, one, 0)


def front(pieces, third, meta, lens, first, vec, weights):
    shapes = [
        sds((6, ROWS, 128), bf16),
        sds((2, ROWS, 128), bf16),
        sds((2, 8, ROWS), f32),
        sds((6, 16) + UNIT, bf16),
    ]
    if third == 0:
        shapes = [sds((ROWS, D), bf16), sds((D, ROWS), bf16), sds((VECS, D), f32)] + shapes
        args = (first,) + tuple(weights) + (() if pieces else (vec,))
        specs = [VM] + [HB] * len(weights) + ([] if pieces else [VM])
    else:
        args = (first, vec) + tuple(weights)
        specs = [VM, VM] + [HB] * len(weights)
    return pl.pallas_call(
        lambda *refs: front_body(pieces, third, *refs),
        out_shape=tuple(shapes),
        in_specs=[SM, SM] + specs,
        out_specs=(VM,) * len(shapes),
        scratch_shapes=[
            pltpu.VMEM((32,) + UNIT, bf16),
            pltpu.SemaphoreType.DMA(()),
            pltpu.SemaphoreType.DMA(()),
        ],
        name=f"front_{third}",
        **params(6e9, 8e6, 20),
    )(meta, lens, *args)


ROW_DN, ROW_G2, ROW_B2, ROW_OB, ROW_UP = 0, 1, 2, 3, 4


def middle_body(pieces, meta, lens, tok, o_0, o_1, o_2, cot, vec, *refs):
    count = 8 if pieces else 2
    quads, refs = refs[:count], refs[count:]
    out_o, dh_o, do_o, own_a, other_a, own_b, other_b, sums_o = refs[:8]
    (
        wo, feed, h_s, a2_s, a2t_s, dm_s, dmt_s, m_s, da2_s, gl_s, dz_s, st, st_o, upb_s,
        sem_w, sem_m, sem_o, sem_p,
    ) = refs[8:]
    if pieces:

        def issue_out_weight(ref, i, core, y):
            pltpu.make_async_copy(
                ref.at[pl.ds(24, 3)], wo.at[pl.ds(3 * y, 3), 2 * i + core], sem_w
            ).start()

        def issue_feed(ref, i, core, y):
            pltpu.make_async_copy(ref.at[pl.ds(0, 24)], feed.at[2 * y + core, i], sem_m).start()

        piece_loop(meta, quads, issue_out_weight)
        piece_loop(meta, quads, issue_feed)
    else:
        pltpu.make_async_copy(quads[0], wo, sem_w).start()
        pltpu.make_async_copy(quads[1], feed, sem_m).start()
    total = lens[0, 0] + lens[0, 1]
    row_of = lambda name: vec[ROW_OF[name] : ROW_OF[name] + 1, :]
    gain2, shift2, outb, downb = (row_of(n) for n in ("gain2", "shift2", "outb", "downb"))
    for t in range(3):
        upb_s[t : t + 1, :] = jnp.concatenate(
            [
                vec[
                    ROW_OF["upb"] + i // 2 : ROW_OF["upb"] + i // 2 + 1,
                    384 * (i % 2) + 128 * t : 384 * (i % 2) + 128 * t + 128,
                ]
                for i in range(8)
            ],
            axis=1,
        )
    sums_o[...] = jnp.zeros_like(sums_o)

    def attended(at):
        return jnp.concatenate([ref[p, at, :] for p in range(2) for ref in (o_0, o_1, o_2)], axis=1)

    wait(wo, sem_w)
    w_out = lanes(wo, 6)

    def prologue(at, r):
        h = tok[at, :].astype(f32) + branch_scale * (nn(attended(at), w_out) + outb)
        h_s[at, :] = h
        n2, _ = normalize(h)
        a2_s[at, :] = (n2 * gain2 + shift2).astype(bf16)
        live = (lax.broadcasted_iota(jnp.int32, (QB, D), 0) + QB * r) < total
        dm = (branch_scale * jnp.where(live, cot[at, :].astype(f32), 0.0)).astype(bf16)
        dm_s[at, :] = dm
        sums_o[ROW_DN : ROW_DN + 1, :D] += jnp.sum(dm.astype(f32), axis=0, keepdims=True)

    over_rows(prologue)
    a2t_s[...] = a2_s[...].T
    dmt_s[...] = dm_s[...].T
    m_s[...] = jnp.zeros_like(m_s)
    da2_s[...] = jnp.zeros_like(da2_s)
    wait(feed, sem_m)
    c0 = 0.7978845608028654
    c1 = 0.044715 * c0

    def emit(own, other, base):
        def issue(ref, i, core, y):
            pltpu.make_async_copy(st.at[2 * y + core, i], ref.at[pl.ds(base, 8)], sem_o).start()

        place_loop(pieces, meta, own, other, issue)

    def step(t, carry):
        up = jnp.concatenate(
            [feed[n, :, pl.ds(8 * t + 2 * h, 2)].reshape(D, 128) for n in range(4) for h in range(2)],
            axis=1,
        )
        dn = jnp.concatenate(
            [feed[:, i, pl.ds(8 * t + 4, 4)].reshape(D, 128) for i in range(8)], axis=1
        )
        bup = upb_s[pl.ds(t, 1), :]
        sums_o[pl.ds(ROW_UP + t, 1), :] = jnp.zeros((1, 1024), f32)

        def some(r, carry):
            at = pl.ds(pl.multiple_of(r * 256, 256), 256)
            z = nn(a2_s[at, :], up) + bup
            dgl = nn(dm_s[at, :], dn)
            zz = z * z
            th = jnp.tanh(z * (c0 + c1 * zz))
            half = 0.5 * th + 0.5
            gl = (z * half).astype(bf16)
            slope = half + (0.5 * z) * (1.0 - th * th) * (c0 + (3.0 * c1) * zz)
            dz = (dgl * slope).astype(bf16)
            gl_s[at, :] = gl
            dz_s[at, :] = dz
            sums_o[pl.ds(ROW_UP + t, 1), :] += jnp.sum(dz.astype(f32), axis=0, keepdims=True)
            m_s[at, :] += nt(gl, dn)
            da2_s[at, :] += nt(dz, up)
            return carry

        lax.fori_loop(0, 4, some, 0)

        @pl.when(t >= 1)
        def _():
            wait(st, sem_o)


        for n in range(4):
            at = pl.ds(256 * n, 256)
            grad = nn(a2t_s[...], dz_s[:, at]).astype(bf16)
            for h in range(2):
                st[n, :, 2 * h : 2 * h + 2] = grad[:, 128 * h : 128 * h + 128].reshape((8, 2) + UNIT)
            grad = nn(dmt_s[...], gl_s[:, at]).astype(bf16)
            for h in range(2):
                st[:, 2 * n + h, 4:8] = grad[:, 128 * h : 128 * h + 128].reshape((4, 4) + UNIT)

        @pl.when(t == 0)
        def _():
            emit(own_a, other_a, 0)

        @pl.when(t == 1)
        def _():
            emit(own_a, other_a, 8)

        @pl.when(t == 2)
        def _():
            emit(own_b, other_b, 0)

        return carry

    lax.fori_loop(0, 3, step, 0)

    def epilogue(at, r):
        h = h_s[at, :]
        out_o[at, :] = (h + branch_scale * (m_s[at, :] + downb)).astype(bf16)
        n2, r2 = normalize(h)
        da2 = da2_s[at, :]
        sums_o[ROW_G2 : ROW_G2 + 1, :D] += jnp.sum(da2 * n2, axis=0, keepdims=True)
        sums_o[ROW_B2 : ROW_B2 + 1, :D] += jnp.sum(da2, axis=0, keepdims=True)
        e = da2 * gain2
        live = (lax.broadcasted_iota(jnp.int32, (QB, D), 0) + QB * r) < total
        dy = jnp.where(live, cot[at, :].astype(f32), 0.0)
        dh = dy + r2 * (
            e
            - jnp.mean(e, axis=-1, keepdims=True)
            - n2 * jnp.mean(e * n2, axis=-1, keepdims=True)
        )
        dh_o[at, :] = dh
        du = (branch_scale * dh).astype(bf16)
        sums_o[ROW_OB : ROW_OB + 1, :D] += jnp.sum(du.astype(f32), axis=0, keepdims=True)
        dm_s[at, :] = du
        do = nt(du, w_out).astype(bf16)
        for g in range(6):
            do_o[g, at, :] = do[:, 128 * g : 128 * g + 128]

    over_rows(epilogue)
    a2t_s[...] = attended(pl.ds(0, ROWS)).T
    grad = nn(a2t_s[...], dm_s[...])
    for g in range(6):
        st_o[g] = grad[:, 128 * g : 128 * g + 128].astype(bf16).reshape((16,) + UNIT)

    def issue_out(ref, i, core, y):
        pltpu.make_async_copy(
            st_o.at[pl.ds(3 * y, 3), 2 * i + core], ref.at[pl.ds(8, 3)], sem_p
        ).start()

    place_loop(pieces, meta, own_b, other_b, issue_out)
    wait(st, sem_o)
    wait(st_o, sem_p)


def middle(pieces, meta, lens, tokens, attended, cotangent, vec, weights):
    block = (16,) + UNIT
    return pl.pallas_call(
        lambda *refs: middle_body(pieces, *refs),
        out_shape=(
            sds((ROWS, D), bf16),
            sds((ROWS, D), f32),
            sds((6, ROWS, 128), bf16),
            *places(pieces, 16),
            *places(pieces, 11),
            sds((8, 1024), f32),
        ),
        in_specs=[SM, SM, VM, VM, VM, VM, VM, VM] + [HB] * len(weights),
        out_specs=(VM, VM, VM, HB, HB, HB, HB, VM),
        scratch_shapes=[
            pltpu.VMEM((6,) + block, bf16),
            pltpu.VMEM((4, 8, 24) + UNIT, bf16),
            pltpu.VMEM((ROWS, D), f32),
            pltpu.VMEM((ROWS, D), bf16),
            pltpu.VMEM((D, ROWS), bf16),
            pltpu.VMEM((ROWS, D), bf16),
            pltpu.VMEM((D, ROWS), bf16),
            pltpu.VMEM((ROWS, D), f32),
            pltpu.VMEM((ROWS, D), f32),
            pltpu.VMEM((ROWS, 1024), bf16),
            pltpu.VMEM((ROWS, 1024), bf16),
            pltpu.VMEM((4, 8, 8) + UNIT, bf16),
            pltpu.VMEM((6,) + block, bf16),
            pltpu.VMEM((8, 1024), f32),
            pltpu.SemaphoreType.DMA(()),
            pltpu.SemaphoreType.DMA(()),
            pltpu.SemaphoreType.DMA(()),
            pltpu.SemaphoreType.DMA(()),
        ],
        name="middle",
        **params(60e9, 40e6, 50),
    )(meta, lens, tokens, *attended, cotangent, vec, *weights)


def back_pair(far, q_ref, k_ref, v_ref, do_ref, lse_ref, out, pair, dk_s, dv_s):
    lane = lax.broadcasted_iota(jnp.int32, (QB, 128), 1)
    causal = lax.broadcasted_iota(jnp.int32, (QB, QB), 0) <= lax.broadcasted_iota(
        jnp.int32, (QB, QB), 1
    )
    kt = k_ref[...].T
    sub = lax.broadcasted_iota(jnp.int32, (128, ROWS), 0)
    dk_s[...] = jnp.zeros_like(dk_s)
    dv_s[...] = jnp.zeros_like(dv_s)
    for j in range(ROWS // QB):
        size = QB * (j + 1)
        q = q_ref[QB * j : size, :]
        do = do_ref[QB * j : size, :]
        dq = jnp.zeros((128, QB), f32)
        dk = jnp.zeros((size, 128), f32)
        dv = jnp.zeros((size, 128), f32)
        for h in range(2):
            mine = (lane < HD) if h == 0 else (lane >= HD)
            qh = jnp.where(mine, q, jnp.zeros_like(q))
            doh = jnp.where(mine, do, jnp.zeros_like(do))
            s = nt(k_ref[:size, :], qh)
            parts = []
            if j >= 2:
                parts.append(s[:512] + far)
                if j == 3:
                    parts.append(s[512:768])
            elif j == 1:
                parts.append(s[:QB])
            parts.append(jnp.where(causal, s[size - QB :], NEG))
            s = jnp.concatenate(parts, axis=0)
            p = jnp.exp(s - lse_ref[h : h + 1, QB * j : size])
            dp = nt(v_ref[:size, :], doh)
            dot = jnp.sum(p * dp, axis=0, keepdims=True)
            ds = (p * (dp - dot)).astype(bf16)
            dv += nn(p.astype(bf16), doh)
            dk += nn(ds, qh)
            keep = (sub < HD) if h == 0 else (sub >= HD)
            dq += nn(jnp.where(keep, kt, jnp.zeros_like(kt))[:, :size], ds)
        out[pair, QB * j : size, :] = (dq.T * (1.0 / HD)).astype(bf16)
        dk_s[:size, :] += dk
        dv_s[:size, :] += dv
    out[2 + pair] = dk_s[...].astype(bf16)
    out[4 + pair] = dv_s[...].astype(bf16)


def back_body(pieces, third, meta, lens, qkv, do, lse, a1t, wq, vec, *refs):
    if third > 0:
        refs = refs[2:]
    if third == 2:
        mid, sums_0, sums_1, *refs = refs
    dqkv_o, own, other, sums_o, dk_s, dv_s, st, st_v, sem, sem2 = refs
    far = jnp.where(lens[0, 0] < ROWS, NEG, 0.0).astype(f32)

    def one(pair, carry):
        back_pair(
            far, qkv.at[pair], qkv.at[2 + pair], qkv.at[4 + pair], do.at[third + 3 * pair], lse.at[pair],
            dqkv_o, pair, dk_s, dv_s,
        )
        return carry

    lax.fori_loop(0, 2, one, 0)
    raw = jnp.zeros((D, 128), f32)
    plain = jnp.zeros((D, 128), f32)
    cols = []
    for two in range(3):
        blocks = nn(a1t[...], jnp.concatenate([dqkv_o[2 * two], dqkv_o[2 * two + 1]], axis=1))
        for g in (2 * two, 2 * two + 1):
            block = blocks[:, 128 * (g % 2) : 128 * (g % 2) + 128]
            col = jnp.sum(dqkv_o[g].astype(f32), axis=0, keepdims=True)
            cols.append(col)
            st[g] = block.astype(bf16).reshape((16,) + UNIT)
            weight = wq[g].reshape(D, 128).astype(f32)
            raw += block * weight
            plain += weight * col
    base = 3 * third

    def issue(ref, i, core, y):
        pltpu.make_async_copy(
            st.at[pl.ds(3 * y, 3), 2 * i + core], ref.at[pl.ds(base, 3)], sem
        ).start()

    place_loop(pieces, meta, own, other, issue)
    raw = jnp.sum(raw, axis=1, keepdims=True)
    plain = jnp.sum(plain, axis=1, keepdims=True)
    lane = lax.broadcasted_iota(jnp.int32, (D, 128), 1)
    flat = jnp.where(lane == 0, raw, plain).T[:8]
    sums = jnp.concatenate([jnp.concatenate(cols, axis=1), flat[:2], jnp.zeros((5, D), f32)], axis=0)
    sums_o[...] = sums
    if third == 2:
        per = [sums_0[...], sums_1[...], sums]
        raw = per[0][1:2] + per[1][1:2] + per[2][1:2]
        shift = per[0][2:3] + per[1][2:3] + per[2][2:3]
        row_of = lambda name: vec[ROW_OF[name] : ROW_OF[name] + 1, :]
        gain = (raw - row_of("shift1") * shift) / row_of("gain1")
        pick = lambda g: jnp.concatenate(
            [per[p % 3][0:1, 128 * (g + p // 3) : 128 * (g + p // 3) + 128] for p in range(6)], axis=1
        )
        known = {
            "outb": mid[ROW_OB : ROW_OB + 1, :D],
            "downb": mid[ROW_DN : ROW_DN + 1, :D],
            "gain1": gain,
            "shift1": shift,
            "gain2": mid[ROW_G2 : ROW_G2 + 1, :D],
            "shift2": mid[ROW_B2 : ROW_B2 + 1, :D],
        }
        rows = {ROW_OF["qv"]: pick(0), ROW_OF["qv"] + 1: pick(4)}
        for name, value in known.items():
            rows[ROW_OF[name]] = value
        for r in range(4):
            rows[ROW_OF["upb"] + r] = jnp.concatenate(
                [
                    mid[ROW_UP + t : ROW_UP + t + 1, 128 * i : 128 * i + 128]
                    for i in (2 * r, 2 * r + 1)
                    for t in range(3)
                ],
                axis=1,
            )
        groups = pack_small(lambda r: rows[r])
        for g in range(3):
            st_v[:, 16 * g : 16 * g + 16, :] = jnp.broadcast_to(
                groups[g][:, None, :], (32, 16, 128)
            ).astype(bf16)

        def issue_small(ref, i, core, y):
            pltpu.make_async_copy(st_v.at[i * 4 + 2 * y + core], ref.at[9], sem2).start()

        place_loop(pieces, meta, own, other, issue_small)
        wait(st_v, sem2)
    wait(st, sem)


def back(pieces, third, meta, lens, qkv, do, lse, a1t, wq, vec, before):
    args = [meta, lens, qkv, do, lse, a1t, wq, vec, *before]
    extra = [HB, HB] * (third > 0) + [VM, VM, VM] * (third == 2)
    return pl.pallas_call(
        lambda *refs: back_body(pieces, third, *refs),
        out_shape=(
            sds((6, ROWS, 128), bf16),
            *places(pieces, 10),
            sds((8, D), f32),
        ),
        in_specs=[SM, SM] + [VM] * 6 + extra,
        out_specs=(VM, HB, HB, VM),
        input_output_aliases={8: 1, 9: 2} if third > 0 else {},
        scratch_shapes=[
            pltpu.VMEM((ROWS, 128), f32),
            pltpu.VMEM((ROWS, 128), f32),
            pltpu.VMEM((6, 16) + UNIT, bf16),
            pltpu.VMEM((32,) + UNIT, bf16),
            pltpu.SemaphoreType.DMA(()),
            pltpu.SemaphoreType.DMA(()),
        ],
        name=f"back_{third}",
        **params(18e9, 8e6, 20),
    )(*args)


def first_norm_back_body(tok, d_0, d_1, d_2, w_0, w_1, w_2, dh, vec, *refs):
    gt_o = refs[-1]
    gain1 = vec[ROW_OF["gain1"] : ROW_OF["gain1"] + 1, :]

    def body(at, r):
        da1 = jnp.zeros((QB, D), f32)
        for grad, weight in ((d_0, w_0), (d_1, w_1), (d_2, w_2)):
            rows = jnp.concatenate([grad[g, at, :] for g in range(6)], axis=1)
            da1 += nt(rows, lanes(weight, 6))
        n1, r1 = normalize(tok[at, :].astype(f32))
        e = da1 * gain1
        back = r1 * (
            e
            - jnp.mean(e, axis=-1, keepdims=True)
            - n1 * jnp.mean(e * n1, axis=-1, keepdims=True)
        )
        gt_o[at, :] = (dh[at, :] + back).astype(bf16)

    over_rows(body, 2)


def first_norm_back(half, tokens, grads, weights, dh, vec, before=None):
    count = ROWS // 2
    rows = pl.BlockSpec((count, D), lambda g: (half, 0))
    every = lambda shape: pl.BlockSpec(shape, lambda g: (0,) * len(shape))
    return pl.pallas_call(
        first_norm_back_body,
        grid=(1,),
        out_shape=sds((ROWS, D), bf16),
        in_specs=[rows]
        + [pl.BlockSpec((6, count, 128), lambda g: (0, half, 0))] * 3
        + [every((6, 16) + UNIT)] * 3
        + [rows, every((VECS, D))]
        + ([] if before is None else [HB]),
        out_specs=rows,
        input_output_aliases={} if before is None else {9: 0},
        name=f"first_norm_back_{half}",
        **params(8e9, 9e6, 14),
    )(tokens, *grads, *weights, dh, vec, *(() if before is None else (before,)))


def links(step):
    pairs = []
    for z in range(4):
        for x in range(2):
            for y in range(2):
                for c in range(2):
                    tz, tx, ty, tc = step(z, x, y, c)
                    pairs.append(((z * 2 + x) * 4 + y * 2 + c, (tz * 2 + tx) * 4 + ty * 2 + tc))
    return pairs


TO_CORE = links(lambda z, x, y, c: (z, x, y, 1 - c))
TO_FIRST = links(lambda z, x, y, c: (z, 1 - x, y, c) if c == 0 else (z, x, 1 - y, c))
TO_SECOND = links(lambda z, x, y, c: (z, x, 1 - y, c) if c == 0 else (z, 1 - x, y, c))
TO_Z = [None] + [links(lambda z, x, y, c, k=k: (z ^ k, x, y, c)) for k in (1, 2, 3)]


def send(value, pairs):
    return lax.ppermute(value, BOTH, pairs)


def after(value, *others):
    return lax.optimization_barrier((value, *others))[0]


def add(*parts):
    total = parts[0].astype(f32)
    for part in parts[1:]:
        total = total + part.astype(f32)
    return total


def split(big, sizes):
    out, at = [], 0
    for size in sizes:
        out.append(big[at : at + size])
        at += size
    return out


def as_units(block):
    a, b = block.shape[0] // 48, block.shape[1] // 128
    return block.reshape(a, 48, b, 128).transpose(2, 0, 1, 3).reshape(a * b, 48, 128)


def first_pieces(qkv_weight, out_weight, small):
    core = lax.axis_index("narrow") % 2
    both = jnp.concatenate([qkv_weight, out_weight], axis=1).astype(bf16)
    keep = jnp.where(core == 0, both[:48], both[48:])
    give = jnp.where(core == 0, both[48:], both[:48])
    got = send(give, TO_CORE)
    left = jnp.where(core == 0, keep, got)
    right = jnp.where(core == 0, got, keep)
    cols = as_units(jnp.concatenate([left[:, :576], right[:, :576]], axis=1))
    out = as_units(jnp.concatenate([left[:, 576:], right[:, 576:]], axis=1))
    thirds = [cols[g] for t in range(3) for g in (t, 3 + t, 6 + t)]
    return jnp.concatenate([jnp.stack(thirds), small], axis=0), out


def feed_pieces(up_weight, down_weight):
    up = as_units(up_weight.astype(bf16))
    down = as_units(down_weight.astype(bf16).T)
    out = []
    for t in range(3):
        out.append(jnp.concatenate([up[2 * t : 2 * t + 2], up[6 + 2 * t : 8 + 2 * t], down[4 * t : 4 * t + 4]]))
    return out


def whole(value, dims):
    for axis, dim in dims:
        value = lax.all_gather(value, axis, axis=dim, tiled=True)
    return value


def plain_weights(qkv_weight, out_weight, up_weight, down_weight, vectors):
    matrix = lambda w: whole(w.astype(bf16), (("narrow", 1), ("wide", 0)))
    blocks = lambda w, b: w.reshape(16, 48, b, 128).transpose(2, 0, 1, 3)
    wq = blocks(matrix(qkv_weight), 18)
    wq = [jnp.stack([wq[g] for g in (t, 3 + t, 6 + t, 9 + t, 12 + t, 15 + t)]) for t in range(3)]
    wo = blocks(matrix(out_weight), 6)
    up = blocks(matrix(up_weight), 24).reshape(4, 2, 3, 8, 2, 48, 128)
    up = up.transpose(0, 3, 2, 1, 4, 5, 6).reshape(4, 8, 3, 4, 48, 128)
    down = blocks(matrix(down_weight).T, 24).reshape(8, 3, 4, 4, 48, 128).transpose(2, 0, 1, 3, 4, 5)
    feed = jnp.concatenate([up, down], axis=3).reshape(4, 8, 24, 48, 128)
    rows = [
        whole(vectors[name].astype(bf16), (("narrow", 0), ("wide", 0))).astype(f32).reshape(count, D)
        for name, _, _, count in SMALL
    ]
    vec = jnp.concatenate(rows + [jnp.zeros((VECS - 12, D), f32)], axis=0)
    return wq, wo, feed, vec


def plain_grads(q_all, m_a, m_b):
    def reduce(matrix):
        rows = lax.psum_scatter(matrix.astype(f32), "wide", scatter_dimension=0, tiled=True)
        return lax.psum_scatter(rows.astype(bf16), "narrow", scatter_dimension=1, tiled=True).astype(f32)

    def vector(values):
        rows = lax.psum_scatter(values, "wide", scatter_dimension=0, tiled=True)
        return lax.psum_scatter(rows.astype(bf16), "narrow", scatter_dimension=0, tiled=True).astype(f32)

    q = q_all[:, :, :9].reshape(8, 2, 2, 3, 3, 48, 128)
    qkv = q.transpose(0, 2, 5, 1, 4, 3, 6).reshape(D, 2304)
    out = m_b[:, :, 8:].reshape(8, 2, 2, 3, 48, 128).transpose(0, 2, 4, 1, 3, 5).reshape(D, D)
    m = jnp.concatenate([m_a, m_b[:, :, :8]], axis=2).reshape(8, 4, 3, 2, 4, 48, 128)
    up = m[:, :, :, 0].reshape(8, 4, 3, 2, 2, 48, 128).transpose(0, 4, 5, 1, 3, 2, 6).reshape(D, FF)
    down = m[:, :, :, 1].transpose(0, 2, 5, 1, 3, 4).reshape(FF, D)
    small = q_all[:, :, 9].reshape(32, 3, 16, 128)[:, :, 0].reshape(32, 384).astype(f32)
    vecs = {name: vector(small[:, off : off + wd].reshape(-1)) for name, off, wd, _ in SMALL}
    return reduce(qkv), reduce(out), reduce(up), reduce(down), vecs


class Spread:
    def __init__(self, piece, *waits):
        near = send(after(piece, *waits), TO_Z[1])
        self.parts = [piece, near] + [send(piece, TO_Z[k]) for k in (2, 3)]

    def along(self, *waits):
        self.line = after(jnp.stack(self.parts, axis=0), *waits)
        self.first = send(self.line, TO_FIRST)
        self.second = send(self.line, TO_SECOND)

    def across(self, *waits):
        self.corner = send(after(self.first, *waits), TO_SECOND)

    def swap(self, *waits):
        self.swapped = [send(after(part, *waits), TO_CORE) for part in (self.line, self.first, self.second)]

    def end(self, *waits):
        last = send(after(self.corner, *waits), TO_CORE)
        return (self.line, self.first, self.second, self.corner, *self.swapped, last)


class Fold:
    def __init__(self, own, other):
        self.own = own
        self.got = send(other, TO_CORE)

    def second(self, *waits):
        self.got = after(self.got, *waits)
        self.sum_2 = add(self.own[2:], self.got[2:]).astype(bf16)
        self.sec = send(self.sum_2, TO_SECOND)

    def first(self, *waits):
        self.sec = after(self.sec, *waits)
        self.sum_1 = add(self.own[1], self.got[1], self.sec[1]).astype(bf16)
        self.fst = send(self.sum_1, TO_FIRST)

    def line(self, *waits):
        self.fst = after(self.fst, *waits)
        mine = [add(self.own[0, k], self.got[0, k], self.sec[0, k], self.fst[k]) for k in range(4)]
        self.mine = mine[0]
        self.sum_0 = [part.astype(bf16) for part in mine[1:]]
        self.far = [send(part, TO_Z[k + 1]) for k, part in enumerate(self.sum_0)]

    def end(self, *waits):
        return add(self.mine, *(after(part, *waits) for part in self.far))


def joined(blocks):
    return jnp.concatenate(blocks, axis=1)


def fast_grads(q_all, m_a, m_b):
    core = lax.axis_index("narrow") % 2
    m = jnp.concatenate([m_a, m_b[:8]], axis=0).reshape(3, 2, 4, 48, 128)
    grad_up = joined([m[t, 0, 2 * h : 2 * h + 2].reshape(96, 128) for h in range(2) for t in range(3)])
    grad_down = joined([m[t, 1].reshape(192, 128) for t in range(3)]).T
    cols = joined([q_all[3 * t + g] for g in range(3) for t in range(3)])
    outs = joined([m_b[8 + g] for g in range(3)])
    low = joined([cols[:, :576], outs[:, :192]])
    high = joined([cols[:, 576:], outs[:, 192:]])
    keep = jnp.where(core == 0, low, high)
    got = send(jnp.where(core == 0, high, low), TO_CORE)
    rows = jnp.concatenate([jnp.where(core == 0, keep, got), jnp.where(core == 0, got, keep)], axis=0)
    small = q_all[9].reshape(3, 16, 128)[:, 0].reshape(384)
    vecs = {name: small[off : off + wd] for name, off, wd, _ in SMALL}
    return rows[:, :576], rows[:, 576:], grad_up, grad_down, vecs


def local(
    tokens,
    qkv_weight,
    qv_bias,
    out_weight,
    out_bias,
    up_weight,
    up_bias,
    down_weight,
    down_bias,
    norm1_gain,
    norm1_bias,
    norm2_gain,
    norm2_bias,
    lengths,
    cotangent,
    fast,
):
    vectors = {
        "qv": qv_bias,
        "outb": out_bias,
        "downb": down_bias,
        "gain1": norm1_gain,
        "shift1": norm1_bias,
        "gain2": norm2_gain,
        "shift2": norm2_bias,
        "upb": up_bias,
    }
    meta = jnp.stack([lax.axis_index("wide"), lax.axis_index("narrow")]).astype(jnp.int32)
    if fast:
        zeros = lambda size: jnp.zeros((size,), f32)
        small = jnp.concatenate(
            [qv_bias, out_bias, down_bias, norm1_gain, zeros(8)]
            + [norm1_bias, norm2_gain, norm2_bias, zeros(56), up_bias, zeros(32)]
        )
        small = jnp.pad(small.astype(bf16).reshape(3, 1, 128), ((0, 0), (0, 15), (0, 0))).reshape(1, 48, 128)
        piece_q, piece_o = first_pieces(qkv_weight, out_weight, small)
        feed = feed_pieces(up_weight, down_weight)
        heads = Spread(piece_q)
        rest = Spread(jnp.concatenate(feed + [piece_o]), heads.parts[1])
        heads.along(rest.parts[1])
        heads.across(rest.parts[2])
        heads.swap()
        ready = heads.end()
        rest.along(heads.corner)
        first = after(tokens, rest.line)
        a1, a1t, vec, qkv_0, o_0, lse_0, wq_0 = front(True, 0, meta, lengths, first, None, ready)
        qkv_1, o_1, lse_1, wq_1 = front(True, 1, meta, lengths, a1, vec, ready)
        rest.across(o_1)
        rest.swap(o_1)
        qkv_2, o_2, lse_2, wq_2 = front(True, 2, meta, lengths, a1, vec, ready)
        weights = rest.end(o_2)
    else:
        wq, wo, feed, vec = plain_weights(qkv_weight, out_weight, up_weight, down_weight, vectors)
        a1, a1t, vec, qkv_0, o_0, lse_0, wq_0 = front(False, 0, meta, lengths, tokens, vec, (wq[0],))
        qkv_1, o_1, lse_1, wq_1 = front(False, 1, meta, lengths, a1, vec, (wq[1],))
        qkv_2, o_2, lse_2, wq_2 = front(False, 2, meta, lengths, a1, vec, (wq[2],))
        weights = (wo, feed)
    output, dh, do, own_a, other_a, own_b, other_b, mid = middle(
        fast, meta, lengths, tokens, (o_0, o_1, o_2), cotangent, vec, weights
    )
    args = lambda qkv, lse, wq: (qkv, do, lse, a1t, wq, vec)
    d_0, own, other, sums_0 = back(fast, 0, meta, lengths, *args(qkv_0, lse_0, wq_0), ())
    if fast:
        ff_a, ff_b = Fold(own_a, other_a), Fold(own_b, other_b)
        ff_a.second(d_0)
        do = after(do, ff_a.sum_2, ff_b.got)
    d_1, own, other, sums_1 = back(fast, 1, meta, lengths, *args(qkv_1, lse_1, wq_1), (own, other))
    if fast:
        ff_b.second(d_1)
        ff_a.first(d_1)
        do = after(do, ff_b.sum_2, ff_a.sum_1)
    d_2, own, other, _ = back(
        fast, 2, meta, lengths, *args(qkv_2, lse_2, wq_2), (own, other, mid, sums_0, sums_1)
    )
    grads, weights = (d_0, d_1, d_2), (wq_0, wq_1, wq_2)
    if fast:
        at = Fold(own, other)
        ff_b.first(d_2)
        dh = after(dh, ff_b.sum_1)
    top = first_norm_back(0, tokens, grads, weights, dh, vec)
    if fast:
        ff_a.line(top)
        at.second(top)
        dh = after(dh, at.sum_2, *ff_a.sum_0)
    grad_tokens = first_norm_back(1, tokens, grads, weights, dh, vec, top)
    if fast:
        at.first(grad_tokens)
        total_a = ff_a.end(at.sum_1)
        ff_b.line(total_a)
        at.line(*ff_b.sum_0)
        g_qkv, g_out, g_up, g_down, vecs = fast_grads(at.end(), total_a, ff_b.end(*at.sum_0))
    else:
        g_qkv, g_out, g_up, g_down, vecs = plain_grads(own, own_a, own_b)
    return (
        output,
        grad_tokens,
        g_qkv,
        vecs["qv"],
        g_out,
        vecs["outb"],
        g_up,
        vecs["upb"],
        g_down,
        vecs["downb"],
        vecs["gain1"],
        vecs["shift1"],
        vecs["gain2"],
        vecs["shift2"],
    )


def solution(mesh):
    fast = mesh.shape["wide"] == 8 and mesh.shape["narrow"] == 4
    rows, matrix, vector = P(BOTH, None), P("wide", "narrow"), P(BOTH)
    return jax.shard_map(
        lambda *args: local(*args, fast),
        mesh=mesh,
        in_specs=(
            rows, matrix, vector, matrix, vector, matrix, vector, matrix, vector,
            vector, vector, vector, vector, rows, rows,
        ),
        out_specs=(
            rows, rows, matrix, vector, matrix, vector, matrix, vector, matrix, vector,
            vector, vector, vector, vector,
        ),
        check_vma=False,
    )
```

```python
import jax
import jax.numpy as jnp
import numpy as np
from jax import lax
from jax.experimental import pallas as pl
from jax.experimental.pallas import tpu as pltpu
from jax.sharding import PartitionSpec as P

HEADS = 12
BOTH = ("wide", "narrow")
bf16 = jnp.bfloat16
f32 = jnp.float32
epsilon = 1e-05
branch_scale = 24 ** (-0.5)
D = 768
FF = 3072
HD = 64
ROWS = 1024
QB = 256
NEG = -1e30
UNIT = (48, 128)
SMALL = (
    ("qv", 0, 48, 2),
    ("outb", 48, 24, 1),
    ("downb", 72, 24, 1),
    ("gain1", 96, 24, 1),
    ("shift1", 128, 24, 1),
    ("gain2", 152, 24, 1),
    ("shift2", 176, 24, 1),
    ("upb", 256, 96, 4),
)
ROW_OF = {}
_row = 0
for _name, _off, _wd, _n in SMALL:
    ROW_OF[_name] = _row
    _row += _n
VECS = 16


def nn(a, b):
    return lax.dot_general(a, b, (((1,), (0,)), ((), ())), preferred_element_type=f32)


def nt(a, b):
    return lax.dot_general(a, b, (((1,), (1,)), ((), ())), preferred_element_type=f32)


def normalize(values):
    average = jnp.mean(values, axis=-1, keepdims=True)
    centred = values - average
    spread = jnp.mean(centred * centred, axis=-1, keepdims=True)
    rinv = lax.rsqrt(spread + epsilon)
    return centred * rinv, rinv


def params(flops, bytes_accessed, mib=60):
    return dict(
        compiler_params=pltpu.CompilerParams(vmem_limit_bytes=mib * 1024 * 1024),
        cost_estimate=pl.CostEstimate(
            flops=int(flops), transcendentals=0, bytes_accessed=int(bytes_accessed)
        ),
    )


VM = pl.BlockSpec(memory_space=pltpu.VMEM)
SM = pl.BlockSpec(memory_space=pltpu.SMEM)
HB = pl.BlockSpec(memory_space=pl.ANY)


def sds(shape, dtype):
    return jax.ShapeDtypeStruct(shape, dtype)


def over_rows(body, blocks=ROWS // QB):
    def step(r, carry):
        body(pl.ds(pl.multiple_of(r * QB, QB), QB), r)
        return carry

    lax.fori_loop(0, blocks, step, 0)


def wait(ref, sem):
    pltpu.make_async_copy(ref, ref, sem).wait()


def lanes(ref, count):
    return jnp.concatenate([ref[g].reshape(D, 128) for g in range(count)], axis=1)


def held_by(meta, q, k, own):
    w, n = meta[0], meta[1]
    z, x, y, c = w // 2, w % 2, n // 2, n % 2
    core = c if own else 1 - c
    first, second = q % 2, q // 2
    dx = jnp.where(core == 0, first, second)
    dy = jnp.where(core == 0, second, first)
    zz = z ^ k
    return zz * 2 + (x ^ dx), core, y ^ dy


def piece_loop(meta, quads, issue):
    for own in (True, False):
        for q in range(4):
            ref = quads[q if own else 4 + q]
            for k in range(4):
                i, core, y = held_by(meta, q, k, own)
                issue(ref.at[k], i, core, y)


def place_loop(pieces, meta, own, other, issue):
    if pieces:
        for mine, ref in ((True, own), (False, other)):
            for q in range(4):
                for k in range(4):
                    i, core, y = held_by(meta, q, k, mine)
                    issue(ref.at[q, k], i, core, y)
    else:
        for i in range(8):
            for n in range(4):
                issue(own.at[i, n], i, n % 2, n // 2)


def places(pieces, units):
    if pieces:
        return (sds((4, 4, units) + UNIT, bf16), sds((4, 4, units) + UNIT, bf16))
    return (sds((8, 4, units) + UNIT, bf16), sds((8, 128), bf16))


def small_map(off, wd, row):
    lane = lax.broadcasted_iota(jnp.int32, (128, D), 1) + row * D
    within = lane - wd * jnp.floor((lane.astype(f32) + 0.5) * (1.0 / wd)).astype(jnp.int32)
    src = lax.broadcasted_iota(jnp.int32, (128, D), 0)
    return jnp.where(src == within + off % 128, 1.0, 0.0).astype(bf16)


def unpack_small(packed):
    rows = []
    for _, off, wd, count in SMALL:
        base = off // 128 * 16
        group = packed[:, base : base + 16, :].astype(f32)[:, 0, :].astype(bf16)
        for row in range(count):
            spread = nn(group, small_map(off, wd, row))
            lane = lax.broadcasted_iota(jnp.int32, (32, D), 1) + row * D
            low = lax.broadcasted_iota(jnp.int32, (32, D), 0) * wd
            keep = (lane >= low) & (lane < low + wd)
            rows.append(jnp.sum(jnp.where(keep, spread, 0.0), axis=0, keepdims=True))
    rows.append(jnp.zeros((VECS - len(rows), D), f32))
    return jnp.concatenate(rows, axis=0)


def pack_small(vec_row):
    groups = [jnp.zeros((32, 128), f32) for _ in range(3)]
    for name, off, wd, count in SMALL:
        for row in range(count):
            lane = lax.broadcasted_iota(jnp.int32, (32, D), 1) + row * D
            low = lax.broadcasted_iota(jnp.int32, (32, D), 0) * wd
            keep = (lane >= low) & (lane < low + wd)
            spread = jnp.where(keep, vec_row(ROW_OF[name] + row), 0.0).astype(bf16)
            groups[off // 128] += nt(spread, small_map(off, wd, row))
    return groups


def attend_rows(far, get, put):
    lane = lax.broadcasted_iota(jnp.int32, (QB, 128), 1)
    causal = lax.broadcasted_iota(jnp.int32, (QB, QB), 1) <= lax.broadcasted_iota(
        jnp.int32, (QB, QB), 0
    )
    for j in range(ROWS // QB):
        size = QB * (j + 1)
        q = get(0, QB * j, QB)
        outs, logs = [], []
        for h in range(2):
            mine = (lane < HD) if h == 0 else (lane >= HD)
            s = nt(jnp.where(mine, q, jnp.zeros_like(q)), get(1, 0, size))
            parts = []
            if j >= 2:
                parts.append(s[:, :512] + far)
                if j == 3:
                    parts.append(s[:, 512:768])
            elif j == 1:
                parts.append(s[:, :QB])
            parts.append(jnp.where(causal, s[:, size - QB :], NEG))
            s = jnp.concatenate(parts, axis=1)
            top = jnp.max(s, axis=1, keepdims=True)
            e = jnp.exp(s - top)
            total = jnp.sum(e, axis=1, keepdims=True)
            outs.append(nn(e.astype(bf16), get(2, 0, size)) * (1.0 / total))
            logs.append(top + jnp.log(total))
        put(QB * j, jnp.where(lane < HD, outs[0], outs[1]).astype(bf16), jnp.where(lane == 0, logs[0], logs[1]).T[:8])


def front_body(pieces, third, meta, lens, *refs):
    count = 8 if pieces else 1
    if third == 0:
        tok, quads, refs = refs[0], refs[1 : 1 + count], refs[1 + count :]
        if not pieces:
            vec_i, refs = refs[0], refs[1:]
        a1, a1t_o, vec, *refs = refs
    else:
        a1, vec, quads, refs = refs[0], refs[1], refs[2 : 2 + count], refs[2 + count :]
    qkv_o, o_o, lse_o, wq, packed, sem, sem2 = refs
    if pieces:

        def issue(ref, i, core, y):
            pltpu.make_async_copy(
                ref.at[pl.ds(3 * third, 3)], wq.at[pl.ds(3 * y, 3), 2 * i + core], sem
            ).start()
            if third == 0:
                pltpu.make_async_copy(ref.at[9], packed.at[i * 4 + 2 * y + core], sem2).start()

        piece_loop(meta, quads, issue)
    else:
        pltpu.make_async_copy(quads[0], wq, sem).start()
    if third == 0:
        if pieces:
            wait(packed, sem2)
            vec[...] = unpack_small(packed[...])
        else:
            vec[...] = vec_i[...]
        def first_norm(at, r):
            n1, _ = normalize(tok[at, :].astype(f32))
            a1[at, :] = (
                n1 * vec[ROW_OF["gain1"] : ROW_OF["gain1"] + 1, :]
                + vec[ROW_OF["shift1"] : ROW_OF["shift1"] + 1, :]
            ).astype(bf16)

        over_rows(first_norm)
        a1t_o[...] = a1[...].T
    wait(wq, sem)
    bias = []
    for g, row in ((0, 0), (1, 0), (4, 1), (5, 1)):
        lane = 128 * (third + 3 * (g % 2))
        bias.append(vec[ROW_OF["qv"] + row : ROW_OF["qv"] + row + 1, lane : lane + 128])
    zero = jnp.zeros((1, 128), f32)
    bias = jnp.concatenate([bias[0], bias[1], zero, zero, bias[2], bias[3]], axis=1)
    weights = lanes(wq, 6)

    def projection(at, r):
        block = (nn(a1[at, :], weights) + bias).astype(bf16)
        for g in range(6):
            part = block[:, 128 * g : 128 * g + 128]
            qkv_o[g, at, :] = part * jnp.asarray(1.0 / HD, bf16) if g < 2 else part

    over_rows(projection)
    far = jnp.where(lens[0, 0] < ROWS, NEG, 0.0).astype(f32)

    def one(pair, carry):
        def put(row, o, lse):
            o_o[pair, row : row + QB, :] = o
            lse_o[pair, :, row : row + QB] = lse

        attend_rows(far, lambda which, row, n: qkv_o[2 * which + pair, row : row + n, :], put)
        return carry

    lax.fori_loop(0, 2, one, 0)


def front(pieces, third, meta, lens, first, vec, weights):
    shapes = [
        sds((6, ROWS, 128), bf16),
        sds((2, ROWS, 128), bf16),
        sds((2, 8, ROWS), f32),
        sds((6, 16) + UNIT, bf16),
    ]
    if third == 0:
        shapes = [sds((ROWS, D), bf16), sds((D, ROWS), bf16), sds((VECS, D), f32)] + shapes
        args = (first,) + tuple(weights) + (() if pieces else (vec,))
        specs = [VM] + [HB] * len(weights) + ([] if pieces else [VM])
    else:
        args = (first, vec) + tuple(weights)
        specs = [VM, VM] + [HB] * len(weights)
    return pl.pallas_call(
        lambda *refs: front_body(pieces, third, *refs),
        out_shape=tuple(shapes),
        in_specs=[SM, SM] + specs,
        out_specs=(VM,) * len(shapes),
        scratch_shapes=[
            pltpu.VMEM((32,) + UNIT, bf16),
            pltpu.SemaphoreType.DMA(()),
            pltpu.SemaphoreType.DMA(()),
        ],
        name=f"front_{third}",
        **params(6e9, 8e6, 20),
    )(meta, lens, *args)


ROW_DN, ROW_G2, ROW_B2, ROW_OB, ROW_UP = 0, 1, 2, 3, 4


def middle_body(pieces, meta, lens, tok, o_0, o_1, o_2, cot, vec, *refs):
    count = 8 if pieces else 2
    quads, refs = refs[:count], refs[count:]
    out_o, dh_o, do_o, own_a, other_a, own_b, other_b, sums_o = refs[:8]
    (
        wo, feed, h_s, a2_s, a2t_s, dm_s, dmt_s, m_s, da2_s, gl_s, dz_s, st, st_o, upb_s,
        sem_w, sem_m, sem_o, sem_p,
    ) = refs[8:]
    if pieces:

        def issue_out_weight(ref, i, core, y):
            pltpu.make_async_copy(
                ref.at[pl.ds(24, 3)], wo.at[pl.ds(3 * y, 3), 2 * i + core], sem_w
            ).start()

        def issue_feed(ref, i, core, y):
            pltpu.make_async_copy(ref.at[pl.ds(0, 24)], feed.at[2 * y + core, i], sem_m).start()

        piece_loop(meta, quads, issue_out_weight)
        piece_loop(meta, quads, issue_feed)
    else:
        pltpu.make_async_copy(quads[0], wo, sem_w).start()
        pltpu.make_async_copy(quads[1], feed, sem_m).start()
    total = lens[0, 0] + lens[0, 1]
    row_of = lambda name: vec[ROW_OF[name] : ROW_OF[name] + 1, :]
    gain2, shift2, outb, downb = (row_of(n) for n in ("gain2", "shift2", "outb", "downb"))
    for t in range(3):
        upb_s[t : t + 1, :] = jnp.concatenate(
            [
                vec[
                    ROW_OF["upb"] + i // 2 : ROW_OF["upb"] + i // 2 + 1,
                    384 * (i % 2) + 128 * t : 384 * (i % 2) + 128 * t + 128,
                ]
                for i in range(8)
            ],
            axis=1,
        )
    sums_o[...] = jnp.zeros_like(sums_o)

    def attended(at):
        return jnp.concatenate([ref[p, at, :] for p in range(2) for ref in (o_0, o_1, o_2)], axis=1)

    wait(wo, sem_w)
    w_out = lanes(wo, 6)

    def prologue(at, r):
        h = tok[at, :].astype(f32) + branch_scale * (nn(attended(at), w_out) + outb)
        h_s[at, :] = h
        n2, _ = normalize(h)
        a2_s[at, :] = (n2 * gain2 + shift2).astype(bf16)
        live = (lax.broadcasted_iota(jnp.int32, (QB, D), 0) + QB * r) < total
        dm = (branch_scale * jnp.where(live, cot[at, :].astype(f32), 0.0)).astype(bf16)
        dm_s[at, :] = dm
        sums_o[ROW_DN : ROW_DN + 1, :D] += jnp.sum(dm.astype(f32), axis=0, keepdims=True)

    over_rows(prologue)
    a2t_s[...] = a2_s[...].T
    dmt_s[...] = dm_s[...].T
    m_s[...] = jnp.zeros_like(m_s)
    da2_s[...] = jnp.zeros_like(da2_s)
    wait(feed, sem_m)
    c0 = 0.7978845608028654
    c1 = 0.044715 * c0

    def emit(own, other, base):
        def issue(ref, i, core, y):
            pltpu.make_async_copy(st.at[2 * y + core, i], ref.at[pl.ds(base, 8)], sem_o).start()

        place_loop(pieces, meta, own, other, issue)

    def step(t, carry):
        up = jnp.concatenate(
            [feed[n, :, pl.ds(8 * t + 2 * h, 2)].reshape(D, 128) for n in range(4) for h in range(2)],
            axis=1,
        )
        dn = jnp.concatenate(
            [feed[:, i, pl.ds(8 * t + 4, 4)].reshape(D, 128) for i in range(8)], axis=1
        )
        bup = upb_s[pl.ds(t, 1), :]
        sums_o[pl.ds(ROW_UP + t, 1), :] = jnp.zeros((1, 1024), f32)

        def some(r, carry):
            at = pl.ds(pl.multiple_of(r * 256, 256), 256)
            z = nn(a2_s[at, :], up) + bup
            dgl = nn(dm_s[at, :], dn)
            zz = z * z
            th = jnp.tanh(z * (c0 + c1 * zz))
            half = 0.5 * th + 0.5
            gl = (z * half).astype(bf16)
            slope = half + (0.5 * z) * (1.0 - th * th) * (c0 + (3.0 * c1) * zz)
            dz = (dgl * slope).astype(bf16)
            gl_s[at, :] = gl
            dz_s[at, :] = dz
            sums_o[pl.ds(ROW_UP + t, 1), :] += jnp.sum(dz.astype(f32), axis=0, keepdims=True)
            m_s[at, :] += nt(gl, dn)
            da2_s[at, :] += nt(dz, up)
            return carry

        lax.fori_loop(0, 4, some, 0)

        @pl.when(t >= 1)
        def _():
            wait(st, sem_o)


        for n in range(4):
            at = pl.ds(256 * n, 256)
            grad = nn(a2t_s[...], dz_s[:, at]).astype(bf16)
            for h in range(2):
                st[n, :, 2 * h : 2 * h + 2] = grad[:, 128 * h : 128 * h + 128].reshape((8, 2) + UNIT)
            grad = nn(dmt_s[...], gl_s[:, at]).astype(bf16)
            for h in range(2):
                st[:, 2 * n + h, 4:8] = grad[:, 128 * h : 128 * h + 128].reshape((4, 4) + UNIT)

        @pl.when(t == 0)
        def _():
            emit(own_a, other_a, 0)

        @pl.when(t == 1)
        def _():
            emit(own_a, other_a, 8)

        @pl.when(t == 2)
        def _():
            emit(own_b, other_b, 0)

        return carry

    lax.fori_loop(0, 3, step, 0)

    def epilogue(at, r):
        h = h_s[at, :]
        out_o[at, :] = (h + branch_scale * (m_s[at, :] + downb)).astype(bf16)
        n2, r2 = normalize(h)
        da2 = da2_s[at, :]
        sums_o[ROW_G2 : ROW_G2 + 1, :D] += jnp.sum(da2 * n2, axis=0, keepdims=True)
        sums_o[ROW_B2 : ROW_B2 + 1, :D] += jnp.sum(da2, axis=0, keepdims=True)
        e = da2 * gain2
        live = (lax.broadcasted_iota(jnp.int32, (QB, D), 0) + QB * r) < total
        dy = jnp.where(live, cot[at, :].astype(f32), 0.0)
        dh = dy + r2 * (
            e
            - jnp.mean(e, axis=-1, keepdims=True)
            - n2 * jnp.mean(e * n2, axis=-1, keepdims=True)
        )
        dh_o[at, :] = dh
        du = (branch_scale * dh).astype(bf16)
        sums_o[ROW_OB : ROW_OB + 1, :D] += jnp.sum(du.astype(f32), axis=0, keepdims=True)
        dm_s[at, :] = du
        do = nt(du, w_out).astype(bf16)
        for g in range(6):
            do_o[g, at, :] = do[:, 128 * g : 128 * g + 128]

    over_rows(epilogue)
    a2t_s[...] = attended(pl.ds(0, ROWS)).T
    grad = nn(a2t_s[...], dm_s[...])
    for g in range(6):
        st_o[g] = grad[:, 128 * g : 128 * g + 128].astype(bf16).reshape((16,) + UNIT)

    def issue_out(ref, i, core, y):
        pltpu.make_async_copy(
            st_o.at[pl.ds(3 * y, 3), 2 * i + core], ref.at[pl.ds(8, 3)], sem_p
        ).start()

    place_loop(pieces, meta, own_b, other_b, issue_out)
    wait(st, sem_o)
    wait(st_o, sem_p)


def middle(pieces, meta, lens, tokens, attended, cotangent, vec, weights):
    block = (16,) + UNIT
    return pl.pallas_call(
        lambda *refs: middle_body(pieces, *refs),
        out_shape=(
            sds((ROWS, D), bf16),
            sds((ROWS, D), f32),
            sds((6, ROWS, 128), bf16),
            *places(pieces, 16),
            *places(pieces, 11),
            sds((8, 1024), f32),
        ),
        in_specs=[SM, SM, VM, VM, VM, VM, VM, VM] + [HB] * len(weights),
        out_specs=(VM, VM, VM, HB, HB, HB, HB, VM),
        scratch_shapes=[
            pltpu.VMEM((6,) + block, bf16),
            pltpu.VMEM((4, 8, 24) + UNIT, bf16),
            pltpu.VMEM((ROWS, D), f32),
            pltpu.VMEM((ROWS, D), bf16),
            pltpu.VMEM((D, ROWS), bf16),
            pltpu.VMEM((ROWS, D), bf16),
            pltpu.VMEM((D, ROWS), bf16),
            pltpu.VMEM((ROWS, D), f32),
            pltpu.VMEM((ROWS, D), f32),
            pltpu.VMEM((ROWS, 1024), bf16),
            pltpu.VMEM((ROWS, 1024), bf16),
            pltpu.VMEM((4, 8, 8) + UNIT, bf16),
            pltpu.VMEM((6,) + block, bf16),
            pltpu.VMEM((8, 1024), f32),
            pltpu.SemaphoreType.DMA(()),
            pltpu.SemaphoreType.DMA(()),
            pltpu.SemaphoreType.DMA(()),
            pltpu.SemaphoreType.DMA(()),
        ],
        name="middle",
        **params(60e9, 40e6, 50),
    )(meta, lens, tokens, *attended, cotangent, vec, *weights)


def back_pair(far, q_ref, k_ref, v_ref, do_ref, lse_ref, out, pair, dk_s, dv_s):
    lane = lax.broadcasted_iota(jnp.int32, (QB, 128), 1)
    causal = lax.broadcasted_iota(jnp.int32, (QB, QB), 0) <= lax.broadcasted_iota(
        jnp.int32, (QB, QB), 1
    )
    kt = k_ref[...].T
    sub = lax.broadcasted_iota(jnp.int32, (128, ROWS), 0)
    dk_s[...] = jnp.zeros_like(dk_s)
    dv_s[...] = jnp.zeros_like(dv_s)
    for j in range(ROWS // QB):
        size = QB * (j + 1)
        q = q_ref[QB * j : size, :]
        do = do_ref[QB * j : size, :]
        dq = jnp.zeros((128, QB), f32)
        dk = jnp.zeros((size, 128), f32)
        dv = jnp.zeros((size, 128), f32)
        for h in range(2):
            mine = (lane < HD) if h == 0 else (lane >= HD)
            qh = jnp.where(mine, q, jnp.zeros_like(q))
            doh = jnp.where(mine, do, jnp.zeros_like(do))
            s = nt(k_ref[:size, :], qh)
            parts = []
            if j >= 2:
                parts.append(s[:512] + far)
                if j == 3:
                    parts.append(s[512:768])
            elif j == 1:
                parts.append(s[:QB])
            parts.append(jnp.where(causal, s[size - QB :], NEG))
            s = jnp.concatenate(parts, axis=0)
            p = jnp.exp(s - lse_ref[h : h + 1, QB * j : size])
            dp = nt(v_ref[:size, :], doh)
            dot = jnp.sum(p * dp, axis=0, keepdims=True)
            ds = (p * (dp - dot)).astype(bf16)
            dv += nn(p.astype(bf16), doh)
            dk += nn(ds, qh)
            keep = (sub < HD) if h == 0 else (sub >= HD)
            dq += nn(jnp.where(keep, kt, jnp.zeros_like(kt))[:, :size], ds)
        out[pair, QB * j : size, :] = (dq.T * (1.0 / HD)).astype(bf16)
        dk_s[:size, :] += dk
        dv_s[:size, :] += dv
    out[2 + pair] = dk_s[...].astype(bf16)
    out[4 + pair] = dv_s[...].astype(bf16)


def back_body(pieces, third, meta, lens, qkv, do, lse, a1t, wq, vec, *refs):
    if third > 0:
        refs = refs[2:]
    if third == 2:
        mid, sums_0, sums_1, *refs = refs
    dqkv_o, own, other, sums_o, dk_s, dv_s, st, st_v, sem, sem2 = refs
    far = jnp.where(lens[0, 0] < ROWS, NEG, 0.0).astype(f32)

    def one(pair, carry):
        back_pair(
            far, qkv.at[pair], qkv.at[2 + pair], qkv.at[4 + pair], do.at[third + 3 * pair], lse.at[pair],
            dqkv_o, pair, dk_s, dv_s,
        )
        return carry

    lax.fori_loop(0, 2, one, 0)
    raw = jnp.zeros((D, 128), f32)
    plain = jnp.zeros((D, 128), f32)
    cols = []
    for two in range(3):
        blocks = nn(a1t[...], jnp.concatenate([dqkv_o[2 * two], dqkv_o[2 * two + 1]], axis=1))
        for g in (2 * two, 2 * two + 1):
            block = blocks[:, 128 * (g % 2) : 128 * (g % 2) + 128]
            col = jnp.sum(dqkv_o[g].astype(f32), axis=0, keepdims=True)
            cols.append(col)
            st[g] = block.astype(bf16).reshape((16,) + UNIT)
            weight = wq[g].reshape(D, 128).astype(f32)
            raw += block * weight
            plain += weight * col
    base = 3 * third

    def issue(ref, i, core, y):
        pltpu.make_async_copy(
            st.at[pl.ds(3 * y, 3), 2 * i + core], ref.at[pl.ds(base, 3)], sem
        ).start()

    place_loop(pieces, meta, own, other, issue)
    raw = jnp.sum(raw, axis=1, keepdims=True)
    plain = jnp.sum(plain, axis=1, keepdims=True)
    lane = lax.broadcasted_iota(jnp.int32, (D, 128), 1)
    flat = jnp.where(lane == 0, raw, plain).T[:8]
    sums = jnp.concatenate([jnp.concatenate(cols, axis=1), flat[:2], jnp.zeros((5, D), f32)], axis=0)
    sums_o[...] = sums
    if third == 2:
        per = [sums_0[...], sums_1[...], sums]
        raw = per[0][1:2] + per[1][1:2] + per[2][1:2]
        shift = per[0][2:3] + per[1][2:3] + per[2][2:3]
        row_of = lambda name: vec[ROW_OF[name] : ROW_OF[name] + 1, :]
        gain = (raw - row_of("shift1") * shift) / row_of("gain1")
        pick = lambda g: jnp.concatenate(
            [per[p % 3][0:1, 128 * (g + p // 3) : 128 * (g + p // 3) + 128] for p in range(6)], axis=1
        )
        known = {
            "outb": mid[ROW_OB : ROW_OB + 1, :D],
            "downb": mid[ROW_DN : ROW_DN + 1, :D],
            "gain1": gain,
            "shift1": shift,
            "gain2": mid[ROW_G2 : ROW_G2 + 1, :D],
            "shift2": mid[ROW_B2 : ROW_B2 + 1, :D],
        }
        rows = {ROW_OF["qv"]: pick(0), ROW_OF["qv"] + 1: pick(4)}
        for name, value in known.items():
            rows[ROW_OF[name]] = value
        for r in range(4):
            rows[ROW_OF["upb"] + r] = jnp.concatenate(
                [
                    mid[ROW_UP + t : ROW_UP + t + 1, 128 * i : 128 * i + 128]
                    for i in (2 * r, 2 * r + 1)
                    for t in range(3)
                ],
                axis=1,
            )
        groups = pack_small(lambda r: rows[r])
        for g in range(3):
            st_v[:, 16 * g : 16 * g + 16, :] = jnp.broadcast_to(
                groups[g][:, None, :], (32, 16, 128)
            ).astype(bf16)

        def issue_small(ref, i, core, y):
            pltpu.make_async_copy(st_v.at[i * 4 + 2 * y + core], ref.at[9], sem2).start()

        place_loop(pieces, meta, own, other, issue_small)
        wait(st_v, sem2)
    wait(st, sem)


def back(pieces, third, meta, lens, qkv, do, lse, a1t, wq, vec, before):
    args = [meta, lens, qkv, do, lse, a1t, wq, vec, *before]
    extra = [HB, HB] * (third > 0) + [VM, VM, VM] * (third == 2)
    return pl.pallas_call(
        lambda *refs: back_body(pieces, third, *refs),
        out_shape=(
            sds((6, ROWS, 128), bf16),
            *places(pieces, 10),
            sds((8, D), f32),
        ),
        in_specs=[SM, SM] + [VM] * 6 + extra,
        out_specs=(VM, HB, HB, VM),
        input_output_aliases={8: 1, 9: 2} if third > 0 else {},
        scratch_shapes=[
            pltpu.VMEM((ROWS, 128), f32),
            pltpu.VMEM((ROWS, 128), f32),
            pltpu.VMEM((6, 16) + UNIT, bf16),
            pltpu.VMEM((32,) + UNIT, bf16),
            pltpu.SemaphoreType.DMA(()),
            pltpu.SemaphoreType.DMA(()),
        ],
        name=f"back_{third}",
        **params(18e9, 8e6, 20),
    )(*args)


def first_norm_back_body(tok, d_0, d_1, d_2, w_0, w_1, w_2, dh, vec, *refs):
    gt_o = refs[-1]
    gain1 = vec[ROW_OF["gain1"] : ROW_OF["gain1"] + 1, :]

    def body(at, r):
        da1 = jnp.zeros((QB, D), f32)
        for grad, weight in ((d_0, w_0), (d_1, w_1), (d_2, w_2)):
            rows = jnp.concatenate([grad[g, at, :] for g in range(6)], axis=1)
            da1 += nt(rows, lanes(weight, 6))
        n1, r1 = normalize(tok[at, :].astype(f32))
        e = da1 * gain1
        back = r1 * (
            e
            - jnp.mean(e, axis=-1, keepdims=True)
            - n1 * jnp.mean(e * n1, axis=-1, keepdims=True)
        )
        gt_o[at, :] = (dh[at, :] + back).astype(bf16)

    over_rows(body, 2)


def first_norm_back(half, tokens, grads, weights, dh, vec, before=None):
    count = ROWS // 2
    rows = pl.BlockSpec((count, D), lambda g: (half, 0))
    every = lambda shape: pl.BlockSpec(shape, lambda g: (0,) * len(shape))
    return pl.pallas_call(
        first_norm_back_body,
        grid=(1,),
        out_shape=sds((ROWS, D), bf16),
        in_specs=[rows]
        + [pl.BlockSpec((6, count, 128), lambda g: (0, half, 0))] * 3
        + [every((6, 16) + UNIT)] * 3
        + [rows, every((VECS, D))]
        + ([] if before is None else [HB]),
        out_specs=rows,
        input_output_aliases={} if before is None else {9: 0},
        name=f"first_norm_back_{half}",
        **params(8e9, 9e6, 14),
    )(tokens, *grads, *weights, dh, vec, *(() if before is None else (before,)))


def links(step):
    pairs = []
    for z in range(4):
        for x in range(2):
            for y in range(2):
                for c in range(2):
                    tz, tx, ty, tc = step(z, x, y, c)
                    pairs.append(((z * 2 + x) * 4 + y * 2 + c, (tz * 2 + tx) * 4 + ty * 2 + tc))
    return pairs


TO_CORE = links(lambda z, x, y, c: (z, x, y, 1 - c))
TO_FIRST = links(lambda z, x, y, c: (z, 1 - x, y, c) if c == 0 else (z, x, 1 - y, c))
TO_SECOND = links(lambda z, x, y, c: (z, x, 1 - y, c) if c == 0 else (z, 1 - x, y, c))
TO_Z = [None] + [links(lambda z, x, y, c, k=k: (z ^ k, x, y, c)) for k in (1, 2, 3)]


def send(value, pairs):
    return lax.ppermute(value, BOTH, pairs)


def after(value, *others):
    return lax.optimization_barrier((value, *others))[0]


def add(*parts):
    total = parts[0].astype(f32)
    for part in parts[1:]:
        total = total + part.astype(f32)
    return total


def split(big, sizes):
    out, at = [], 0
    for size in sizes:
        out.append(big[at : at + size])
        at += size
    return out


def as_units(block):
    a, b = block.shape[0] // 48, block.shape[1] // 128
    return block.reshape(a, 48, b, 128).transpose(2, 0, 1, 3).reshape(a * b, 48, 128)


def first_pieces(qkv_weight, out_weight, small):
    core = lax.axis_index("narrow") % 2
    both = jnp.concatenate([qkv_weight, out_weight], axis=1).astype(bf16)
    keep = jnp.where(core == 0, both[:48], both[48:])
    give = jnp.where(core == 0, both[48:], both[:48])
    got = send(give, TO_CORE)
    left = jnp.where(core == 0, keep, got)
    right = jnp.where(core == 0, got, keep)
    cols = as_units(jnp.concatenate([left[:, :576], right[:, :576]], axis=1))
    out = as_units(jnp.concatenate([left[:, 576:], right[:, 576:]], axis=1))
    thirds = [cols[g] for t in range(3) for g in (t, 3 + t, 6 + t)]
    return jnp.concatenate([jnp.stack(thirds), small], axis=0), out


def feed_pieces(up_weight, down_weight):
    up = as_units(up_weight.astype(bf16))
    down = as_units(down_weight.astype(bf16).T)
    out = []
    for t in range(3):
        out.append(jnp.concatenate([up[2 * t : 2 * t + 2], up[6 + 2 * t : 8 + 2 * t], down[4 * t : 4 * t + 4]]))
    return out


def whole(value, dims):
    for axis, dim in dims:
        value = lax.all_gather(value, axis, axis=dim, tiled=True)
    return value


def plain_weights(qkv_weight, out_weight, up_weight, down_weight, vectors):
    matrix = lambda w: whole(w.astype(bf16), (("narrow", 1), ("wide", 0)))
    blocks = lambda w, b: w.reshape(16, 48, b, 128).transpose(2, 0, 1, 3)
    wq = blocks(matrix(qkv_weight), 18)
    wq = [jnp.stack([wq[g] for g in (t, 3 + t, 6 + t, 9 + t, 12 + t, 15 + t)]) for t in range(3)]
    wo = blocks(matrix(out_weight), 6)
    up = blocks(matrix(up_weight), 24).reshape(4, 2, 3, 8, 2, 48, 128)
    up = up.transpose(0, 3, 2, 1, 4, 5, 6).reshape(4, 8, 3, 4, 48, 128)
    down = blocks(matrix(down_weight).T, 24).reshape(8, 3, 4, 4, 48, 128).transpose(2, 0, 1, 3, 4, 5)
    feed = jnp.concatenate([up, down], axis=3).reshape(4, 8, 24, 48, 128)
    rows = [
        whole(vectors[name].astype(bf16), (("narrow", 0), ("wide", 0))).astype(f32).reshape(count, D)
        for name, _, _, count in SMALL
    ]
    vec = jnp.concatenate(rows + [jnp.zeros((VECS - 12, D), f32)], axis=0)
    return wq, wo, feed, vec


def plain_grads(q_all, m_a, m_b):
    def reduce(matrix):
        rows = lax.psum_scatter(matrix.astype(f32), "wide", scatter_dimension=0, tiled=True)
        return lax.psum_scatter(rows.astype(bf16), "narrow", scatter_dimension=1, tiled=True).astype(f32)

    def vector(values):
        rows = lax.psum_scatter(values, "wide", scatter_dimension=0, tiled=True)
        return lax.psum_scatter(rows.astype(bf16), "narrow", scatter_dimension=0, tiled=True).astype(f32)

    q = q_all[:, :, :9].reshape(8, 2, 2, 3, 3, 48, 128)
    qkv = q.transpose(0, 2, 5, 1, 4, 3, 6).reshape(D, 2304)
    out = m_b[:, :, 8:].reshape(8, 2, 2, 3, 48, 128).transpose(0, 2, 4, 1, 3, 5).reshape(D, D)
    m = jnp.concatenate([m_a, m_b[:, :, :8]], axis=2).reshape(8, 4, 3, 2, 4, 48, 128)
    up = m[:, :, :, 0].reshape(8, 4, 3, 2, 2, 48, 128).transpose(0, 4, 5, 1, 3, 2, 6).reshape(D, FF)
    down = m[:, :, :, 1].transpose(0, 2, 5, 1, 3, 4).reshape(FF, D)
    small = q_all[:, :, 9].reshape(32, 3, 16, 128)[:, :, 0].reshape(32, 384).astype(f32)
    vecs = {name: vector(small[:, off : off + wd].reshape(-1)) for name, off, wd, _ in SMALL}
    return reduce(qkv), reduce(out), reduce(up), reduce(down), vecs


class Spread:
    def __init__(self, piece, *waits):
        near = send(after(piece, *waits), TO_Z[1])
        self.parts = [piece, near] + [send(piece, TO_Z[k]) for k in (2, 3)]

    def along(self, *waits):
        self.line = after(jnp.stack(self.parts, axis=0), *waits)
        self.first = send(self.line, TO_FIRST)
        self.second = send(self.line, TO_SECOND)

    def across(self, *waits):
        self.corner = send(after(self.first, *waits), TO_SECOND)

    def swap(self, *waits):
        self.swapped = [send(after(part, *waits), TO_CORE) for part in (self.line, self.first, self.second)]

    def end(self, *waits):
        last = send(after(self.corner, *waits), TO_CORE)
        return (self.line, self.first, self.second, self.corner, *self.swapped, last)


class Fold:
    def __init__(self, own, other):
        self.own = own
        self.got = send(other, TO_CORE)

    def second(self, *waits):
        self.got = after(self.got, *waits)
        self.sum_2 = add(self.own[2:], self.got[2:]).astype(bf16)
        self.sec = send(self.sum_2, TO_SECOND)

    def first(self, *waits):
        self.sec = after(self.sec, *waits)
        self.sum_1 = add(self.own[1], self.got[1], self.sec[1]).astype(bf16)
        self.fst = send(self.sum_1, TO_FIRST)

    def line(self, *waits):
        self.fst = after(self.fst, *waits)
        mine = [add(self.own[0, k], self.got[0, k], self.sec[0, k], self.fst[k]) for k in range(4)]
        self.mine = mine[0]
        self.sum_0 = [part.astype(bf16) for part in mine[1:]]
        self.far = [send(part, TO_Z[k + 1]) for k, part in enumerate(self.sum_0)]

    def end(self, *waits):
        return add(self.mine, *(after(part, *waits) for part in self.far))


def joined(blocks):
    return jnp.concatenate(blocks, axis=1)


def fast_grads(q_all, m_a, m_b):
    core = lax.axis_index("narrow") % 2
    m = jnp.concatenate([m_a, m_b[:8]], axis=0).reshape(3, 2, 4, 48, 128)
    grad_up = joined([m[t, 0, 2 * h : 2 * h + 2].reshape(96, 128) for h in range(2) for t in range(3)])
    grad_down = joined([m[t, 1].reshape(192, 128) for t in range(3)]).T
    cols = joined([q_all[3 * t + g] for g in range(3) for t in range(3)])
    outs = joined([m_b[8 + g] for g in range(3)])
    low = joined([cols[:, :576], outs[:, :192]])
    high = joined([cols[:, 576:], outs[:, 192:]])
    keep = jnp.where(core == 0, low, high)
    got = send(jnp.where(core == 0, high, low), TO_CORE)
    rows = jnp.concatenate([jnp.where(core == 0, keep, got), jnp.where(core == 0, got, keep)], axis=0)
    small = q_all[9].reshape(3, 16, 128)[:, 0].reshape(384)
    vecs = {name: small[off : off + wd] for name, off, wd, _ in SMALL}
    return rows[:, :576], rows[:, 576:], grad_up, grad_down, vecs


def local(
    tokens,
    qkv_weight,
    qv_bias,
    out_weight,
    out_bias,
    up_weight,
    up_bias,
    down_weight,
    down_bias,
    norm1_gain,
    norm1_bias,
    norm2_gain,
    norm2_bias,
    lengths,
    cotangent,
    fast,
):
    vectors = {
        "qv": qv_bias,
        "outb": out_bias,
        "downb": down_bias,
        "gain1": norm1_gain,
        "shift1": norm1_bias,
        "gain2": norm2_gain,
        "shift2": norm2_bias,
        "upb": up_bias,
    }
    meta = jnp.stack([lax.axis_index("wide"), lax.axis_index("narrow")]).astype(jnp.int32)
    if fast:
        zeros = lambda size: jnp.zeros((size,), f32)
        small = jnp.concatenate(
            [qv_bias, out_bias, down_bias, norm1_gain, zeros(8)]
            + [norm1_bias, norm2_gain, norm2_bias, zeros(56), up_bias, zeros(32)]
        )
        small = jnp.pad(small.astype(bf16).reshape(3, 1, 128), ((0, 0), (0, 15), (0, 0))).reshape(1, 48, 128)
        piece_q, piece_o = first_pieces(qkv_weight, out_weight, small)
        feed = feed_pieces(up_weight, down_weight)
        heads = Spread(piece_q)
        rest = Spread(jnp.concatenate(feed + [piece_o]), heads.parts[1])
        heads.along(rest.parts[1])
        heads.across(rest.parts[2])
        heads.swap()
        ready = heads.end()
        rest.along(heads.corner)
        first = after(tokens, rest.line)
        a1, a1t, vec, qkv_0, o_0, lse_0, wq_0 = front(True, 0, meta, lengths, first, None, ready)
        qkv_1, o_1, lse_1, wq_1 = front(True, 1, meta, lengths, a1, vec, ready)
        rest.across(o_1)
        rest.swap(o_1)
        qkv_2, o_2, lse_2, wq_2 = front(True, 2, meta, lengths, a1, vec, ready)
        weights = rest.end(o_2)
    else:
        wq, wo, feed, vec = plain_weights(qkv_weight, out_weight, up_weight, down_weight, vectors)
        a1, a1t, vec, qkv_0, o_0, lse_0, wq_0 = front(False, 0, meta, lengths, tokens, vec, (wq[0],))
        qkv_1, o_1, lse_1, wq_1 = front(False, 1, meta, lengths, a1, vec, (wq[1],))
        qkv_2, o_2, lse_2, wq_2 = front(False, 2, meta, lengths, a1, vec, (wq[2],))
        weights = (wo, feed)
    output, dh, do, own_a, other_a, own_b, other_b, mid = middle(
        fast, meta, lengths, tokens, (o_0, o_1, o_2), cotangent, vec, weights
    )
    args = lambda qkv, lse, wq: (qkv, do, lse, a1t, wq, vec)
    d_0, own, other, sums_0 = back(fast, 0, meta, lengths, *args(qkv_0, lse_0, wq_0), ())
    if fast:
        ff_a, ff_b = Fold(own_a, other_a), Fold(own_b, other_b)
        ff_a.second(d_0)
        do = after(do, ff_a.sum_2, ff_b.got)
    d_1, own, other, sums_1 = back(fast, 1, meta, lengths, *args(qkv_1, lse_1, wq_1), (own, other))
    if fast:
        ff_b.second(d_1)
        ff_a.first(d_1)
        do = after(do, ff_b.sum_2, ff_a.sum_1)
    d_2, own, other, _ = back(
        fast, 2, meta, lengths, *args(qkv_2, lse_2, wq_2), (own, other, mid, sums_0, sums_1)
    )
    grads, weights = (d_0, d_1, d_2), (wq_0, wq_1, wq_2)
    if fast:
        at = Fold(own, other)
        ff_b.first(d_2)
        dh = after(dh, ff_b.sum_1)
    top = first_norm_back(0, tokens, grads, weights, dh, vec)
    if fast:
        ff_a.line(top)
        at.second(top)
        dh = after(dh, at.sum_2, *ff_a.sum_0)
    grad_tokens = first_norm_back(1, tokens, grads, weights, dh, vec, top)
    if fast:
        at.first(grad_tokens)
        total_a = ff_a.end(at.sum_1)
        ff_b.line(total_a)
        at.line(*ff_b.sum_0)
        g_qkv, g_out, g_up, g_down, vecs = fast_grads(at.end(), total_a, ff_b.end(at.far[0]))
    else:
        g_qkv, g_out, g_up, g_down, vecs = plain_grads(own, own_a, own_b)
    return (
        output,
        grad_tokens,
        g_qkv,
        vecs["qv"],
        g_out,
        vecs["outb"],
        g_up,
        vecs["upb"],
        g_down,
        vecs["downb"],
        vecs["gain1"],
        vecs["shift1"],
        vecs["gain2"],
        vecs["shift2"],
    )


def solution(mesh):
    fast = mesh.shape["wide"] == 8 and mesh.shape["narrow"] == 4
    rows, matrix, vector = P(BOTH, None), P("wide", "narrow"), P(BOTH)
    return jax.shard_map(
        lambda *args: local(*args, fast),
        mesh=mesh,
        in_specs=(
            rows, matrix, vector, matrix, vector, matrix, vector, matrix, vector,
            vector, vector, vector, vector, rows, rows,
        ),
        out_specs=(
            rows, rows, matrix, vector, matrix, vector, matrix, vector, matrix, vector,
            vector, vector, vector, vector,
        ),
        check_vma=False,
    )
```

```python
import jax
import jax.numpy as jnp
import numpy as np
from jax import lax
from jax.experimental import pallas as pl
from jax.experimental.pallas import tpu as pltpu
from jax.sharding import PartitionSpec as P

HEADS = 12
BOTH = ("wide", "narrow")
bf16 = jnp.bfloat16
f32 = jnp.float32
epsilon = 1e-05
branch_scale = 24 ** (-0.5)
D = 768
FF = 3072
HD = 64
ROWS = 1024
QB = 256
NEG = -1e30
UNIT = (48, 128)
SMALL = (
    ("qv", 0, 48, 2),
    ("outb", 48, 24, 1),
    ("downb", 72, 24, 1),
    ("gain1", 96, 24, 1),
    ("shift1", 128, 24, 1),
    ("gain2", 152, 24, 1),
    ("shift2", 176, 24, 1),
    ("upb", 256, 96, 4),
)
ROW_OF = {}
_row = 0
for _name, _off, _wd, _n in SMALL:
    ROW_OF[_name] = _row
    _row += _n
VECS = 16


def nn(a, b):
    return lax.dot_general(a, b, (((1,), (0,)), ((), ())), preferred_element_type=f32)


def nt(a, b):
    return lax.dot_general(a, b, (((1,), (1,)), ((), ())), preferred_element_type=f32)


def normalize(values):
    average = jnp.mean(values, axis=-1, keepdims=True)
    centred = values - average
    spread = jnp.mean(centred * centred, axis=-1, keepdims=True)
    rinv = lax.rsqrt(spread + epsilon)
    return centred * rinv, rinv


def params(flops, bytes_accessed, mib=60):
    return dict(
        compiler_params=pltpu.CompilerParams(vmem_limit_bytes=mib * 1024 * 1024),
        cost_estimate=pl.CostEstimate(
            flops=int(flops), transcendentals=0, bytes_accessed=int(bytes_accessed)
        ),
    )


VM = pl.BlockSpec(memory_space=pltpu.VMEM)
SM = pl.BlockSpec(memory_space=pltpu.SMEM)
HB = pl.BlockSpec(memory_space=pl.ANY)


def sds(shape, dtype):
    return jax.ShapeDtypeStruct(shape, dtype)


def over_rows(body, blocks=ROWS // QB):
    def step(r, carry):
        body(pl.ds(pl.multiple_of(r * QB, QB), QB), r)
        return carry

    lax.fori_loop(0, blocks, step, 0)


def wait(ref, sem):
    pltpu.make_async_copy(ref, ref, sem).wait()


def lanes(ref, count):
    return jnp.concatenate([ref[g].reshape(D, 128) for g in range(count)], axis=1)


def held_by(meta, q, k, own):
    w, n = meta[0], meta[1]
    z, x, y, c = w // 2, w % 2, n // 2, n % 2
    core = c if own else 1 - c
    first, second = q % 2, q // 2
    dx = jnp.where(core == 0, first, second)
    dy = jnp.where(core == 0, second, first)
    zz = z ^ k
    return zz * 2 + (x ^ dx), core, y ^ dy


def piece_loop(meta, quads, issue):
    for own in (True, False):
        for q in range(4):
            ref = quads[q if own else 4 + q]
            for k in range(4):
                i, core, y = held_by(meta, q, k, own)
                issue(ref.at[k], i, core, y)


def place_loop(pieces, meta, own, other, issue):
    if pieces:
        for mine, ref in ((True, own), (False, other)):
            for q in range(4):
                for k in range(4):
                    i, core, y = held_by(meta, q, k, mine)
                    issue(ref.at[q, k], i, core, y)
    else:
        for i in range(8):
            for n in range(4):
                issue(own.at[i, n], i, n % 2, n // 2)


def places(pieces, units):
    if pieces:
        return (sds((4, 4, units) + UNIT, bf16), sds((4, 4, units) + UNIT, bf16))
    return (sds((8, 4, units) + UNIT, bf16), sds((8, 128), bf16))


def small_map(off, wd, row):
    lane = lax.broadcasted_iota(jnp.int32, (128, D), 1) + row * D
    within = lane - wd * jnp.floor((lane.astype(f32) + 0.5) * (1.0 / wd)).astype(jnp.int32)
    src = lax.broadcasted_iota(jnp.int32, (128, D), 0)
    return jnp.where(src == within + off % 128, 1.0, 0.0).astype(bf16)


def unpack_small(packed):
    rows = []
    for _, off, wd, count in SMALL:
        base = off // 128 * 16
        group = packed[:, base : base + 16, :].astype(f32)[:, 0, :].astype(bf16)
        for row in range(count):
            spread = nn(group, small_map(off, wd, row))
            lane = lax.broadcasted_iota(jnp.int32, (32, D), 1) + row * D
            low = lax.broadcasted_iota(jnp.int32, (32, D), 0) * wd
            keep = (lane >= low) & (lane < low + wd)
            rows.append(jnp.sum(jnp.where(keep, spread, 0.0), axis=0, keepdims=True))
    rows.append(jnp.zeros((VECS - len(rows), D), f32))
    return jnp.concatenate(rows, axis=0)


def pack_small(vec_row):
    groups = [jnp.zeros((32, 128), f32) for _ in range(3)]
    for name, off, wd, count in SMALL:
        for row in range(count):
            lane = lax.broadcasted_iota(jnp.int32, (32, D), 1) + row * D
            low = lax.broadcasted_iota(jnp.int32, (32, D), 0) * wd
            keep = (lane >= low) & (lane < low + wd)
            spread = jnp.where(keep, vec_row(ROW_OF[name] + row), 0.0).astype(bf16)
            groups[off // 128] += nt(spread, small_map(off, wd, row))
    return groups


def attend_rows(far, get, put):
    lane = lax.broadcasted_iota(jnp.int32, (QB, 128), 1)
    causal = lax.broadcasted_iota(jnp.int32, (QB, QB), 1) <= lax.broadcasted_iota(
        jnp.int32, (QB, QB), 0
    )
    for j in range(ROWS // QB):
        size = QB * (j + 1)
        q = get(0, QB * j, QB)
        outs, logs = [], []
        for h in range(2):
            mine = (lane < HD) if h == 0 else (lane >= HD)
            s = nt(jnp.where(mine, q, jnp.zeros_like(q)), get(1, 0, size))
            parts = []
            if j >= 2:
                parts.append(s[:, :512] + far)
                if j == 3:
                    parts.append(s[:, 512:768])
            elif j == 1:
                parts.append(s[:, :QB])
            parts.append(jnp.where(causal, s[:, size - QB :], NEG))
            s = jnp.concatenate(parts, axis=1)
            top = jnp.max(s, axis=1, keepdims=True)
            e = jnp.exp(s - top)
            total = jnp.sum(e, axis=1, keepdims=True)
            outs.append(nn(e.astype(bf16), get(2, 0, size)) * (1.0 / total))
            logs.append(top + jnp.log(total))
        put(QB * j, jnp.where(lane < HD, outs[0], outs[1]).astype(bf16), jnp.where(lane == 0, logs[0], logs[1]).T[:8])


def front_body(pieces, third, meta, lens, *refs):
    count = 8 if pieces else 1
    if third == 0:
        tok, quads, refs = refs[0], refs[1 : 1 + count], refs[1 + count :]
        if not pieces:
            vec_i, refs = refs[0], refs[1:]
        a1, a1t_o, vec, *refs = refs
    else:
        a1, vec, quads, refs = refs[0], refs[1], refs[2 : 2 + count], refs[2 + count :]
    qkv_o, o_o, lse_o, wq, packed, sem, sem2 = refs
    if pieces:

        def issue(ref, i, core, y):
            pltpu.make_async_copy(
                ref.at[pl.ds(3 * third, 3)], wq.at[pl.ds(3 * y, 3), 2 * i + core], sem
            ).start()
            if third == 0:
                pltpu.make_async_copy(ref.at[9], packed.at[i * 4 + 2 * y + core], sem2).start()

        piece_loop(meta, quads, issue)
    else:
        pltpu.make_async_copy(quads[0], wq, sem).start()
    if third == 0:
        if pieces:
            wait(packed, sem2)
            vec[...] = unpack_small(packed[...])
        else:
            vec[...] = vec_i[...]
        def first_norm(at, r):
            n1, _ = normalize(tok[at, :].astype(f32))
            a1[at, :] = (
                n1 * vec[ROW_OF["gain1"] : ROW_OF["gain1"] + 1, :]
                + vec[ROW_OF["shift1"] : ROW_OF["shift1"] + 1, :]
            ).astype(bf16)

        over_rows(first_norm)
        a1t_o[...] = a1[...].T
    wait(wq, sem)
    bias = []
    for g, row in ((0, 0), (1, 0), (4, 1), (5, 1)):
        lane = 128 * (third + 3 * (g % 2))
        bias.append(vec[ROW_OF["qv"] + row : ROW_OF["qv"] + row + 1, lane : lane + 128])
    zero = jnp.zeros((1, 128), f32)
    bias = jnp.concatenate([bias[0], bias[1], zero, zero, bias[2], bias[3]], axis=1)
    weights = lanes(wq, 6)

    def projection(at, r):
        block = (nn(a1[at, :], weights) + bias).astype(bf16)
        for g in range(6):
            part = block[:, 128 * g : 128 * g + 128]
            qkv_o[g, at, :] = part * jnp.asarray(1.0 / HD, bf16) if g < 2 else part

    over_rows(projection)
    far = jnp.where(lens[0, 0] < ROWS, NEG, 0.0).astype(f32)

    def one(pair, carry):
        def put(row, o, lse):
            o_o[pair, row : row + QB, :] = o
            lse_o[pair, :, row : row + QB] = lse

        attend_rows(far, lambda which, row, n: qkv_o[2 * which + pair, row : row + n, :], put)
        return carry

    lax.fori_loop(0, 2, one, 0)


def front(pieces, third, meta, lens, first, vec, weights):
    shapes = [
        sds((6, ROWS, 128), bf16),
        sds((2, ROWS, 128), bf16),
        sds((2, 8, ROWS), f32),
        sds((6, 16) + UNIT, bf16),
    ]
    if third == 0:
        shapes = [sds((ROWS, D), bf16), sds((D, ROWS), bf16), sds((VECS, D), f32)] + shapes
        args = (first,) + tuple(weights) + (() if pieces else (vec,))
        specs = [VM] + [HB] * len(weights) + ([] if pieces else [VM])
    else:
        args = (first, vec) + tuple(weights)
        specs = [VM, VM] + [HB] * len(weights)
    return pl.pallas_call(
        lambda *refs: front_body(pieces, third, *refs),
        out_shape=tuple(shapes),
        in_specs=[SM, SM] + specs,
        out_specs=(VM,) * len(shapes),
        scratch_shapes=[
            pltpu.VMEM((32,) + UNIT, bf16),
            pltpu.SemaphoreType.DMA(()),
            pltpu.SemaphoreType.DMA(()),
        ],
        name=f"front_{third}",
        **params(6e9, 8e6, 20),
    )(meta, lens, *args)


ROW_DN, ROW_G2, ROW_B2, ROW_OB, ROW_UP = 0, 1, 2, 3, 4


def middle_body(pieces, meta, lens, tok, o_0, o_1, o_2, cot, vec, *refs):
    count = 8 if pieces else 2
    quads, refs = refs[:count], refs[count:]
    out_o, dh_o, do_o, own_a, other_a, own_b, other_b, sums_o = refs[:8]
    (
        wo, feed, h_s, a2_s, a2t_s, dm_s, dmt_s, m_s, da2_s, gl_s, dz_s, st, st_o, upb_s,
        sem_w, sem_m, sem_o, sem_p,
    ) = refs[8:]
    if pieces:

        def issue_out_weight(ref, i, core, y):
            pltpu.make_async_copy(
                ref.at[pl.ds(24, 3)], wo.at[pl.ds(3 * y, 3), 2 * i + core], sem_w
            ).start()

        def issue_feed(ref, i, core, y):
            pltpu.make_async_copy(ref.at[pl.ds(0, 24)], feed.at[2 * y + core, i], sem_m).start()

        piece_loop(meta, quads, issue_out_weight)
        piece_loop(meta, quads, issue_feed)
    else:
        pltpu.make_async_copy(quads[0], wo, sem_w).start()
        pltpu.make_async_copy(quads[1], feed, sem_m).start()
    total = lens[0, 0] + lens[0, 1]
    row_of = lambda name: vec[ROW_OF[name] : ROW_OF[name] + 1, :]
    gain2, shift2, outb, downb = (row_of(n) for n in ("gain2", "shift2", "outb", "downb"))
    for t in range(3):
        upb_s[t : t + 1, :] = jnp.concatenate(
            [
                vec[
                    ROW_OF["upb"] + i // 2 : ROW_OF["upb"] + i // 2 + 1,
                    384 * (i % 2) + 128 * t : 384 * (i % 2) + 128 * t + 128,
                ]
                for i in range(8)
            ],
            axis=1,
        )
    sums_o[...] = jnp.zeros_like(sums_o)

    def attended(at):
        return jnp.concatenate([ref[p, at, :] for p in range(2) for ref in (o_0, o_1, o_2)], axis=1)

    wait(wo, sem_w)
    w_out = lanes(wo, 6)

    def prologue(at, r):
        h = tok[at, :].astype(f32) + branch_scale * (nn(attended(at), w_out) + outb)
        h_s[at, :] = h
        n2, _ = normalize(h)
        a2_s[at, :] = (n2 * gain2 + shift2).astype(bf16)
        live = (lax.broadcasted_iota(jnp.int32, (QB, D), 0) + QB * r) < total
        dm = (branch_scale * jnp.where(live, cot[at, :].astype(f32), 0.0)).astype(bf16)
        dm_s[at, :] = dm
        sums_o[ROW_DN : ROW_DN + 1, :D] += jnp.sum(dm.astype(f32), axis=0, keepdims=True)

    for r in range(ROWS // QB):
        prologue(pl.ds(QB * r, QB), r)
    a2t_s[...] = a2_s[...].T
    dmt_s[...] = dm_s[...].T
    m_s[...] = jnp.zeros_like(m_s)
    da2_s[...] = jnp.zeros_like(da2_s)
    wait(feed, sem_m)
    c0 = 0.7978845608028654
    c1 = 0.044715 * c0

    def emit(own, other, base):
        def issue(ref, i, core, y):
            pltpu.make_async_copy(st.at[2 * y + core, i], ref.at[pl.ds(base, 8)], sem_o).start()

        place_loop(pieces, meta, own, other, issue)

    def step(t, carry):
        up = jnp.concatenate(
            [feed[n, :, pl.ds(8 * t + 2 * h, 2)].reshape(D, 128) for n in range(4) for h in range(2)],
            axis=1,
        )
        dn = jnp.concatenate(
            [feed[:, i, pl.ds(8 * t + 4, 4)].reshape(D, 128) for i in range(8)], axis=1
        )
        bup = upb_s[pl.ds(t, 1), :]
        sums_o[pl.ds(ROW_UP + t, 1), :] = jnp.zeros((1, 1024), f32)

        def some(r, carry):
            at = pl.ds(pl.multiple_of(r * 256, 256), 256)
            z = nn(a2_s[at, :], up) + bup
            dgl = nn(dm_s[at, :], dn)
            zz = z * z
            th = jnp.tanh(z * (c0 + c1 * zz))
            half = 0.5 * th + 0.5
            gl = (z * half).astype(bf16)
            slope = half + (0.5 * z) * (1.0 - th * th) * (c0 + (3.0 * c1) * zz)
            dz = (dgl * slope).astype(bf16)
            gl_s[at, :] = gl
            dz_s[at, :] = dz
            sums_o[pl.ds(ROW_UP + t, 1), :] += jnp.sum(dz.astype(f32), axis=0, keepdims=True)
            m_s[at, :] += nt(gl, dn)
            da2_s[at, :] += nt(dz, up)
            return carry

        lax.fori_loop(0, 4, some, 0)

        @pl.when(t >= 1)
        def _():
            wait(st, sem_o)


        for n in range(4):
            at = pl.ds(256 * n, 256)
            grad = nn(a2t_s[...], dz_s[:, at]).astype(bf16)
            for h in range(2):
                st[n, :, 2 * h : 2 * h + 2] = grad[:, 128 * h : 128 * h + 128].reshape((8, 2) + UNIT)
            grad = nn(dmt_s[...], gl_s[:, at]).astype(bf16)
            for h in range(2):
                st[:, 2 * n + h, 4:8] = grad[:, 128 * h : 128 * h + 128].reshape((4, 4) + UNIT)

        @pl.when(t == 0)
        def _():
            emit(own_a, other_a, 0)

        @pl.when(t == 1)
        def _():
            emit(own_a, other_a, 8)

        @pl.when(t == 2)
        def _():
            emit(own_b, other_b, 0)

        return carry

    lax.fori_loop(0, 3, step, 0)

    def epilogue(at, r):
        h = h_s[at, :]
        out_o[at, :] = (h + branch_scale * (m_s[at, :] + downb)).astype(bf16)
        n2, r2 = normalize(h)
        da2 = da2_s[at, :]
        sums_o[ROW_G2 : ROW_G2 + 1, :D] += jnp.sum(da2 * n2, axis=0, keepdims=True)
        sums_o[ROW_B2 : ROW_B2 + 1, :D] += jnp.sum(da2, axis=0, keepdims=True)
        e = da2 * gain2
        live = (lax.broadcasted_iota(jnp.int32, (QB, D), 0) + QB * r) < total
        dy = jnp.where(live, cot[at, :].astype(f32), 0.0)
        dh = dy + r2 * (
            e
            - jnp.mean(e, axis=-1, keepdims=True)
            - n2 * jnp.mean(e * n2, axis=-1, keepdims=True)
        )
        dh_o[at, :] = dh
        du = (branch_scale * dh).astype(bf16)
        sums_o[ROW_OB : ROW_OB + 1, :D] += jnp.sum(du.astype(f32), axis=0, keepdims=True)
        dm_s[at, :] = du
        do = nt(du, w_out).astype(bf16)
        for g in range(6):
            do_o[g, at, :] = do[:, 128 * g : 128 * g + 128]

    for r in range(ROWS // QB):
        epilogue(pl.ds(QB * r, QB), r)
    a2t_s[...] = attended(pl.ds(0, ROWS)).T
    grad = nn(a2t_s[...], dm_s[...])
    for g in range(6):
        st_o[g] = grad[:, 128 * g : 128 * g + 128].astype(bf16).reshape((16,) + UNIT)

    def issue_out(ref, i, core, y):
        pltpu.make_async_copy(
            st_o.at[pl.ds(3 * y, 3), 2 * i + core], ref.at[pl.ds(8, 3)], sem_p
        ).start()

    place_loop(pieces, meta, own_b, other_b, issue_out)
    wait(st, sem_o)
    wait(st_o, sem_p)


def middle(pieces, meta, lens, tokens, attended, cotangent, vec, weights):
    block = (16,) + UNIT
    return pl.pallas_call(
        lambda *refs: middle_body(pieces, *refs),
        out_shape=(
            sds((ROWS, D), bf16),
            sds((ROWS, D), f32),
            sds((6, ROWS, 128), bf16),
            *places(pieces, 16),
            *places(pieces, 11),
            sds((8, 1024), f32),
        ),
        in_specs=[SM, SM, VM, VM, VM, VM, VM, VM] + [HB] * len(weights),
        out_specs=(VM, VM, VM, HB, HB, HB, HB, VM),
        scratch_shapes=[
            pltpu.VMEM((6,) + block, bf16),
            pltpu.VMEM((4, 8, 24) + UNIT, bf16),
            pltpu.VMEM((ROWS, D), f32),
            pltpu.VMEM((ROWS, D), bf16),
            pltpu.VMEM((D, ROWS), bf16),
            pltpu.VMEM((ROWS, D), bf16),
            pltpu.VMEM((D, ROWS), bf16),
            pltpu.VMEM((ROWS, D), f32),
            pltpu.VMEM((ROWS, D), f32),
            pltpu.VMEM((ROWS, 1024), bf16),
            pltpu.VMEM((ROWS, 1024), bf16),
            pltpu.VMEM((4, 8, 8) + UNIT, bf16),
            pltpu.VMEM((6,) + block, bf16),
            pltpu.VMEM((8, 1024), f32),
            pltpu.SemaphoreType.DMA(()),
            pltpu.SemaphoreType.DMA(()),
            pltpu.SemaphoreType.DMA(()),
            pltpu.SemaphoreType.DMA(()),
        ],
        name="middle",
        **params(60e9, 40e6, 56),
    )(meta, lens, tokens, *attended, cotangent, vec, *weights)


def back_pair(far, q_ref, k_ref, v_ref, do_ref, lse_ref, out, pair, dk_s, dv_s):
    lane = lax.broadcasted_iota(jnp.int32, (QB, 128), 1)
    causal = lax.broadcasted_iota(jnp.int32, (QB, QB), 0) <= lax.broadcasted_iota(
        jnp.int32, (QB, QB), 1
    )
    kt = k_ref[...].T
    sub = lax.broadcasted_iota(jnp.int32, (128, ROWS), 0)
    dk_s[...] = jnp.zeros_like(dk_s)
    dv_s[...] = jnp.zeros_like(dv_s)
    for j in range(ROWS // QB):
        size = QB * (j + 1)
        q = q_ref[QB * j : size, :]
        do = do_ref[QB * j : size, :]
        dq = jnp.zeros((128, QB), f32)
        dk = jnp.zeros((size, 128), f32)
        dv = jnp.zeros((size, 128), f32)
        for h in range(2):
            mine = (lane < HD) if h == 0 else (lane >= HD)
            qh = jnp.where(mine, q, jnp.zeros_like(q))
            doh = jnp.where(mine, do, jnp.zeros_like(do))
            s = nt(k_ref[:size, :], qh)
            parts = []
            if j >= 2:
                parts.append(s[:512] + far)
                if j == 3:
                    parts.append(s[512:768])
            elif j == 1:
                parts.append(s[:QB])
            parts.append(jnp.where(causal, s[size - QB :], NEG))
            s = jnp.concatenate(parts, axis=0)
            p = jnp.exp(s - lse_ref[h : h + 1, QB * j : size])
            dp = nt(v_ref[:size, :], doh)
            dot = jnp.sum(p * dp, axis=0, keepdims=True)
            ds = (p * (dp - dot)).astype(bf16)
            dv += nn(p.astype(bf16), doh)
            dk += nn(ds, qh)
            keep = (sub < HD) if h == 0 else (sub >= HD)
            dq += nn(jnp.where(keep, kt, jnp.zeros_like(kt))[:, :size], ds)
        out[pair, QB * j : size, :] = (dq.T * (1.0 / HD)).astype(bf16)
        dk_s[:size, :] += dk
        dv_s[:size, :] += dv
    out[2 + pair] = dk_s[...].astype(bf16)
    out[4 + pair] = dv_s[...].astype(bf16)


def back_body(pieces, third, meta, lens, qkv, do, lse, a1t, wq, vec, *refs):
    if third > 0:
        refs = refs[2:]
    if third == 2:
        mid, sums_0, sums_1, *refs = refs
    dqkv_o, own, other, sums_o, dk_s, dv_s, st, st_v, sem, sem2 = refs
    far = jnp.where(lens[0, 0] < ROWS, NEG, 0.0).astype(f32)

    def one(pair, carry):
        back_pair(
            far, qkv.at[pair], qkv.at[2 + pair], qkv.at[4 + pair], do.at[third + 3 * pair], lse.at[pair],
            dqkv_o, pair, dk_s, dv_s,
        )
        return carry

    lax.fori_loop(0, 2, one, 0)
    raw = jnp.zeros((D, 128), f32)
    plain = jnp.zeros((D, 128), f32)
    cols = []
    for two in range(3):
        blocks = nn(a1t[...], jnp.concatenate([dqkv_o[2 * two], dqkv_o[2 * two + 1]], axis=1))
        for g in (2 * two, 2 * two + 1):
            block = blocks[:, 128 * (g % 2) : 128 * (g % 2) + 128]
            col = jnp.sum(dqkv_o[g].astype(f32), axis=0, keepdims=True)
            cols.append(col)
            st[g] = block.astype(bf16).reshape((16,) + UNIT)
            weight = wq[g].reshape(D, 128).astype(f32)
            raw += block * weight
            plain += weight * col
    base = 3 * third

    def issue(ref, i, core, y):
        pltpu.make_async_copy(
            st.at[pl.ds(3 * y, 3), 2 * i + core], ref.at[pl.ds(base, 3)], sem
        ).start()

    place_loop(pieces, meta, own, other, issue)
    raw = jnp.sum(raw, axis=1, keepdims=True)
    plain = jnp.sum(plain, axis=1, keepdims=True)
    lane = lax.broadcasted_iota(jnp.int32, (D, 128), 1)
    flat = jnp.where(lane == 0, raw, plain).T[:8]
    sums = jnp.concatenate([jnp.concatenate(cols, axis=1), flat[:2], jnp.zeros((5, D), f32)], axis=0)
    sums_o[...] = sums
    if third == 2:
        per = [sums_0[...], sums_1[...], sums]
        raw = per[0][1:2] + per[1][1:2] + per[2][1:2]
        shift = per[0][2:3] + per[1][2:3] + per[2][2:3]
        row_of = lambda name: vec[ROW_OF[name] : ROW_OF[name] + 1, :]
        gain = (raw - row_of("shift1") * shift) / row_of("gain1")
        pick = lambda g: jnp.concatenate(
            [per[p % 3][0:1, 128 * (g + p // 3) : 128 * (g + p // 3) + 128] for p in range(6)], axis=1
        )
        known = {
            "outb": mid[ROW_OB : ROW_OB + 1, :D],
            "downb": mid[ROW_DN : ROW_DN + 1, :D],
            "gain1": gain,
            "shift1": shift,
            "gain2": mid[ROW_G2 : ROW_G2 + 1, :D],
            "shift2": mid[ROW_B2 : ROW_B2 + 1, :D],
        }
        rows = {ROW_OF["qv"]: pick(0), ROW_OF["qv"] + 1: pick(4)}
        for name, value in known.items():
            rows[ROW_OF[name]] = value
        for r in range(4):
            rows[ROW_OF["upb"] + r] = jnp.concatenate(
                [
                    mid[ROW_UP + t : ROW_UP + t + 1, 128 * i : 128 * i + 128]
                    for i in (2 * r, 2 * r + 1)
                    for t in range(3)
                ],
                axis=1,
            )
        groups = pack_small(lambda r: rows[r])
        for g in range(3):
            st_v[:, 16 * g : 16 * g + 16, :] = jnp.broadcast_to(
                groups[g][:, None, :], (32, 16, 128)
            ).astype(bf16)

        def issue_small(ref, i, core, y):
            pltpu.make_async_copy(st_v.at[i * 4 + 2 * y + core], ref.at[9], sem2).start()

        place_loop(pieces, meta, own, other, issue_small)
        wait(st_v, sem2)
    wait(st, sem)


def back(pieces, third, meta, lens, qkv, do, lse, a1t, wq, vec, before):
    args = [meta, lens, qkv, do, lse, a1t, wq, vec, *before]
    extra = [HB, HB] * (third > 0) + [VM, VM, VM] * (third == 2)
    return pl.pallas_call(
        lambda *refs: back_body(pieces, third, *refs),
        out_shape=(
            sds((6, ROWS, 128), bf16),
            *places(pieces, 10),
            sds((8, D), f32),
        ),
        in_specs=[SM, SM] + [VM] * 6 + extra,
        out_specs=(VM, HB, HB, VM),
        input_output_aliases={8: 1, 9: 2} if third > 0 else {},
        scratch_shapes=[
            pltpu.VMEM((ROWS, 128), f32),
            pltpu.VMEM((ROWS, 128), f32),
            pltpu.VMEM((6, 16) + UNIT, bf16),
            pltpu.VMEM((32,) + UNIT, bf16),
            pltpu.SemaphoreType.DMA(()),
            pltpu.SemaphoreType.DMA(()),
        ],
        name=f"back_{third}",
        **params(18e9, 8e6, 20),
    )(*args)


def first_norm_back_body(tok, d_0, d_1, d_2, w_0, w_1, w_2, dh, vec, *refs):
    gt_o = refs[-1]
    gain1 = vec[ROW_OF["gain1"] : ROW_OF["gain1"] + 1, :]

    def body(at, r):
        da1 = jnp.zeros((QB, D), f32)
        for grad, weight in ((d_0, w_0), (d_1, w_1), (d_2, w_2)):
            rows = jnp.concatenate([grad[g, at, :] for g in range(6)], axis=1)
            da1 += nt(rows, lanes(weight, 6))
        n1, r1 = normalize(tok[at, :].astype(f32))
        e = da1 * gain1
        back = r1 * (
            e
            - jnp.mean(e, axis=-1, keepdims=True)
            - n1 * jnp.mean(e * n1, axis=-1, keepdims=True)
        )
        gt_o[at, :] = (dh[at, :] + back).astype(bf16)

    over_rows(body, 2)


def first_norm_back(half, tokens, grads, weights, dh, vec, before=None):
    count = ROWS // 2
    rows = pl.BlockSpec((count, D), lambda g: (half, 0))
    every = lambda shape: pl.BlockSpec(shape, lambda g: (0,) * len(shape))
    return pl.pallas_call(
        first_norm_back_body,
        grid=(1,),
        out_shape=sds((ROWS, D), bf16),
        in_specs=[rows]
        + [pl.BlockSpec((6, count, 128), lambda g: (0, half, 0))] * 3
        + [every((6, 16) + UNIT)] * 3
        + [rows, every((VECS, D))]
        + ([] if before is None else [HB]),
        out_specs=rows,
        input_output_aliases={} if before is None else {9: 0},
        name=f"first_norm_back_{half}",
        **params(8e9, 9e6, 14),
    )(tokens, *grads, *weights, dh, vec, *(() if before is None else (before,)))


def links(step):
    pairs = []
    for z in range(4):
        for x in range(2):
            for y in range(2):
                for c in range(2):
                    tz, tx, ty, tc = step(z, x, y, c)
                    pairs.append(((z * 2 + x) * 4 + y * 2 + c, (tz * 2 + tx) * 4 + ty * 2 + tc))
    return pairs


TO_CORE = links(lambda z, x, y, c: (z, x, y, 1 - c))
TO_FIRST = links(lambda z, x, y, c: (z, 1 - x, y, c) if c == 0 else (z, x, 1 - y, c))
TO_SECOND = links(lambda z, x, y, c: (z, x, 1 - y, c) if c == 0 else (z, 1 - x, y, c))
TO_Z = [None] + [links(lambda z, x, y, c, k=k: (z ^ k, x, y, c)) for k in (1, 2, 3)]


def send(value, pairs):
    return lax.ppermute(value, BOTH, pairs)


def after(value, *others):
    return lax.optimization_barrier((value, *others))[0]


def add(*parts):
    total = parts[0].astype(f32)
    for part in parts[1:]:
        total = total + part.astype(f32)
    return total


def split(big, sizes):
    out, at = [], 0
    for size in sizes:
        out.append(big[at : at + size])
        at += size
    return out


def as_units(block):
    a, b = block.shape[0] // 48, block.shape[1] // 128
    return block.reshape(a, 48, b, 128).transpose(2, 0, 1, 3).reshape(a * b, 48, 128)


def first_pieces(qkv_weight, out_weight, small):
    core = lax.axis_index("narrow") % 2
    both = jnp.concatenate([qkv_weight, out_weight], axis=1).astype(bf16)
    keep = jnp.where(core == 0, both[:48], both[48:])
    give = jnp.where(core == 0, both[48:], both[:48])
    got = send(give, TO_CORE)
    left = jnp.where(core == 0, keep, got)
    right = jnp.where(core == 0, got, keep)
    cols = as_units(jnp.concatenate([left[:, :576], right[:, :576]], axis=1))
    out = as_units(jnp.concatenate([left[:, 576:], right[:, 576:]], axis=1))
    thirds = [cols[g] for t in range(3) for g in (t, 3 + t, 6 + t)]
    return jnp.concatenate([jnp.stack(thirds), small], axis=0), out


def feed_pieces(up_weight, down_weight):
    up = as_units(up_weight.astype(bf16))
    down = as_units(down_weight.astype(bf16).T)
    out = []
    for t in range(3):
        out.append(jnp.concatenate([up[2 * t : 2 * t + 2], up[6 + 2 * t : 8 + 2 * t], down[4 * t : 4 * t + 4]]))
    return out


def whole(value, dims):
    for axis, dim in dims:
        value = lax.all_gather(value, axis, axis=dim, tiled=True)
    return value


def plain_weights(qkv_weight, out_weight, up_weight, down_weight, vectors):
    matrix = lambda w: whole(w.astype(bf16), (("narrow", 1), ("wide", 0)))
    blocks = lambda w, b: w.reshape(16, 48, b, 128).transpose(2, 0, 1, 3)
    wq = blocks(matrix(qkv_weight), 18)
    wq = [jnp.stack([wq[g] for g in (t, 3 + t, 6 + t, 9 + t, 12 + t, 15 + t)]) for t in range(3)]
    wo = blocks(matrix(out_weight), 6)
    up = blocks(matrix(up_weight), 24).reshape(4, 2, 3, 8, 2, 48, 128)
    up = up.transpose(0, 3, 2, 1, 4, 5, 6).reshape(4, 8, 3, 4, 48, 128)
    down = blocks(matrix(down_weight).T, 24).reshape(8, 3, 4, 4, 48, 128).transpose(2, 0, 1, 3, 4, 5)
    feed = jnp.concatenate([up, down], axis=3).reshape(4, 8, 24, 48, 128)
    rows = [
        whole(vectors[name].astype(bf16), (("narrow", 0), ("wide", 0))).astype(f32).reshape(count, D)
        for name, _, _, count in SMALL
    ]
    vec = jnp.concatenate(rows + [jnp.zeros((VECS - 12, D), f32)], axis=0)
    return wq, wo, feed, vec


def plain_grads(q_all, m_a, m_b):
    def reduce(matrix):
        rows = lax.psum_scatter(matrix.astype(f32), "wide", scatter_dimension=0, tiled=True)
        return lax.psum_scatter(rows.astype(bf16), "narrow", scatter_dimension=1, tiled=True).astype(f32)

    def vector(values):
        rows = lax.psum_scatter(values, "wide", scatter_dimension=0, tiled=True)
        return lax.psum_scatter(rows.astype(bf16), "narrow", scatter_dimension=0, tiled=True).astype(f32)

    q = q_all[:, :, :9].reshape(8, 2, 2, 3, 3, 48, 128)
    qkv = q.transpose(0, 2, 5, 1, 4, 3, 6).reshape(D, 2304)
    out = m_b[:, :, 8:].reshape(8, 2, 2, 3, 48, 128).transpose(0, 2, 4, 1, 3, 5).reshape(D, D)
    m = jnp.concatenate([m_a, m_b[:, :, :8]], axis=2).reshape(8, 4, 3, 2, 4, 48, 128)
    up = m[:, :, :, 0].reshape(8, 4, 3, 2, 2, 48, 128).transpose(0, 4, 5, 1, 3, 2, 6).reshape(D, FF)
    down = m[:, :, :, 1].transpose(0, 2, 5, 1, 3, 4).reshape(FF, D)
    small = q_all[:, :, 9].reshape(32, 3, 16, 128)[:, :, 0].reshape(32, 384).astype(f32)
    vecs = {name: vector(small[:, off : off + wd].reshape(-1)) for name, off, wd, _ in SMALL}
    return reduce(qkv), reduce(out), reduce(up), reduce(down), vecs


class Spread:
    def __init__(self, piece, *waits):
        near = send(after(piece, *waits), TO_Z[1])
        self.parts = [piece, near] + [send(piece, TO_Z[k]) for k in (2, 3)]

    def along(self, *waits):
        self.line = after(jnp.stack(self.parts, axis=0), *waits)
        self.first = send(self.line, TO_FIRST)
        self.second = send(self.line, TO_SECOND)

    def across(self, *waits):
        self.corner = send(after(self.first, *waits), TO_SECOND)

    def swap(self, *waits):
        self.swapped = [send(after(part, *waits), TO_CORE) for part in (self.line, self.first, self.second)]

    def end(self, *waits):
        last = send(after(self.corner, *waits), TO_CORE)
        return (self.line, self.first, self.second, self.corner, *self.swapped, last)


class Fold:
    def __init__(self, own, other):
        self.own = own
        self.got = send(other, TO_CORE)

    def second(self, *waits):
        self.got = after(self.got, *waits)
        self.sum_2 = add(self.own[2:], self.got[2:]).astype(bf16)
        self.sec = send(self.sum_2, TO_SECOND)

    def first(self, *waits):
        self.sec = after(self.sec, *waits)
        self.sum_1 = add(self.own[1], self.got[1], self.sec[1]).astype(bf16)
        self.fst = send(self.sum_1, TO_FIRST)

    def line(self, *waits):
        self.fst = after(self.fst, *waits)
        mine = [add(self.own[0, k], self.got[0, k], self.sec[0, k], self.fst[k]) for k in range(4)]
        self.mine = mine[0]
        self.sum_0 = [part.astype(bf16) for part in mine[1:]]
        self.far = [send(part, TO_Z[k + 1]) for k, part in enumerate(self.sum_0)]

    def end(self, *waits):
        return add(self.mine, *(after(part, *waits) for part in self.far))


def joined(blocks):
    return jnp.concatenate(blocks, axis=1)


def fast_grads(q_all, m_a, m_b):
    core = lax.axis_index("narrow") % 2
    m = jnp.concatenate([m_a, m_b[:8]], axis=0).reshape(3, 2, 4, 48, 128)
    grad_up = joined([m[t, 0, 2 * h : 2 * h + 2].reshape(96, 128) for h in range(2) for t in range(3)])
    grad_down = joined([m[t, 1].reshape(192, 128) for t in range(3)]).T
    cols = joined([q_all[3 * t + g] for g in range(3) for t in range(3)])
    outs = joined([m_b[8 + g] for g in range(3)])
    low = joined([cols[:, :576], outs[:, :192]])
    high = joined([cols[:, 576:], outs[:, 192:]])
    keep = jnp.where(core == 0, low, high)
    got = send(jnp.where(core == 0, high, low), TO_CORE)
    rows = jnp.concatenate([jnp.where(core == 0, keep, got), jnp.where(core == 0, got, keep)], axis=0)
    small = q_all[9].reshape(3, 16, 128)[:, 0].reshape(384)
    vecs = {name: small[off : off + wd] for name, off, wd, _ in SMALL}
    return rows[:, :576], rows[:, 576:], grad_up, grad_down, vecs


def local(
    tokens,
    qkv_weight,
    qv_bias,
    out_weight,
    out_bias,
    up_weight,
    up_bias,
    down_weight,
    down_bias,
    norm1_gain,
    norm1_bias,
    norm2_gain,
    norm2_bias,
    lengths,
    cotangent,
    fast,
):
    vectors = {
        "qv": qv_bias,
        "outb": out_bias,
        "downb": down_bias,
        "gain1": norm1_gain,
        "shift1": norm1_bias,
        "gain2": norm2_gain,
        "shift2": norm2_bias,
        "upb": up_bias,
    }
    meta = jnp.stack([lax.axis_index("wide"), lax.axis_index("narrow")]).astype(jnp.int32)
    if fast:
        zeros = lambda size: jnp.zeros((size,), f32)
        small = jnp.concatenate(
            [qv_bias, out_bias, down_bias, norm1_gain, zeros(8)]
            + [norm1_bias, norm2_gain, norm2_bias, zeros(56), up_bias, zeros(32)]
        )
        small = jnp.pad(small.astype(bf16).reshape(3, 1, 128), ((0, 0), (0, 15), (0, 0))).reshape(1, 48, 128)
        piece_q, piece_o = first_pieces(qkv_weight, out_weight, small)
        feed = feed_pieces(up_weight, down_weight)
        heads = Spread(piece_q)
        rest = Spread(jnp.concatenate(feed + [piece_o]), heads.parts[1])
        heads.along(rest.parts[1])
        heads.across(rest.parts[2])
        heads.swap()
        ready = heads.end()
        rest.along(heads.corner)
        first = after(tokens, rest.line)
        a1, a1t, vec, qkv_0, o_0, lse_0, wq_0 = front(True, 0, meta, lengths, first, None, ready)
        qkv_1, o_1, lse_1, wq_1 = front(True, 1, meta, lengths, a1, vec, ready)
        rest.across(o_1)
        rest.swap(o_1)
        qkv_2, o_2, lse_2, wq_2 = front(True, 2, meta, lengths, a1, vec, ready)
        weights = rest.end(o_2)
    else:
        wq, wo, feed, vec = plain_weights(qkv_weight, out_weight, up_weight, down_weight, vectors)
        a1, a1t, vec, qkv_0, o_0, lse_0, wq_0 = front(False, 0, meta, lengths, tokens, vec, (wq[0],))
        qkv_1, o_1, lse_1, wq_1 = front(False, 1, meta, lengths, a1, vec, (wq[1],))
        qkv_2, o_2, lse_2, wq_2 = front(False, 2, meta, lengths, a1, vec, (wq[2],))
        weights = (wo, feed)
    output, dh, do, own_a, other_a, own_b, other_b, mid = middle(
        fast, meta, lengths, tokens, (o_0, o_1, o_2), cotangent, vec, weights
    )
    args = lambda qkv, lse, wq: (qkv, do, lse, a1t, wq, vec)
    d_0, own, other, sums_0 = back(fast, 0, meta, lengths, *args(qkv_0, lse_0, wq_0), ())
    if fast:
        ff_a, ff_b = Fold(own_a, other_a), Fold(own_b, other_b)
        ff_a.second(d_0)
        do = after(do, ff_a.sum_2, ff_b.got)
    d_1, own, other, sums_1 = back(fast, 1, meta, lengths, *args(qkv_1, lse_1, wq_1), (own, other))
    if fast:
        ff_b.second(d_1)
        ff_a.first(d_1)
        do = after(do, ff_b.sum_2, ff_a.sum_1)
    d_2, own, other, _ = back(
        fast, 2, meta, lengths, *args(qkv_2, lse_2, wq_2), (own, other, mid, sums_0, sums_1)
    )
    grads, weights = (d_0, d_1, d_2), (wq_0, wq_1, wq_2)
    if fast:
        at = Fold(own, other)
        ff_b.first(d_2)
        dh = after(dh, ff_b.sum_1)
    top = first_norm_back(0, tokens, grads, weights, dh, vec)
    if fast:
        ff_a.line(top)
        at.second(top)
        dh = after(dh, at.sum_2, *ff_a.sum_0)
    grad_tokens = first_norm_back(1, tokens, grads, weights, dh, vec, top)
    if fast:
        at.first(grad_tokens)
        total_a = ff_a.end(at.sum_1)
        ff_b.line(total_a)
        at.line(*ff_b.sum_0)
        g_qkv, g_out, g_up, g_down, vecs = fast_grads(at.end(), total_a, ff_b.end(at.far[0]))
    else:
        g_qkv, g_out, g_up, g_down, vecs = plain_grads(own, own_a, own_b)
    return (
        output,
        grad_tokens,
        g_qkv,
        vecs["qv"],
        g_out,
        vecs["outb"],
        g_up,
        vecs["upb"],
        g_down,
        vecs["downb"],
        vecs["gain1"],
        vecs["shift1"],
        vecs["gain2"],
        vecs["shift2"],
    )


def solution(mesh):
    fast = mesh.shape["wide"] == 8 and mesh.shape["narrow"] == 4
    rows, matrix, vector = P(BOTH, None), P("wide", "narrow"), P(BOTH)
    return jax.shard_map(
        lambda *args: local(*args, fast),
        mesh=mesh,
        in_specs=(
            rows, matrix, vector, matrix, vector, matrix, vector, matrix, vector,
            vector, vector, vector, vector, rows, rows,
        ),
        out_specs=(
            rows, rows, matrix, vector, matrix, vector, matrix, vector, matrix, vector,
            vector, vector, vector, vector,
        ),
        check_vma=False,
    )
```
